32 devices in a mesh: fsdp: 2 (over y), ctx: 4 (over z), tp: 4 (over x, core).
Axes of the slice: x: 2, y: 2, z: 4, core: 2. Of those that a mesh axis runs over, the one named last changes fastest.
Arguments:
- tokens: bfloat16 [5120, 2, 1024], P(('ctx', 'tp'), 'fsdp'), may hold values from -6 to 6
- first_values: bfloat16 [5120, 2, 1024], P('ctx', 'fsdp', 'tp'), may hold values from -6 to 6
- cotangent: bfloat16 [5120, 2, 1024], P(('ctx', 'tp'), 'fsdp'), may hold values from -6 to 6
- parents: int32 [2, 13], P('fsdp'), may hold values from 0 to 11, as said below
- seg_lengths: int32 [2, 13], P('fsdp'), may hold values from 1 to 2048, 5120 in all within a row
- w_query: bfloat16 [1024, 1024], P('fsdp', 'tp'), may hold values from -0.1875 to 0.1875
- w_key: bfloat16 [1024, 1024], P('fsdp', 'tp'), may hold values from -0.1875 to 0.1875
- w_value: bfloat16 [1024, 1024], P('fsdp', 'tp'), may hold values from -0.1875 to 0.1875
- w_out: bfloat16 [1024, 1024], P('fsdp', 'tp'), may hold values from -1.5 to 1.5
- w_gate: bfloat16 [1024, 2816], P('fsdp', 'tp'), may hold values from -0.1875 to 0.1875
- w_up: bfloat16 [1024, 2816], P('fsdp', 'tp'), may hold values from -0.1875 to 0.1875
- w_down: bfloat16 [1024, 2816], P('fsdp', 'tp'), may hold values from -0.109375 to 0.109375
- gain_attn: bfloat16 [1024], P('fsdp'), may hold values from 0.5 to 1.5
- gain_ffn: bfloat16 [1024], P('fsdp'), may hold values from 0.5 to 1.5
Outputs:
- layer_out: bfloat16 [5120, 2, 1024], P(('ctx', 'tp'), 'fsdp')
- grad_tokens: float32 [5120, 2, 1024], P(('ctx', 'tp'), 'fsdp')
- grad_values: float32 [5120, 2, 1024], P('ctx', 'fsdp', 'tp')
- grad_query: float32 [1024, 1024], P('fsdp', 'tp')
- grad_key: float32 [1024, 1024], P('fsdp', 'tp')
- grad_value: float32 [1024, 1024], P('fsdp', 'tp')
- grad_out: float32 [1024, 1024], P('fsdp', 'tp')
- grad_gate: float32 [1024, 2816], P('fsdp', 'tp')
- grad_up: float32 [1024, 2816], P('fsdp', 'tp')
- grad_down: float32 [1024, 2816], P('fsdp', 'tp')
- grad_gain_attn: float32 [1024], P('fsdp')
- grad_gain_ffn: float32 [1024], P('fsdp')
The draws below stay inside these ranges and needn't reach their ends.
Inputs may be any that keep to these rules, and one draw needn't show every extreme that they name: `parents`: segment 0 of each tree is its root and names itself; every other segment's parent comes before it, at most 4 places back; the last segment's parent is the one just before it.
All inputs are finite; a program needn't handle non-finite values.
Results may differ from the reference program's by a relative error of at most 0.022.
Values may be sent and summed in bfloat16 or wider, within the bound.
No kernel may reach another device: no remote copies, remote signals or barrier semaphores. Data moves between devices by JAX's collectives and lax.ppermute only.
A program may use at most 192 MiB of HBM per device.

```python
import math
import jax
import jax.numpy as jnp
import numpy as np
from jax import lax

D = 1024
HEADS = 16
HEAD = 64
FF = 2816
TREE_LEN = 5120
SEGS = 13
SEG_MOST = 2048
TREES = 2


def draw_parents(key, part):
    jump_back = jax.random.randint(key, (TREES, SEGS), 0, 4, dtype=jnp.int32)
    seg_index = jnp.arange(SEGS, dtype=jnp.int32)
    parent_seg = jnp.maximum(seg_index[None, :] - 1 - jump_back, 0)
    return jnp.where(seg_index[None, :] == SEGS - 1, SEGS - 2, parent_seg).astype(jnp.int32)


def block_levels(rng, extent, shards, smallest, largest):
    factor_of, own = 1.0, jax.random.fold_in(rng, 6)
    for dim, parts in shards:
        steps = jnp.exp(jax.random.uniform(jax.random.fold_in(own, dim), (parts,), jnp.float32, smallest / len(shards), largest / len(shards)))
        factor_of = factor_of * jnp.repeat(steps, extent[dim] // parts).reshape([-1 if axis == dim else 1 for axis in range(len(extent))])
    return factor_of


def length_profile(number_of, total, most, slope):
    portions = [(1 << 20) // math.isqrt(grade ** slope) + 1 for grade in range(2, number_of + 1)]
    surplus, counts = total - most - (number_of - 1), [1] * (number_of - 1)
    while surplus > 0:
        free = [i for i in range(number_of - 1) if counts[i] < most]
        mass, left = sum([portions[i] for i in free]), surplus
        for i in free:
            extra = min(most - counts[i], max(1, left * portions[i] // mass), surplus)
            counts[i] = counts[i] + extra
            surplus = surplus - extra
    return np.array([most] + counts)


def uneven(key, amount, total, most, slope):
    if amount == 2:
        one = jax.random.randint(key, (), max(1, total - most), min(most, total - 1) + 1)
        return jnp.stack([one, total - one])
    sizes = jnp.asarray(length_profile(amount, total, most, slope), jnp.int32)
    twos = (amount - 1) // 2
    donor, receiver = sizes[1:1 + 2 * twos:2], sizes[2:2 + 2 * twos:2]
    margin = jnp.minimum(donor - 1, most - receiver)
    shifted = jax.random.randint(jax.random.fold_in(key, 1), (twos,), 0, 1 << 20) % (margin + 1)
    sizes = sizes.at[1:1 + 2 * twos:2].set(donor - shifted).at[2:2 + 2 * twos:2].set(receiver + shifted)
    return sizes[jax.random.permutation(jax.random.fold_in(key, 2), amount)]


def bell_draw(key, dims, deviation, limit, shards=(), kind=jnp.bfloat16):
    drawn = deviation * jax.random.normal(key, dims, jnp.float32)
    if shards:
        drawn = drawn * block_levels(key, dims, shards, -0.22, 0.18)
    return jnp.clip(drawn, -limit, limit).astype(kind)


def setup_inputs(seed: int = 0) -> dict:
    keys = jax.random.split(jax.random.key(seed), 15)
    return {
        "tokens": bell_draw(keys[0], (TREE_LEN, TREES, D), 1.0, 6.0, ((0, 16), (1, 2))),
        "first_values": bell_draw(keys[1], (TREE_LEN, TREES, HEADS * HEAD), 1.0, 6.0, ((0, 4), (1, 2), (2, 4))),
        "cotangent": bell_draw(keys[2], (TREE_LEN, TREES, D), 1.0, 6.0, ((0, 16), (1, 2))),
        "parents": draw_parents(jax.random.fold_in(keys[14], 71), 0),
        "seg_lengths": jax.vmap(lambda own: uneven(own, SEGS, TREE_LEN, SEG_MOST, 2))(jax.random.split(keys[4], TREES)).reshape((TREES, SEGS)).astype(jnp.int32),
        "w_query": bell_draw(keys[5], (D, HEADS * HEAD), D ** -0.5, 0.1875, ((0, 2), (1, 4))),
        "w_key": bell_draw(keys[6], (D, HEADS * HEAD), D ** -0.5, 0.1875, ((0, 2), (1, 4))),
        "w_value": bell_draw(keys[7], (D, HEADS * HEAD), D ** -0.5, 0.1875, ((0, 2), (1, 4))),
        "w_out": bell_draw(keys[8], (D, HEADS * HEAD), 16 ** -0.5, 1.5, ((0, 2), (1, 4))),
        "w_gate": bell_draw(keys[9], (D, FF), D ** -0.5, 0.1875, ((0, 2), (1, 4))),
        "w_up": bell_draw(keys[10], (D, FF), D ** -0.5, 0.1875, ((0, 2), (1, 4))),
        "w_down": bell_draw(keys[11], (D, FF), FF ** -0.5, 0.109375, ((0, 2), (1, 4))),
        "gain_attn": jnp.clip(1.0 + 0.1 * jax.random.normal(keys[12], (D,), jnp.float32), 0.5, 1.5).astype(jnp.bfloat16),
        "gain_ffn": jnp.clip(1.0 + 0.1 * jax.random.normal(keys[13], (D,), jnp.float32), 0.5, 1.5).astype(jnp.bfloat16),
    }


epsilon = 1e-05
masked_score = -1e+30
highest = lax.Precision.HIGHEST

@jax.custom_vjp
def low(v):
    return lax.optimization_barrier(v.astype(jnp.bfloat16)).astype(jnp.float32)

@jax.custom_vjp
def low_back(v):
    return v

def low_keep(v):
    return (low(v), None)

def low_pass(kept, grad):
    return (grad,)

def back_keep(v):
    return (v, None)

def back_low(kept, grad):
    return (low(grad),)
low.defvjp(low_keep, low_pass)
low_back.defvjp(back_keep, back_low)

def rms_scale(values, scale_gain):
    return values * lax.rsqrt(lax.optimization_barrier(jnp.mean(values * values, axis=-1, keepdims=True)) + epsilon) * scale_gain

def gated(joined):
    middle_at = joined.shape[-1] // 2
    return jax.nn.silu(joined[..., :middle_at]) * joined[..., middle_at:]

def rotary(values, position, direction):
    half_head = HEAD // 2
    frequency = jnp.exp(-math.log(10000.0) * jnp.arange(half_head, dtype=jnp.float32) / half_head)
    angles = position[..., None] * frequency
    cosine = jnp.cos(angles)[..., None, :]
    sine_term = direction * jnp.sin(angles)[..., None, :]
    shaped = values.reshape(values.shape[:-1] + (values.shape[-1] // HEAD, HEAD))
    first_half = shaped[..., :half_head]
    second_half = shaped[..., half_head:]
    rotated = jnp.concatenate([first_half * cosine - second_half * sine_term, second_half * cosine + first_half * sine_term], axis=-1)
    return rotated.reshape(values.shape)

def tree_layout(parents, lengths):
    seg_count = parents.shape[-1]
    seg_index = jnp.arange(seg_count, dtype=jnp.int32)
    parent_link = ((parents[:, :, None] == seg_index[None, None, :]) & (seg_index[None, :, None] > 0)).astype(jnp.float32)
    identity = jnp.eye(seg_count, dtype=jnp.float32)

    def climb_step(step_at, ancestors):
        reached = lax.optimization_barrier(jnp.sum(parent_link[:, :, :, None] * ancestors[:, None, :, :], axis=2))
        return jnp.minimum(identity + reached, 1.0)
    ancestors = lax.fori_loop(0, seg_count, climb_step, jnp.broadcast_to(identity, parent_link.shape))
    offsets = (jnp.cumsum(lengths, axis=-1) - lengths).astype(jnp.int32)
    above_len = lax.optimization_barrier(jnp.sum((ancestors - identity) * lengths.astype(jnp.float32)[:, None, :], axis=-1))
    token_index = jnp.arange(TREE_LEN, dtype=jnp.int32)
    token_segment = (lax.optimization_barrier(jnp.sum((offsets[:, None, :] <= token_index[None, :, None]).astype(jnp.int32), axis=-1)) - 1).astype(jnp.int32)
    seg_start = jnp.take_along_axis(offsets.astype(jnp.float32), token_segment, axis=1)
    seg_depth = jnp.take_along_axis(above_len, token_segment, axis=1)
    position = token_index.astype(jnp.float32)[None, :] - seg_start + seg_depth
    ancestry = jnp.take_along_axis(ancestors, token_segment[:, :, None], axis=1)
    return (token_segment, ancestry, position)

def reference(tokens, first_values, cotangent, parents, seg_lengths, w_query, w_key, w_value, w_out, w_gate, w_up, w_down, gain_attn, gain_ffn):
    token_segment, ancestry, position = tree_layout(parents, seg_lengths)
    row_position = jnp.transpose(position)
    query_rows = math.gcd(TREE_LEN, 512)
    token_index = jnp.arange(TREE_LEN, dtype=jnp.int32)

    def attend_tree(packed):
        query_tree, key_tree, value_tree, reach_tree, segment_tree = packed

        def attend_block(block_at):
            begin = block_at * query_rows
            query_block = lax.dynamic_slice_in_dim(query_tree, begin, query_rows, 0)
            reach_block = lax.dynamic_slice_in_dim(reach_tree, begin, query_rows, 0)
            linked = jnp.take(reach_block, segment_tree, axis=1) > 0.5
            query_index = begin + jnp.arange(query_rows, dtype=jnp.int32)
            allowed = linked & (token_index[None, :] <= query_index[:, None])
            raw_scores = jnp.einsum('qhd,khd->hqk', query_block, key_tree, precision=highest) * HEAD ** (-0.5)
            scores = jnp.where(allowed[None], low_back(raw_scores), masked_score)
            probability = jax.nn.softmax(scores, axis=-1)
            mixed = jnp.einsum('hqk,khd->qhd', low(probability), value_tree, precision=highest)
            return low(low_back(mixed))
        blocks = lax.map(jax.checkpoint(attend_block), jnp.arange(TREE_LEN // query_rows, dtype=jnp.int32))
        return blocks.reshape(TREE_LEN, HEADS * HEAD)

    def forward(token_single, first_single, query_w, key_w, value_w, out_w, gate_w, up_w, down_w, attention_gain, ffn_gain):
        tree_total = token_single.shape[1]
        normed = low(rms_scale(token_single, attention_gain))
        flat_rows = normed.reshape(-1, D)
        query_pre = low_back(jnp.dot(flat_rows, query_w, precision=highest)).reshape(TREE_LEN, tree_total, -1)
        key_pre = low_back(jnp.dot(flat_rows, key_w, precision=highest)).reshape(TREE_LEN, tree_total, -1)
        value_pre = low_back(jnp.dot(flat_rows, value_w, precision=highest)).reshape(TREE_LEN, tree_total, -1)
        queries = low(rotary(query_pre, row_position, 1.0))
        key_vectors = low(rotary(key_pre, row_position, 1.0))
        values = low(0.5 * value_pre + 0.5 * first_single)

        def by_tree(array):
            return jnp.transpose(array, (1, 0, 2)).reshape(tree_total, TREE_LEN, HEADS, HEAD)
        mixed = lax.map(jax.checkpoint(attend_tree), (by_tree(queries), by_tree(key_vectors), by_tree(values), ancestry, token_segment))
        mixed = jnp.transpose(mixed, (1, 0, 2)).reshape(-1, HEADS * HEAD)
        attention_sum = low_back(jnp.dot(mixed, jnp.transpose(out_w), precision=highest)).reshape(token_single.shape)
        middle = token_single + attention_sum
        ffn_normed = low(rms_scale(middle, ffn_gain)).reshape(-1, D)
        joined = low_back(jnp.dot(ffn_normed, jnp.concatenate([gate_w, up_w], axis=1), precision=highest))
        hidden = low(gated(joined))
        return middle + jnp.dot(hidden, jnp.transpose(down_w), precision=highest).reshape(token_single.shape)
    floats = [source.astype(jnp.float32) for source in (tokens, first_values, w_query, w_key, w_value, w_out, w_gate, w_up, w_down, gain_attn, gain_ffn)]
    result, pull_back = jax.vjp(forward, *floats)
    gradients = pull_back(cotangent.astype(jnp.float32))
    return (result.astype(jnp.bfloat16), gradients[0], gradients[1], gradients[2], gradients[3], gradients[4], gradients[5], gradients[6], gradients[7], gradients[8], gradients[9], gradients[10])
```

```python
import functools
import math

import jax
import jax.numpy as jnp
from jax import lax
from jax.experimental import pallas as pl
from jax.experimental.pallas import tpu as pltpu
from jax.sharding import PartitionSpec as P

HEAD = 64
HALF = HEAD // 2
CHUNK = 128
BIG = 1e30
LOG2E = 1.4426950408889634
SCORE_SCALE = HEAD**-0.5
QUERY_SCALE = SCORE_SCALE * LOG2E
epsilon = 1e-05
f32 = jnp.float32
bf16 = jnp.bfloat16


def dot(a, b, ca, cb):
    return lax.dot_general(a, b, (((ca,), (cb,)), ((), ())), preferred_element_type=f32)


def layout_kernel(par_ref, len_ref, pos_ref, qx_ref, kx_ref, seg_ref, need_ref, anc_sc, above_sc, *, segs, tokens):
    token = lax.broadcasted_iota(jnp.int32, (1, tokens), 1)
    pos = jnp.zeros((1, tokens), jnp.int32)
    seg_of = jnp.full((1, tokens), -1, jnp.int32)
    bits = jnp.zeros((1, tokens), jnp.int32)
    for b in range(tokens // CHUNK):
        seg_ref[b] = 0
        need_ref[b] = 0
    off = jnp.int32(0)
    for s in range(segs):
        length = len_ref[0, s]
        if s == 0:
            anc, above = jnp.int32(1), jnp.int32(0)
        else:
            parent = par_ref[0, s]
            anc = anc_sc[parent] | jnp.int32(1 << s)
            above = above_sc[parent] + len_ref[0, parent]
        anc_sc[s] = anc
        above_sc[s] = above
        started = token >= off
        seg_of = jnp.where(started, s, seg_of)
        pos = jnp.where(started, token - off + above, pos)
        bits = jnp.where(started, anc, bits)

        def mark(b, carry, anc=anc, s=s):
            seg_ref[b] = seg_ref[b] | jnp.int32(1 << s)
            need_ref[b] = need_ref[b] | anc
            return carry

        lax.fori_loop(off // CHUNK, (off + length - 1) // CHUNK + 1, mark, 0)
        off = off + length
    pos_ref[...] = pos.astype(f32)
    row = lax.broadcasted_iota(jnp.int32, (kx_ref.shape[0], tokens), 0)
    kx_ref[...] = jnp.where(row == seg_of, -BIG, 0.0).astype(bf16)
    linked = lax.shift_right_logical(jnp.broadcast_to(bits, row.shape), row) & 1
    qx_ref[...] = jnp.where(linked == 1, 0.0, 1.0).astype(bf16)


SMEM = pl.BlockSpec(memory_space=pltpu.SMEM)
VMEM = pl.BlockSpec(memory_space=pltpu.VMEM)


def layout_call(parents, lengths, tokens):
    segs = parents.shape[-1]
    rows = -(-segs // 16) * 16
    return pl.pallas_call(
        functools.partial(layout_kernel, segs=segs, tokens=tokens),
        out_shape=(
            jax.ShapeDtypeStruct((1, tokens), f32),
            jax.ShapeDtypeStruct((rows, tokens), bf16),
            jax.ShapeDtypeStruct((rows, tokens), bf16),
            jax.ShapeDtypeStruct((tokens // CHUNK,), jnp.int32),
            jax.ShapeDtypeStruct((tokens // CHUNK,), jnp.int32),
        ),
        in_specs=[SMEM, SMEM],
        out_specs=(VMEM, VMEM, VMEM, SMEM, SMEM),
        scratch_shapes=[pltpu.SMEM((segs,), jnp.int32), pltpu.SMEM((segs,), jnp.int32)],
        cost_estimate=pl.CostEstimate(flops=0, bytes_accessed=1 << 20, transcendentals=0),
        name="layout",
    )(parents, lengths)


def any_bits(ref, first, count):
    bits = ref[first]
    for j in range(1, count):
        bits = bits | ref[first + j]
    return bits


def causal(scores, key_first, query_first):
    key_at = key_first + lax.broadcasted_iota(jnp.int32, scores.shape, 0)
    query_at = query_first + lax.broadcasted_iota(jnp.int32, scores.shape, 1)
    return jnp.where(key_at <= query_at, scores, -BIG)


def piece_place(place_ref, at):
    shift, half = divmod(at, 2)
    ctx = lax.rem(place_ref[0] - shift + place_ref[2], place_ref[2])
    return ctx * 2 + lax.rem(place_ref[1] + half, 2)


def chunks_at(ref, first, count):
    return jnp.concatenate([ref[first + j] for j in range(count)], axis=1)


def fwd_kernel(place_ref, seg_ref, need_ref, qx_ref, kx_ref, *rest, tile, pieces, extra):
    qkv_refs = rest[:pieces]
    out_ref, full_ref, lse_ref, keys, values, queries, top, total = rest[pieces:]
    at = pl.program_id(0)
    piece = qkv_refs[0].shape[1]
    per = piece // CHUNK
    pad = jnp.zeros((128 - HEAD - extra, CHUNK), bf16)

    @pl.when(at == 0)
    def _():
        for p in range(pieces):
            place = piece_place(place_ref, p)
            for c in range(per):
                g = place * per + c
                lanes = slice(c * CHUNK, (c + 1) * CHUNK)
                rows = pl.ds(pl.multiple_of(g * CHUNK, CHUNK), CHUNK)
                ref = qkv_refs[p]
                keys[rows, :] = jnp.concatenate([ref[HEAD : 2 * HEAD, lanes], kx_ref[:, rows], pad], axis=0).T
                values[g] = jnp.concatenate([ref[2 * HEAD :, lanes], jnp.ones((16, CHUNK), bf16)], axis=0)
                queries[g] = jnp.concatenate([ref[:HEAD, lanes], qx_ref[:, rows], pad], axis=0)

    per_tile = tile // CHUNK
    query = chunks_at(queries, at * per_tile, per_tile)
    need = any_bits(need_ref, at * per_tile, per_tile)

    def visit(key_at, diagonal):
        scores = dot(keys[pl.ds(pl.multiple_of(key_at * tile, tile), tile), :], query, 1, 0)
        value = chunks_at(values, key_at * per_tile, per_tile)
        if diagonal:
            scores = causal(scores, key_at * tile, at * tile)
            new_top = jnp.max(scores, axis=0, keepdims=True)
            weights = jnp.exp2(scores - new_top).astype(bf16)
            total[...] = dot(value, weights, 1, 0)
        else:
            old_top = top[...]
            new_top = jnp.maximum(old_top, jnp.max(scores, axis=0, keepdims=True))
            weights = jnp.exp2(scores - new_top).astype(bf16)
            total[...] = total[...] * jnp.exp2(old_top - new_top) + dot(value, weights, 1, 0)
        top[...] = new_top

    visit(at, True)

    def step(key_at, carry):
        @pl.when((any_bits(seg_ref, key_at * per_tile, per_tile) & need) != 0)
        def _():
            visit(key_at, False)

        return carry

    lax.fori_loop(0, at, step, 0)
    final = total[...]
    weight_sum = final[HEAD : HEAD + 1, :]
    mixed = final[:HEAD, :] * (1.0 / weight_sum)
    lse = top[...] + jnp.log2(weight_sum)
    for j in range(per_tile):
        g = at * per_tile + j
        lanes = slice(j * CHUNK, (j + 1) * CHUNK)
        out_ref[g // per, :, pl.ds(pl.multiple_of(lax.rem(g, per) * CHUNK, CHUNK), CHUNK)] = mixed[:, lanes].astype(bf16)
        full_ref[g] = mixed[:, lanes]
        lse_ref[g] = lse[:, lanes]


def fwd_call(place, seg, need, qx, kx, qkv, tile=512):
    pieces, piece = len(qkv), qkv[0].shape[1]
    tokens = pieces * piece
    chunks = tokens // CHUNK
    return pl.pallas_call(
        functools.partial(fwd_kernel, tile=tile, pieces=pieces, extra=qx.shape[0]),
        grid=(tokens // tile,),
        out_shape=(
            jax.ShapeDtypeStruct((pieces, HEAD, piece), bf16),
            jax.ShapeDtypeStruct((chunks, HEAD, CHUNK), f32),
            jax.ShapeDtypeStruct((chunks, 1, CHUNK), f32),
        ),
        in_specs=[SMEM, SMEM, SMEM] + [VMEM] * (2 + pieces),
        out_specs=(VMEM, VMEM, VMEM),
        scratch_shapes=[
            pltpu.VMEM((tokens, 128), bf16),
            pltpu.VMEM((chunks, HEAD + 16, CHUNK), bf16),
            pltpu.VMEM((chunks, 128, CHUNK), bf16),
            pltpu.VMEM((1, tile), f32),
            pltpu.VMEM((HEAD + 16, tile), f32),
        ],
        compiler_params=pltpu.CompilerParams(vmem_limit_bytes=40 << 20),
        cost_estimate=pl.CostEstimate(flops=tokens * tokens * HEAD * 4, bytes_accessed=8 << 20, transcendentals=tokens * tokens // 2),
        name="attend",
    )(place, seg, need, qx, kx, *qkv)


def three_parts(row):
    at = lax.broadcasted_iota(jnp.int32, (16, row.shape[1]), 0)
    high = row.astype(bf16).astype(f32)
    rest = row - high
    mid = rest.astype(bf16).astype(f32)
    low = rest - mid
    return jnp.where(at == 0, high, jnp.where(at == 1, mid, jnp.where(at == 2, low, 0.0))).astype(bf16)


def unrotate(values, cosine, sine):
    a, b = values[:HALF], values[HALF:]
    return jnp.concatenate([a * cosine + b * sine, b * cosine - a * sine], axis=0)


def bwd_kernel(place_ref, seg_ref, need_ref, qx_ref, kx_ref, full_ref, lse_ref, cos_ref, sin_ref, *rest, tile, pieces, extra):
    qkv_refs, grad_refs = rest[:pieces], rest[pieces : 2 * pieces]
    out_ref, keys, values, queries, grads, key_lanes, key_sum, value_sum, query_sum = rest[2 * pieces :]
    at = pl.program_id(0)
    piece = qkv_refs[0].shape[1]
    per = piece // CHUNK

    @pl.when(at == 0)
    def _():
        minus = jnp.full((16, CHUNK), -1.0, bf16)
        pad_key = jnp.zeros((128 - HEAD - extra - 16, CHUNK), bf16)
        pad_value = jnp.zeros((128 - HEAD - 16, CHUNK), bf16)
        for p in range(pieces):
            place = piece_place(place_ref, p)
            for c in range(per):
                g = place * per + c
                lanes = slice(c * CHUNK, (c + 1) * CHUNK)
                rows = pl.ds(pl.multiple_of(g * CHUNK, CHUNK), CHUNK)
                ref = qkv_refs[p]
                key = ref[HEAD : 2 * HEAD, lanes]
                grad = grad_refs[p][:, lanes]
                key_lanes[g] = key
                keys[rows, :] = jnp.concatenate([key, kx_ref[:, rows], minus, pad_key], axis=0).T
                values[rows, :] = jnp.concatenate([ref[2 * HEAD :, lanes], minus, pad_value], axis=0).T
                queries[g] = jnp.concatenate([ref[:HEAD, lanes], qx_ref[:, rows], three_parts(lse_ref[g]), pad_key], axis=0)
                delta = jnp.sum(grad.astype(f32) * full_ref[g], axis=0, keepdims=True)
                grads[g] = jnp.concatenate([grad, three_parts(delta), pad_value], axis=0)
        key_sum[...] = jnp.zeros(key_sum.shape, f32)
        value_sum[...] = jnp.zeros(value_sum.shape, f32)

    per_tile = tile // CHUNK
    query = chunks_at(queries, at * per_tile, per_tile)
    grad = chunks_at(grads, at * per_tile, per_tile)
    need = any_bits(need_ref, at * per_tile, per_tile)

    def visit(key_at, diagonal):
        rows = pl.ds(pl.multiple_of(key_at * tile, tile), tile)
        scores = dot(keys[rows, :], query, 1, 0)
        if diagonal:
            scores = causal(scores, key_at * tile, at * tile)
        probs = jnp.exp2(scores)
        prob_grad = dot(values[rows, :], grad, 1, 0)
        score_grad = (probs * prob_grad).astype(bf16)
        query_part = dot(chunks_at(key_lanes, key_at * per_tile, per_tile), score_grad, 1, 0)
        value_part = dot(grad[:HEAD], probs.astype(bf16), 1, 1)
        key_part = dot(query[:HEAD], score_grad, 1, 1)
        if diagonal:
            query_sum[...] = query_part
        else:
            query_sum[...] += query_part
        for j in range(per_tile):
            lanes = slice(j * CHUNK, (j + 1) * CHUNK)
            value_sum[key_at * per_tile + j] += value_part[:, lanes]
            key_sum[key_at * per_tile + j] += key_part[:, lanes]

    visit(at, True)

    def step(key_at, carry):
        @pl.when((any_bits(seg_ref, key_at * per_tile, per_tile) & need) != 0)
        def _():
            visit(key_at, False)

        return carry

    lax.fori_loop(0, at, step, 0)
    for j in range(per_tile):
        g = at * per_tile + j
        lanes = slice(j * CHUNK, (j + 1) * CHUNK)
        rows = pl.ds(pl.multiple_of(g * CHUNK, CHUNK), CHUNK)
        out_ref[g // per, :HEAD, pl.ds(pl.multiple_of(lax.rem(g, per) * CHUNK, CHUNK), CHUNK)] = unrotate(
            query_sum[:, lanes] * SCORE_SCALE, cos_ref[:, rows], sin_ref[:, rows]
        ).astype(bf16)

    @pl.when(at == pl.num_programs(0) - 1)
    def _():
        for p in range(pieces):
            for c in range(per):
                g = p * per + c
                lanes = slice(c * CHUNK, (c + 1) * CHUNK)
                rows = slice(g * CHUNK, (g + 1) * CHUNK)
                out_ref[p, HEAD : 2 * HEAD, lanes] = unrotate(
                    key_sum[g] * (1.0 / LOG2E), cos_ref[:, rows], sin_ref[:, rows]
                ).astype(bf16)
                out_ref[p, 2 * HEAD :, lanes] = (0.5 * value_sum[g]).astype(bf16)


def bwd_call(place, seg, need, qx, kx, full, lse, cosine, sine, qkv, grads, tile=512):
    pieces, piece = len(qkv), qkv[0].shape[1]
    tokens = pieces * piece
    chunks = tokens // CHUNK
    return pl.pallas_call(
        functools.partial(bwd_kernel, tile=tile, pieces=pieces, extra=qx.shape[0]),
        grid=(tokens // tile,),
        out_shape=jax.ShapeDtypeStruct((pieces, 3 * HEAD, piece), bf16),
        in_specs=[SMEM, SMEM, SMEM] + [VMEM] * (6 + 2 * pieces),
        out_specs=VMEM,
        scratch_shapes=[
            pltpu.VMEM((tokens, 128), bf16),
            pltpu.VMEM((tokens, 128), bf16),
            pltpu.VMEM((chunks, 128, CHUNK), bf16),
            pltpu.VMEM((chunks, 128, CHUNK), bf16),
            pltpu.VMEM((chunks, HEAD, CHUNK), bf16),
            pltpu.VMEM((chunks, HEAD, CHUNK), f32),
            pltpu.VMEM((chunks, HEAD, CHUNK), f32),
            pltpu.VMEM((HEAD, tile), f32),
        ],
        compiler_params=pltpu.CompilerParams(vmem_limit_bytes=48 << 20),
        cost_estimate=pl.CostEstimate(flops=tokens * tokens * HEAD * 8, bytes_accessed=12 << 20, transcendentals=tokens * tokens // 2),
        name="attend_back",
    )(place, seg, need, qx, kx, full, lse, cosine, sine, *qkv, *grads)


def on_device(
    tokens, first_values, cotangent, parents, seg_lengths,
    w_query, w_key, w_value, w_out, w_gate, w_up, w_down, gain_attn, gain_ffn,
):
    assert tokens.shape[1] == 1
    fsdp_count, ctx_count, tp_count = (lax.axis_size(a) for a in ("fsdp", "ctx", "tp"))
    assert tp_count == 4
    fsdp_at, ctx_at, tp_at = (lax.axis_index(a) for a in ("fsdp", "ctx", "tp"))
    core_at, x_at = tp_at % 2, tp_at // 2
    own_rows, width = tokens.shape[0], tokens.shape[2]
    chip_rows = 2 * own_rows
    heads = w_query.shape[1] // HEAD
    assert heads == ctx_count
    tree_len = own_rows * tp_count * ctx_count
    weight_rows = w_query.shape[0]

    def over_core(value):
        return lax.ppermute(value, "tp", [(i, i ^ 1) for i in range(tp_count)])

    def over_x(value):
        return lax.ppermute(value, "tp", [(i, i ^ 2) for i in range(tp_count)])

    def ctx_shift(value, shift):
        return lax.ppermute(value, "ctx", [(i, (i + shift) % ctx_count) for i in range(ctx_count)])

    def fsdp_shift(value, shift):
        return lax.ppermute(value, "fsdp", [(i, (i + shift) % fsdp_count) for i in range(fsdp_count)])

    def by_core(own, other):
        return jnp.where(core_at == 0, jnp.concatenate([own, other], axis=0), jnp.concatenate([other, own], axis=0))

    def full_rows(shard):
        if fsdp_count != 2:
            return lax.all_gather(shard, "fsdp", axis=0, tiled=True)
        size = shard.shape[0]
        whole = jnp.zeros((size * fsdp_count,) + shard.shape[1:], shard.dtype)
        whole = lax.dynamic_update_slice_in_dim(whole, shard, fsdp_at * size, 0)
        for shift in range(1, fsdp_count):
            source = (fsdp_at - shift) % fsdp_count
            whole = lax.dynamic_update_slice_in_dim(whole, fsdp_shift(shard, shift), source * size, 0)
        return whole

    def reduce_grad(partial):
        if fsdp_count != 2:
            low = lax.psum_scatter(partial.astype(bf16), "fsdp", scatter_dimension=0, tiled=True)
            return lax.psum(low, "ctx").astype(f32)
        total = lax.dynamic_slice_in_dim(partial, fsdp_at * weight_rows, weight_rows, 0)
        for shift in range(1, fsdp_count):
            target = (fsdp_at + shift) % fsdp_count
            piece = lax.dynamic_slice_in_dim(partial, target * weight_rows, weight_rows, 0).astype(bf16)
            total = total + fsdp_shift(piece, shift).astype(f32)
        if ctx_count != 4:
            return lax.psum(total.astype(bf16), "ctx").astype(f32)
        low = total.astype(bf16)
        low = (low.astype(f32) + lax.ppermute(low, "ctx", [(0, 1), (3, 2)]).astype(f32)).astype(bf16)
        low = (low.astype(f32) + lax.ppermute(low, "ctx", [(1, 2), (2, 1)]).astype(f32)).astype(bf16)
        back = lax.ppermute(low, "ctx", [(1, 0), (2, 3)])
        return jnp.where((ctx_at == 0) | (ctx_at == 3), back, low).astype(f32)

    own_tokens, own_cot = tokens[:, 0, :], cotangent[:, 0, :]
    token_core = over_core(own_tokens)
    token_x = over_x(own_tokens)
    attention_gain = full_rows(gain_attn.reshape(weight_rows, 1)).reshape(1, width).astype(f32)
    w_query, w_key, w_value = full_rows(w_query), full_rows(w_key), full_rows(w_value)
    token_x_core = over_core(token_x)
    qkv_weight = jnp.concatenate([w_query, w_key, w_value], axis=1)
    out_weight = full_rows(w_out)
    out_weight_x = over_x(out_weight)
    cot_core = over_core(own_cot)
    cot_x = over_x(own_cot)
    cot_x_core = over_core(cot_x)
    down_weight = full_rows(w_down)
    gate_weight = full_rows(w_gate)
    up_weight = full_rows(w_up)
    ffn_gain = full_rows(gain_ffn.reshape(weight_rows, 1)).reshape(1, width).astype(f32)

    place = jnp.stack([ctx_at, x_at, jnp.full_like(ctx_at, ctx_count)]).astype(jnp.int32)
    position, query_extra, key_extra, seg_bits, need_bits = layout_call(parents, seg_lengths, tree_len)
    frequency = jnp.exp(-math.log(10000.0) * jnp.arange(HALF, dtype=f32) / HALF)
    angles = frequency[:, None] * position
    cosine, sine = jnp.cos(angles), jnp.sin(angles)

    def normalize(rows_f32):
        return lax.rsqrt(jnp.mean(rows_f32 * rows_f32, axis=-1, keepdims=True) + epsilon)

    first_flat = first_values[:, 0, :]

    def project(rows, x_half):
        single = rows.astype(f32)
        unit = single * normalize(single)
        normed = (unit * attention_gain).astype(bf16)
        projected = dot(qkv_weight, normed, 0, 1).reshape(3, heads, HEAD, chip_rows)
        where_at = (ctx_at * 2 + x_half) * chip_rows
        cos_own = lax.dynamic_slice_in_dim(cosine, where_at, chip_rows, 1)
        sin_own = lax.dynamic_slice_in_dim(sine, where_at, chip_rows, 1)
        a, b = projected[:2, :, :HALF], projected[:2, :, HALF:]
        turned = jnp.concatenate([a * cos_own - b * sin_own, b * cos_own + a * sin_own], axis=2)
        first = lax.dynamic_slice_in_dim(first_flat, x_half * chip_rows, chip_rows, 0).T.reshape(heads, HEAD, chip_rows)
        value = 0.5 * projected[2] + 0.5 * first.astype(f32)
        joined = jnp.stack([turned[0] * QUERY_SCALE, turned[1], value], axis=1).astype(bf16)
        return joined.reshape(heads, 3 * HEAD, chip_rows), normed

    def head_exchange(by_head):
        received = []
        for shift in range(ctx_count):
            piece = lax.dynamic_index_in_dim(by_head, (ctx_at + shift) % ctx_count, 0, keepdims=False)
            received.append(ctx_shift(piece, shift) if shift else piece)
        return received

    chip_tokens = by_core(own_tokens, token_core)
    far_tokens = by_core(token_x, token_x_core)
    near_qkv, near_normed = project(chip_tokens, x_at)
    near_pieces = head_exchange(near_qkv)
    far_qkv, far_normed = project(far_tokens, 1 - x_at)
    far_pieces = head_exchange(far_qkv)
    qkv = [p for pair in zip(near_pieces, far_pieces) for p in pair]

    mixed_all, mixed_full, log_total = fwd_call(place, seg_bits, need_bits, query_extra, key_extra, qkv)

    def token_exchange(pieces, half, feature):
        buffer = jnp.zeros((feature // HEAD, heads, HEAD, chip_rows), bf16)
        for shift in range(ctx_count):
            target = (ctx_at + shift) % ctx_count
            piece = lax.dynamic_index_in_dim(pieces, target * 2 + half, 0, keepdims=False)
            got = ctx_shift(piece, shift) if shift else piece
            source = (ctx_at - shift) % ctx_count
            buffer = lax.dynamic_update_slice(
                buffer, got.reshape(feature // HEAD, 1, HEAD, chip_rows), (0, source, 0, 0)
            )
        return buffer.reshape(feature * heads, chip_rows)

    far_mixed = token_exchange(mixed_all, 1 - x_at, HEAD)
    far_mixed_recv = over_x(far_mixed)
    near_mixed = token_exchange(mixed_all, x_at, HEAD)

    middle_part = dot(near_mixed, out_weight, 0, 1) + dot(far_mixed_recv, out_weight_x, 0, 1)
    other_part = lax.dynamic_slice_in_dim(middle_part, (1 - core_at) * own_rows, own_rows, 0).astype(bf16)
    own_part = lax.dynamic_slice_in_dim(middle_part, core_at * own_rows, own_rows, 0)
    middle = own_tokens.astype(f32) + own_part + over_core(other_part).astype(f32)

    middle_scale = normalize(middle)
    ffn_own = (middle * middle_scale * ffn_gain).astype(bf16)
    ffn_core = over_core(ffn_own)
    ffn_x = over_x(ffn_own)
    ffn_x_core = over_core(ffn_x)

    def feed(rows, cot_rows):
        gate = dot(rows, gate_weight, 1, 0)
        up = dot(rows, up_weight, 1, 0)
        hidden_grad = dot(cot_rows, down_weight, 1, 0)
        sig = 1.0 / (1.0 + jnp.exp(-gate))
        act = gate * sig
        hidden = (act * up).astype(bf16)
        gate_grad = (hidden_grad * up * (sig * (1.0 + gate * (1.0 - sig)))).astype(bf16)
        up_grad = (hidden_grad * act).astype(bf16)
        result = dot(hidden, down_weight, 1, 1)
        back = dot(gate_grad, gate_weight, 1, 1) + dot(up_grad, up_weight, 1, 1)
        return hidden, gate_grad, up_grad, result, back

    near_ffn = jnp.concatenate([ffn_own, ffn_core], axis=0)
    far_ffn = jnp.concatenate([ffn_x, ffn_x_core], axis=0)
    near_cot = jnp.concatenate([own_cot, cot_core], axis=0)
    far_cot = jnp.concatenate([cot_x, cot_x_core], axis=0)
    near_hidden, near_gate, near_up, near_result, near_back = feed(near_ffn, near_cot)
    far_hidden, far_gate, far_up, far_result, far_back = feed(far_ffn, far_cot)

    def scatter_rows(near, far):
        far_sum = far[:own_rows] + over_core(far[own_rows:].astype(bf16)).astype(f32)
        near_sum = near[:own_rows] + over_core(near[own_rows:].astype(bf16)).astype(f32)
        return near_sum + over_x(far_sum.astype(bf16)).astype(f32)

    ffn_grad = scatter_rows(near_back, far_back)
    weighted = ffn_grad * ffn_gain
    middle_grad = (
        own_cot.astype(f32)
        + middle_scale * weighted
        - middle * (middle_scale**3 * jnp.mean(weighted * middle, axis=-1, keepdims=True))
    )
    ffn_gain_part = jnp.sum(ffn_grad * middle * middle_scale, axis=0)
    middle_low = middle_grad.astype(bf16)
    low_core = over_core(middle_low)
    chip_low = by_core(middle_low, low_core)
    far_heads = dot(out_weight_x, chip_low, 0, 1).astype(bf16)
    far_out_grad = over_x(far_heads).reshape(heads, HEAD, chip_rows)
    near_out_grad = dot(out_weight, chip_low, 0, 1).astype(bf16).reshape(heads, HEAD, chip_rows)
    near_grads = head_exchange(near_out_grad)
    far_grads = head_exchange(far_out_grad)
    grads = [p for pair in zip(near_grads, far_grads) for p in pair]

    layer_out = (middle + scatter_rows(near_result, far_result)).astype(bf16)
    grad_down = reduce_grad(dot(near_cot, near_hidden, 0, 0) + dot(far_cot, far_hidden, 0, 0))
    grad_gate = reduce_grad(dot(near_ffn, near_gate, 0, 0) + dot(far_ffn, far_gate, 0, 0))
    grad_up = reduce_grad(dot(near_ffn, near_up, 0, 0) + dot(far_ffn, far_up, 0, 0))
    low_x = over_x(middle_low)
    far_low = by_core(low_x, over_core(low_x))
    grad_out = reduce_grad(dot(chip_low, near_mixed, 0, 1) + dot(far_low, far_mixed, 0, 1))

    back_all = bwd_call(
        place, seg_bits, need_bits, query_extra, key_extra, mixed_full, log_total, cosine, sine, qkv, grads
    )
    far_projected = token_exchange(back_all, 1 - x_at, 3 * HEAD)
    near_projected = token_exchange(back_all, x_at, 3 * HEAD)

    far_normed_grad = dot(far_projected, qkv_weight, 0, 1)
    near_normed_grad = dot(near_projected, qkv_weight, 0, 1)

    def split_core(rows):
        mine = lax.dynamic_slice_in_dim(rows, core_at * own_rows, own_rows, 0)
        other = lax.dynamic_slice_in_dim(rows, (1 - core_at) * own_rows, own_rows, 0)
        return mine, other.astype(bf16)

    far_mine, far_other = split_core(far_normed_grad)
    far_sum = (far_mine + over_core(far_other).astype(f32)).astype(bf16)
    near_mine, near_other = split_core(near_normed_grad)
    normed_grad = near_mine + over_core(near_other).astype(f32) + over_x(far_sum).astype(f32)

    single = own_tokens.astype(f32)
    scale = normalize(single)
    weighted = normed_grad * attention_gain
    grad_tokens = (
        middle_grad + scale * weighted - single * (scale**3 * jnp.mean(weighted * single, axis=-1, keepdims=True))
    )
    attention_gain_part = jnp.sum(normed_grad * single * scale, axis=0)

    grad_qkv = dot(near_normed, near_projected, 0, 1) + dot(far_normed, far_projected, 0, 1)
    head_width = heads * HEAD
    grad_query = reduce_grad(grad_qkv[:, :head_width])
    grad_key = reduce_grad(grad_qkv[:, head_width : 2 * head_width])
    grad_value = reduce_grad(grad_qkv[:, 2 * head_width :])

    gains = lax.psum(jnp.stack([attention_gain_part, ffn_gain_part]), ("fsdp", "ctx", "tp"))
    gains = lax.dynamic_slice_in_dim(gains, fsdp_at * weight_rows, weight_rows, 1)

    near_value = near_projected[2 * head_width :].T.astype(f32)
    far_value = far_projected[2 * head_width :].T.astype(f32)
    grad_values = jnp.where(
        x_at == 0, jnp.concatenate([near_value, far_value], axis=0), jnp.concatenate([far_value, near_value], axis=0)
    )
    return (
        layer_out[:, None, :],
        grad_tokens[:, None, :],
        grad_values[:, None, :],
        grad_query,
        grad_key,
        grad_value,
        grad_out,
        grad_gate,
        grad_up,
        grad_down,
        gains[0],
        gains[1],
    )


def solution(mesh):
    rows, columns = P(("ctx", "tp"), "fsdp", None), P("ctx", "fsdp", "tp")
    weight, gain = P("fsdp", "tp"), P("fsdp")
    return jax.shard_map(
        on_device,
        mesh=mesh,
        in_specs=(rows, columns, rows, P("fsdp", None), P("fsdp", None)) + (weight,) * 7 + (gain,) * 2,
        out_specs=(rows, rows, columns) + (weight,) * 7 + (gain,) * 2,
        check_vma=False,
    )
```

```python
import functools
import math

import jax
import jax.numpy as jnp
from jax import lax
from jax.experimental import pallas as pl
from jax.experimental.pallas import tpu as pltpu
from jax.sharding import PartitionSpec as P

HEAD = 64
HALF = HEAD // 2
BIG = 1e30
LOG2E = 1.4426950408889634
SCORE_SCALE = HEAD**-0.5
QUERY_SCALE = SCORE_SCALE * LOG2E
epsilon = 1e-05
f32 = jnp.float32
bf16 = jnp.bfloat16


def dot(a, b, ca, cb):
    return lax.dot_general(a, b, (((ca,), (cb,)), ((), ())), preferred_element_type=f32)


def layout_kernel(par_ref, len_ref, pos_ref, qx_ref, kx_ref, seg_ref, need_ref, anc_sc, above_sc, *, segs, tokens, piece):
    token = lax.broadcasted_iota(jnp.int32, (1, tokens), 1)
    pos = jnp.zeros((1, tokens), jnp.int32)
    seg_of = jnp.full((1, tokens), -1, jnp.int32)
    bits = jnp.zeros((1, tokens), jnp.int32)
    for b in range(tokens // piece):
        seg_ref[b] = 0
        need_ref[b] = 0
    off = jnp.int32(0)
    for s in range(segs):
        length = len_ref[0, s]
        if s == 0:
            anc, above = jnp.int32(1), jnp.int32(0)
        else:
            parent = par_ref[0, s]
            anc = anc_sc[parent] | jnp.int32(1 << s)
            above = above_sc[parent] + len_ref[0, parent]
        anc_sc[s] = anc
        above_sc[s] = above
        started = token >= off
        seg_of = jnp.where(started, s, seg_of)
        pos = jnp.where(started, token - off + above, pos)
        bits = jnp.where(started, anc, bits)

        def mark(b, carry, anc=anc, s=s):
            seg_ref[b] = seg_ref[b] | jnp.int32(1 << s)
            need_ref[b] = need_ref[b] | anc
            return carry

        lax.fori_loop(off // piece, (off + length - 1) // piece + 1, mark, 0)
        off = off + length
    row = lax.broadcasted_iota(jnp.int32, (kx_ref.shape[1], tokens), 0)
    key_extra = jnp.where(row == seg_of, -BIG, 0.0).astype(bf16)
    linked = lax.shift_right_logical(jnp.broadcast_to(bits, row.shape), row) & 1
    query_extra = jnp.where(linked == 1, 0.0, 1.0).astype(bf16)
    for p in range(tokens // piece):
        lanes = slice(p * piece, (p + 1) * piece)
        pos_ref[p] = pos[:, lanes].astype(f32)
        kx_ref[p] = key_extra[:, lanes]
        qx_ref[p] = query_extra[:, lanes]


SMEM = pl.BlockSpec(memory_space=pltpu.SMEM)
VMEM = pl.BlockSpec(memory_space=pltpu.VMEM)


def layout_call(parents, lengths, tokens, piece):
    segs = parents.shape[-1]
    rows = -(-segs // 16) * 16
    return pl.pallas_call(
        functools.partial(layout_kernel, segs=segs, tokens=tokens, piece=piece),
        out_shape=(
            jax.ShapeDtypeStruct((tokens // piece, 1, piece), f32),
            jax.ShapeDtypeStruct((tokens // piece, rows, piece), bf16),
            jax.ShapeDtypeStruct((tokens // piece, rows, piece), bf16),
            jax.ShapeDtypeStruct((tokens // piece,), jnp.int32),
            jax.ShapeDtypeStruct((tokens // piece,), jnp.int32),
        ),
        in_specs=[SMEM, SMEM],
        out_specs=(VMEM, VMEM, VMEM, SMEM, SMEM),
        scratch_shapes=[pltpu.SMEM((segs,), jnp.int32), pltpu.SMEM((segs,), jnp.int32)],
        cost_estimate=pl.CostEstimate(flops=0, bytes_accessed=1 << 16, transcendentals=0),
        name="layout",
    )(parents, lengths)


def causal(scores):
    key_at = lax.broadcasted_iota(jnp.int32, scores.shape, 0)
    query_at = lax.broadcasted_iota(jnp.int32, scores.shape, 1)
    return jnp.where(key_at <= query_at, scores, -BIG)


def three_parts(row):
    at = lax.broadcasted_iota(jnp.int32, (16, row.shape[1]), 0)
    high = row.astype(bf16).astype(f32)
    rest = row - high
    mid = rest.astype(bf16).astype(f32)
    low = rest - mid
    return jnp.where(at == 0, high, jnp.where(at == 1, mid, jnp.where(at == 2, low, 0.0))).astype(bf16)


def unrotate(values, cosine, sine):
    a, b = values[:HALF], values[HALF:]
    return jnp.concatenate([a * cosine + b * sine, b * cosine - a * sine], axis=0)


def prep_kernel(place_ref, qx_ref, kx_ref, got_ref, keys, key_lanes, value_lanes, values, queries):
    piece = got_ref.shape[2] // 2
    extra = qx_ref.shape[1]
    minus = jnp.full((16, piece), -1.0, bf16)
    pad_key = jnp.zeros((128 - HEAD - extra - 16, piece), bf16)
    pad_value = jnp.zeros((128 - HEAD - 16, piece), bf16)
    for half in (0, 1):
        for p in range(got_ref.shape[0]):
            at = 2 * p + (place_ref[0] ^ half)
            got = got_ref[p, :, half * piece : (half + 1) * piece]
            query, key, value = got[:HEAD, :], got[HEAD : 2 * HEAD, :], got[2 * HEAD :, :]
            key_lanes[at] = key
            keys[at] = jnp.concatenate([key, kx_ref[at], minus, pad_key], axis=0).T
            value_lanes[at] = jnp.concatenate([value, -minus], axis=0)
            values[at] = jnp.concatenate([value, minus, pad_value], axis=0).T
            queries[at] = jnp.concatenate([query, qx_ref[at], jnp.zeros((128 - HEAD - extra, piece), bf16)], axis=0)


def shape_of(*sizes, dtype=bf16):
    return jax.ShapeDtypeStruct(sizes, dtype)


def call(kernel, name, out_shape, operands, scratch=(), scalars=1, mib=20, late=()):
    outs = out_shape if isinstance(out_shape, tuple) else (out_shape,)
    arrays = operands[scalars:]
    count, total = len(arrays), len(arrays) + len(outs)

    def body(*refs):
        first, rest = refs[:scalars], refs[scalars:]
        outside, inside, sems, rest = rest[:total], rest[total : 2 * total], rest[2 * total], rest[2 * total + 1 :]
        copies = [pltpu.make_async_copy(outside[i], inside[i], sems.at[i]) for i in range(count)]
        for copy in copies:
            copy.start()
        for i in range(count):
            if i not in late:
                copies[i].wait()
        more = {"ready": lambda: [copies[i].wait() for i in late]} if late else {}
        kernel(*first, *inside, *rest, **more)
        copies = [pltpu.make_async_copy(inside[i], outside[i], sems.at[i]) for i in range(count, total)]
        for copy in copies:
            copy.start()
        for copy in copies:
            copy.wait()

    got = pl.pallas_call(
        body,
        out_shape=outs,
        in_specs=[SMEM] * scalars + [pl.BlockSpec(memory_space=pltpu.HBM)] * count,
        out_specs=(pl.BlockSpec(memory_space=pltpu.HBM),) * len(outs),
        scratch_shapes=[pltpu.VMEM(x.shape, x.dtype) for x in (*arrays, *outs)]
        + [pltpu.SemaphoreType.DMA((total,))]
        + list(scratch),
        compiler_params=pltpu.CompilerParams(vmem_limit_bytes=60 << 20),
        cost_estimate=pl.CostEstimate(flops=0, bytes_accessed=1 << 16, transcendentals=0),
        name=name,
    )(*operands)
    return got if isinstance(out_shape, tuple) else got[0]


def prep_call(place, qx, kx, got):
    pieces, piece = 2 * got.shape[0], got.shape[2] // 2
    return call(
        prep_kernel,
        "prepare",
        (
            shape_of(pieces, piece, 128),
            shape_of(pieces, HEAD, piece),
            shape_of(pieces, HEAD + 16, piece),
            shape_of(pieces, piece, 128),
            shape_of(pieces, 128, piece),
        ),
        (place, qx, kx, got),
    )


def norm_kernel(place_ref, own_ref, other_ref, gain_ref, out_ref, *, swap):
    rows, width = own_ref.shape
    for half, ref in enumerate((own_ref, other_ref)):
        single = ref[...].astype(f32)
        scale = lax.rsqrt(jnp.mean(single * single, axis=-1, keepdims=True) + epsilon)
        if swap:
            turned = jnp.concatenate([single[:, width // 2 :], single[:, : width // 2]], axis=1)
            single = jnp.where(place_ref[3] == 0, single, turned)
        at = pl.multiple_of((place_ref[1] ^ half) * rows, rows)
        out_ref[pl.ds(at, rows), :] = (single * scale * gain_ref[...]).astype(bf16)


def norm_call(place, own, other, gain, swap):
    return call(
        functools.partial(norm_kernel, swap=swap), "normalise", shape_of(2 * own.shape[0], own.shape[1]),
        (place, own, other, gain), mib=16,
    )


def cut(ref, count):
    size = ref.shape[1] // count
    return [ref[:, i * size : (i + 1) * size] for i in range(count)]


def project_kernel(place_ref, near_ref, far_ref, cos_ref, sin_ref, first_ref, *rest, count):
    weights, (out, raw) = rest[:count], rest[count:]
    width = raw.shape[0] // 3
    size = near_ref.shape[1] // count
    piece = near_ref.shape[0]
    turned = [[w[i * size : (i + 1) * size, :].T for w in weights] for i in range(3)]
    for half, rows_ref in enumerate((near_ref, far_ref)):
        rows = cut(rows_ref, count)
        for i in range(3):
            raw[i * width : (i + 1) * width, :] = sum(dot(w, r, 1, 1) for w, r in zip(turned[i], rows))
        x_half = place_ref[0] ^ half
        at = 2 * place_ref[2] + x_half
        cosine, sine = cos_ref[at], sin_ref[at]
        start = pl.multiple_of(x_half * piece, piece)
        first = first_ref[pl.ds(start, piece), :].astype(f32).T

        def turn(values):
            a, b = values[:HALF], values[HALF:]
            return jnp.concatenate([a * cosine - b * sine, b * cosine + a * sine], axis=0)

        lanes = slice(half * piece, (half + 1) * piece)
        for at in range(width // HEAD):
            rows_at = [slice(i * width + at * HEAD, i * width + (at + 1) * HEAD) for i in range(3)]
            value = 0.5 * raw[rows_at[2], :] + 0.5 * first[at * HEAD : (at + 1) * HEAD]
            out[at, :HEAD, lanes] = (turn(raw[rows_at[0], :]) * QUERY_SCALE).astype(bf16)
            out[at, HEAD : 2 * HEAD, lanes] = turn(raw[rows_at[1], :]).astype(bf16)
            out[at, 2 * HEAD :, lanes] = value.astype(bf16)


def project_call(place, near, far, cosine, sine, first, weights):
    piece, width = near.shape[0], weights[0].shape[1]
    return call(
        functools.partial(project_kernel, count=len(weights)), "project",
        shape_of(width // HEAD, 3 * HEAD, 2 * piece),
        (place, near, far, cosine, sine, first, *weights),
        scratch=[pltpu.VMEM((3 * width, piece), f32)],
    )


def stack_kernel(*refs):
    out, at = refs[-1], 0
    for ref in refs[:-1]:
        rows = ref.shape[0]
        out[at : at + rows, :] = ref[...]
        at += rows


def pick_kernel(*refs):
    out = refs[-1]
    rows = out.shape[0]
    size = out.shape[1] // (len(refs) - 1)
    for i, ref in enumerate(refs[:-1]):
        out[:, i * size : (i + 1) * size] = ref[ref.shape[0] - rows :, :]


def pick_call(blocks, rows):
    return call(pick_kernel, "pick", shape_of(rows, blocks[0].shape[1] * len(blocks)), tuple(blocks), scalars=0)


def stack_call(*arrays):
    rows = sum(a.shape[0] for a in arrays)
    return call(stack_kernel, "stack", shape_of(rows, arrays[0].shape[1]), arrays, scalars=0, mib=16)


def split_core(place_ref, total, mine_ref, other_ref):
    rows = mine_ref.shape[0]
    mine_ref[...] = total[pl.ds(pl.multiple_of(place_ref[1] * rows, rows), rows), :]
    other_ref[...] = total[pl.ds(pl.multiple_of((1 - place_ref[1]) * rows, rows), rows), :].astype(bf16)


def output_kernel(place_ref, near_ref, far_ref, *rest):
    near_weight, far_weight, mine_ref, other_ref, total = rest
    total[...] = dot(near_ref[...].T, near_weight[...], 1, 0) + dot(far_ref[...].T, far_weight[...], 1, 0)
    split_core(place_ref, total, mine_ref, other_ref)


def output_call(place, near, far, near_weight, far_weight):
    rows, width = near.shape[1], near_weight.shape[1]
    return call(
        output_kernel, "out_project",
        (shape_of(rows // 2, width, dtype=f32), shape_of(rows // 2, width)),
        (place, near, far, near_weight, far_weight),
        scratch=[pltpu.VMEM((rows, width), f32)],
    )


def heads_kernel(place_ref, own_ref, other_ref, near_weight, far_weight, near_out, far_out, chip):
    rows = own_ref.shape[0]
    for half, ref in enumerate((own_ref, other_ref)):
        chip[pl.ds(pl.multiple_of((place_ref[1] ^ half) * rows, rows), rows), :] = ref[...]
    far_out[...] = dot(far_weight[...], chip[...], 1, 1).astype(bf16)
    near_out[...] = dot(near_weight[...], chip[...], 1, 1).astype(bf16)


def heads_call(place, own, other, near_weight, far_weight):
    rows, columns = 2 * own.shape[0], near_weight.shape[0]
    return call(
        heads_kernel, "out_back",
        (shape_of(columns, rows), shape_of(columns, rows), shape_of(rows, own.shape[1])),
        (place, own, other, near_weight, far_weight),
    )


def feed_kernel(rows_ref, other_ref, cot_ref, cot_other_ref, *rest, count):
    hidden = rest[count].shape[2]
    gate_w, up_w, down_w = ([w.at[i * hidden : (i + 1) * hidden] for w in rest[:count]] for i in range(3))
    hidden_ref, gate_ref, up_ref, mine_ref, sent_ref, rows_sc, cot_sc, back_sc = rest[count:]
    size = rows_ref.shape[0]
    rows_sc[0], rows_sc[1] = rows_ref[...], other_ref[...]
    cot_sc[0], cot_sc[1] = cot_ref[...], cot_other_ref[...]
    block = rows_ref.shape[1] // count

    def step(at, carry):
        lanes = [slice(i * block, (i + 1) * block) for i in range(count)]
        rows, cots = [rows_sc[at, :, s] for s in lanes], [cot_sc[at, :, s] for s in lanes]
        gate = sum(dot(r, w[...], 1, 1) for r, w in zip(rows, gate_w))
        up = sum(dot(r, w[...], 1, 1) for r, w in zip(rows, up_w))
        hidden_grad = sum(dot(r, w[...], 1, 1) for r, w in zip(cots, down_w))
        sig = 1.0 / (1.0 + jnp.exp(-gate))
        act = gate * sig
        hidden_ref[at] = (act * up).astype(bf16)
        gate_grad = (hidden_grad * up * (sig * (1.0 + gate * (1.0 - sig)))).astype(bf16)
        up_grad = (hidden_grad * act).astype(bf16)
        gate_ref[at] = gate_grad
        up_ref[at] = up_grad
        for i in range(count):
            back_sc[at, :, lanes[i]] = dot(gate_grad, gate_w[i][...], 1, 0) + dot(up_grad, up_w[i][...], 1, 0)
        return carry

    lax.fori_loop(0, 2, step, 0)
    mine_ref[...] = back_sc[0]
    sent_ref[...] = back_sc[1].astype(bf16)


def feed_call(rows, other, cot, cot_other, weights, hidden):
    size, width = rows.shape
    count = len(weights)
    return call(
        functools.partial(feed_kernel, count=count), "feed",
        (shape_of(2, size, hidden),) * 3 + (shape_of(size, width, dtype=f32), shape_of(size, width)),
        (rows, other, cot, cot_other, *weights),
        scratch=[pltpu.VMEM((2, size, width), bf16)] * 2 + [pltpu.VMEM((2, size, width), f32)],
        scalars=0, mib=40,
    )


def prep_back_kernel(place_ref, queries, near_grad, far_grad, near_full, far_full, near_lse, far_lse, queries_out, grads_out, *, extra):
    places, _, piece = near_grad.shape
    queries_out[...] = queries[...]
    pad = jnp.zeros((128 - HEAD - 16, piece), bf16)
    for half, (grad, full, lse) in enumerate(((near_grad, near_full, near_lse), (far_grad, far_full, far_lse))):
        for p in range(places):
            at = 2 * p + (place_ref[0] ^ half)
            queries_out[at, HEAD + extra : HEAD + extra + 16, :] = lse[p]
            delta = jnp.sum(grad[p].astype(f32) * full[p], axis=0, keepdims=True)
            grads_out[at] = jnp.concatenate([grad[p], three_parts(delta), pad], axis=0)


def prep_back_call(place, queries, extra, *rest):
    return call(
        functools.partial(prep_back_kernel, extra=extra), "prepare_back",
        (shape_of(*queries.shape), shape_of(*queries.shape)), (place, queries, *rest), mib=16,
    )


def weights_kernel(near_rows, far_rows, far_kv, last, *rest, count):
    width = near_rows.shape[1] // count
    columns = far_kv.shape[0] * HEAD
    flat = lambda ref, at: ref[:, at * HEAD : (at + 1) * HEAD, :].reshape(columns, ref.shape[2])
    pairs = ((flat(last, 2), flat(last, 3)), (flat(last, 0), flat(far_kv, 0)), (flat(last, 1), flat(far_kv, 1)))
    for i, (near, far) in enumerate(pairs):
        for b in range(count):
            lanes = slice(b * width, (b + 1) * width)
            total = dot(near, near_rows[:, lanes], 1, 0) + dot(far, far_rows[:, lanes], 1, 0)
            rest[b][i * width : (i + 1) * width, :] = total.T.astype(bf16)


def weights_call(near_rows, far_rows, far_kv, last, count):
    width, columns = near_rows.shape[1] // count, far_kv.shape[0] * HEAD
    return call(
        functools.partial(weights_kernel, count=count), "weight_grads",
        tuple(shape_of(3 * width, columns) for _ in range(count)),
        (near_rows, far_rows, far_kv, last), scalars=0,
    )


def rows_kernel(place_ref, rows_ref, kv, last, *rest, half, count):
    weights, (mine_ref, other_ref, gain_ref, total) = rest[:count], rest[count:]
    columns = kv.shape[0] * HEAD
    flat = lambda ref, at: ref[:, at * HEAD : (at + 1) * HEAD, :].reshape(columns, ref.shape[2])
    if half:
        grads = flat(last, 3), flat(kv, 0), flat(kv, 1)
    else:
        grads = flat(last, 2), flat(last, 0), flat(last, 1)
    grads = [g.T for g in grads]
    size = total.shape[1] // count
    for i in range(count):
        part = sum(dot(g, weights[i][j * size : (j + 1) * size, :], 1, 1) for j, g in enumerate(grads))
        lanes = slice(i * size, (i + 1) * size)
        total[:, lanes] = part
        gain_ref[:, lanes] = jnp.sum(part * rows_ref[:, lanes].astype(f32), axis=0, keepdims=True)
    split_core(place_ref, total, mine_ref, other_ref)


def rows_call(place, rows, kv, last, weights, half):
    size, width = rows.shape
    return call(
        functools.partial(rows_kernel, half=half, count=len(weights)), "rows_back",
        (shape_of(size // 2, width, dtype=f32), shape_of(size // 2, width), shape_of(1, width, dtype=f32)),
        (place, rows, kv, last, *weights),
        scratch=[pltpu.VMEM((size, width), f32)],
    )


def feed_grads_kernel(near_gate, far_gate, near_up, far_up, near_hidden, far_hidden, *refs):
    rows, cots, outs = refs[:4], refs[4:8], refs[8:]
    count = len(outs) // 2
    size = rows[0].shape[1] // count
    hidden = near_gate.shape[2]
    pairs = ((near_gate, far_gate, rows), (near_up, far_up, rows), (near_hidden, far_hidden, cots))
    for b in range(count):
        lanes = slice(b * size, (b + 1) * size)
        for i, (near, far, right) in enumerate(pairs):
            near, far = (ref[...].reshape(2 * ref.shape[1], hidden) for ref in (near, far))
            near_right, far_right = (jnp.concatenate([right[j][:, lanes], right[j + 1][:, lanes]], axis=0) for j in (0, 2))
            total = (dot(near, near_right, 0, 0) + dot(far, far_right, 0, 0)).astype(bf16)
            if i < 2:
                outs[b][i * hidden : (i + 1) * hidden, :] = total
            else:
                outs[count + b][...] = total


def feed_grads_call(lefts, hiddens, rows, cots, count):
    hidden, size = lefts[0].shape[2], rows[0].shape[1] // count
    outs = call(
        feed_grads_kernel, "feed_grads",
        (shape_of(2 * hidden, size),) * count + (shape_of(hidden, size),) * count,
        (*lefts, *hiddens, *rows, *cots), scalars=0, mib=40,
    )
    return outs[:count], outs[count:]


def result_kernel(near_hidden, far_hidden, *rest, count):
    weights, (near_mine, far_mine, sent) = rest[:count], rest[count:]
    size = near_mine.shape[1] // count
    for at, (ref, mine) in enumerate(((near_hidden, near_mine), (far_hidden, far_mine))):
        for i in range(count):
            lanes = slice(i * size, (i + 1) * size)
            weight = weights[i][2 * ref.shape[2] : 3 * ref.shape[2], :]
            mine[:, lanes] = dot(ref[0], weight, 1, 0)
            sent[at, :, lanes] = dot(ref[1], weight, 1, 0).astype(bf16)


def result_call(near_hidden, far_hidden, weights):
    _, size, _ = near_hidden.shape
    count = len(weights)
    width = weights[0].shape[1] * count
    return call(
        functools.partial(result_kernel, count=count), "result",
        (shape_of(size, width, dtype=f32), shape_of(size, width, dtype=f32), shape_of(2, size, width)),
        (near_hidden, far_hidden, *weights), scalars=0, mib=24,
    )


def out_grads_kernel(place_ref, chip_low, far_own, far_other, near_mixed, far_mixed, *rest):
    outs, far_low = rest[:-1], rest[-1]
    count = len(outs)
    rows = far_own.shape[0]
    for half, ref in enumerate((far_own, far_other)):
        far_low[pl.ds(pl.multiple_of((place_ref[1] ^ half) * rows, rows), rows), :] = ref[...]
    near, far = near_mixed[...], far_mixed[...]
    for out, near_rows, far_rows in zip(outs, cut(chip_low, count), cut(far_low, count)):
        out[...] = (dot(near, near_rows, 1, 0) + dot(far, far_rows, 1, 0)).T.astype(bf16)


def out_grads_call(place, chip_low, far_own, far_other, near_mixed, far_mixed, count):
    width, columns = chip_low.shape[1] // count, near_mixed.shape[0]
    return call(
        out_grads_kernel, "out_grads", tuple(shape_of(width, columns) for _ in range(count)),
        (place, chip_low, far_own, far_other, near_mixed, far_mixed),
        scratch=[pltpu.VMEM(chip_low.shape, bf16)],
    )


def join_kernel(*refs):
    count = len(refs) // 3
    for i in range(count):
        a, b, out = refs[2 * i], refs[2 * i + 1], refs[2 * count + i]
        out[...] = (a[...].astype(f32) + b[...].astype(f32)).astype(bf16)


def join_call(*pairs):
    outs = call(
        join_kernel, "join", tuple(shape_of(*a.shape) for a, _ in pairs), [x for pair in pairs for x in pair],
        scalars=0, mib=16,
    )
    return list(outs)


def collect(first, last, hit, todo):
    def step(at, count):
        todo[count] = at
        return count + hit(at).astype(jnp.int32)

    return lax.fori_loop(first, last, step, jnp.int32(0))


def two_ahead(count, todo, first, fill, work):
    def step(j, now):
        middle, after = todo[2 * j], todo[2 * j + 1]
        fill(1, middle)
        work(0, now)
        fill(0, after)
        work(1, middle)
        return after

    last = lax.fori_loop(0, count // 2, step, first)

    @pl.when(lax.rem(count, 2) == 0)
    def _():
        work(0, last)

    @pl.when(lax.rem(count, 2) == 1)
    def _():
        final = todo[count - 1]
        fill(1, final)
        work(0, last)
        work(1, final)


def fwd_kernel(todo_ref, seg_ref, need_ref, keys, values, queries, out_ref, full_ref, lse_ref, score_a, score_b, top, total, todo):
    scores = (score_a, score_b)

    def attend(i, carry):
        at = todo_ref[i]
        need = need_ref[at]
        count = collect(0, at, lambda k: (seg_ref[k] & need) != 0, todo)
        query = queries[at]
        score_a[...] = causal(dot(keys[at], query, 1, 0))
        top[...] = jnp.full(top.shape, -BIG, f32)
        total[...] = jnp.zeros(total.shape, f32)

        def fill(slot, key_at):
            scores[slot][...] = dot(keys[key_at], query, 1, 0)

        def work(slot, key_at):
            score = scores[slot][...]
            old_top = top[...]
            new_top = jnp.maximum(old_top, jnp.max(score, axis=0, keepdims=True))
            weights = jnp.exp2(score - new_top).astype(bf16)
            total[...] = total[...] * jnp.exp2(old_top - new_top) + dot(values[key_at], weights, 1, 0)
            top[...] = new_top

        two_ahead(count, todo, at, fill, work)
        final = total[...]
        weight_sum = final[HEAD : HEAD + 1, :]
        mixed = final[:HEAD, :] * (1.0 / weight_sum)
        out_ref[i] = mixed.astype(bf16)
        full_ref[i] = mixed
        lse_ref[i] = three_parts(top[...] + jnp.log2(weight_sum))
        return carry

    lax.fori_loop(0, out_ref.shape[0], attend, 0)


def fwd_call(todo, seg, need, keys, values, queries):
    count, (pieces, _, piece) = todo.shape[0], queries.shape
    return call(
        fwd_kernel, "attend",
        (shape_of(count, HEAD, piece), shape_of(count, HEAD, piece, dtype=f32), shape_of(count, 16, piece)),
        (todo, seg, need, keys, values, queries),
        scratch=[pltpu.VMEM((piece, piece), f32)] * 2
        + [pltpu.VMEM((1, piece), f32), pltpu.VMEM((HEAD + 16, piece), f32), pltpu.SMEM((pieces,), jnp.int32)],
        scalars=3, mib=22,
    )


def bwd_kernel(todo_ref, place_ref, seg_ref, need_ref, cos_ref, sin_ref, keys, key_lanes, values, queries, grads, *rest, stage, todo_count, ready):
    if stage:
        kept, sum_in, rest = rest[0], rest[1], rest[2:]
    outs, rest = rest[: (2, 3, 1)[stage]], rest[(2, 3, 1)[stage] :]
    score_a, grad_a, score_b, grad_b, key_sum, value_sum, todo = rest[:7]
    sums = rest[7] if stage == 2 else outs[-1]
    pieces = queries.shape[0]
    scores, prob_grads = (score_a, score_b), (grad_a, grad_b)
    sums[...] = sum_in[...] if stage else jnp.zeros(sums.shape, f32)
    if stage == 1:
        outs[0][:2] = kept[...]
    if stage == 2:
        outs[0][2:, : 2 * HEAD, :] = kept[...]
    ready()

    def attend(i, carry):
        at = todo_ref[i]
        seg = seg_ref[at]
        count = collect(at + 1, pieces, lambda q: (need_ref[q] & seg) != 0, todo)
        key, value, key_lane = keys[at], values[at], key_lanes[at]
        score_a[...] = causal(dot(key, queries[at], 1, 0))
        grad_a[...] = dot(value, grads[at], 1, 0)
        key_sum[...] = jnp.zeros(key_sum.shape, f32)
        value_sum[...] = jnp.zeros(value_sum.shape, f32)

        def fill(slot, query_at):
            scores[slot][...] = dot(key, queries[query_at], 1, 0)
            prob_grads[slot][...] = dot(value, grads[query_at], 1, 0)

        def work(slot, query_at):
            probs = jnp.exp2(scores[slot][...])
            score_grad = (probs * prob_grads[slot][...]).astype(bf16)
            value_sum[...] += dot(grads[query_at, :HEAD, :], probs.astype(bf16), 1, 1)
            key_sum[...] += dot(queries[query_at, :HEAD, :], score_grad, 1, 1)
            sums[query_at] += dot(key_lane, score_grad, 1, 0)

        two_ahead(count, todo, at, fill, work)
        key_grad = unrotate(key_sum[...] * (1.0 / LOG2E), cos_ref[at], sin_ref[at]).astype(bf16)
        value_grad = (0.5 * value_sum[...]).astype(bf16)

        def write(ref, place):
            ref[place, :HEAD, :] = key_grad
            ref[place, HEAD : 2 * HEAD, :] = value_grad

        if stage == 1:
            pl.when(i < 2)(lambda: write(outs[0], 2 + i))
            pl.when(i >= 2)(lambda: write(outs[1], i - 2))
        else:
            write(outs[0], i)
        return carry

    lax.fori_loop(0, todo_count, attend, 0)
    if stage == 2:
        for p in range(pieces):
            grad = unrotate(sums[p] * SCORE_SCALE, cos_ref[p], sin_ref[p]).astype(bf16)
            start = pl.multiple_of((2 + ((p % 2) ^ place_ref[0])) * HEAD, HEAD)
            outs[0][p // 2, pl.ds(start, HEAD), :] = grad


def bwd_call(stage, todo, place, seg, need, cosine, sine, keys, key_lanes, values, queries, grads, kept, query_sum):
    count, (pieces, _, piece) = todo.shape[0], queries.shape
    places = pieces // 2
    sums = shape_of(pieces, HEAD, piece, dtype=f32)
    outs = (
        (shape_of(2, 2 * HEAD, piece), sums),
        (shape_of(places, 2 * HEAD, piece), shape_of(2, 2 * HEAD, piece), sums),
        (shape_of(places, 4 * HEAD, piece),),
    )[stage]
    operands = (cosine, sine, keys, key_lanes, values, queries, grads) + ((kept, query_sum) if stage else ())
    got = call(
        functools.partial(bwd_kernel, stage=stage, todo_count=count), "attend_back", outs,
        (todo, place, seg, need, *operands),
        scratch=[pltpu.VMEM((piece, piece), f32)] * 4
        + [pltpu.VMEM((HEAD, piece), f32)] * 2
        + [pltpu.SMEM((pieces,), jnp.int32)]
        + ([pltpu.VMEM(sums.shape, f32)] if stage == 2 else []),
        scalars=4, mib=36, late=(0, 1),
    )
    return got[0] if stage == 2 else got


def after(value, *earlier):
    return lax.optimization_barrier((value,) + earlier)[0]


def on_device(
    tokens, first_values, cotangent, parents, seg_lengths,
    w_query, w_key, w_value, w_out, w_gate, w_up, w_down, gain_attn, gain_ffn,
):
    assert tokens.shape[1] == 1
    fsdp_count, ctx_count, tp_count = (lax.axis_size(a) for a in ("fsdp", "ctx", "tp"))
    assert tp_count == 4 and ctx_count == 4
    fsdp_at, ctx_at, tp_at = (lax.axis_index(a) for a in ("fsdp", "ctx", "tp"))
    core_at, x_at = tp_at % 2, tp_at // 2
    own_rows, width = tokens.shape[0], tokens.shape[2]
    chip_rows = 2 * own_rows
    heads = w_query.shape[1] // HEAD
    head_width = heads * HEAD
    assert heads == ctx_count
    tree_len = own_rows * tp_count * ctx_count
    weight_rows, hidden = w_query.shape[0], w_gate.shape[1]
    two = fsdp_count == 2

    def over_core(value):
        return lax.ppermute(value, "tp", [(i, i ^ 1) for i in range(tp_count)])

    def over_x(value):
        return lax.ppermute(value, "tp", [(i, i ^ 2) for i in range(tp_count)])

    def over_fsdp(value):
        return lax.ppermute(value, "fsdp", [(0, 1), (1, 0)])

    def over_ctx(value, flip):
        return lax.ppermute(value, "ctx", [(i, i ^ flip) for i in range(ctx_count)])

    def exchange(by_place):
        return lax.all_to_all(by_place, "ctx", 0, 0, tiled=True)

    def relative(rows):
        if not two:
            return rows
        swapped = jnp.concatenate([rows[..., weight_rows:], rows[..., :weight_rows]], axis=-1)
        return jnp.where(fsdp_at == 0, rows, swapped)

    def by_x(near, far):
        return jnp.where(x_at == 0, jnp.concatenate([near, far], axis=0), jnp.concatenate([far, near], axis=0))

    def fsdp_sum(parts, axis=0):
        if not two:
            return lax.psum_scatter(parts[0], "fsdp", scatter_dimension=axis, tiled=True)
        return parts[0], over_fsdp(parts[1])

    def inward(low):
        return low, lax.ppermute(low, "ctx", [(0, 1), (3, 2)])

    def across(low):
        return low, lax.ppermute(low, "ctx", [(1, 2), (2, 1)])

    def outward(low):
        return low, lax.ppermute(low, "ctx", [(1, 0), (2, 3)])

    def join(pair):
        return (pair[0].astype(f32) + pair[1].astype(f32)).astype(bf16)

    def finish(pair):
        return jnp.where((ctx_at == 0) | (ctx_at == 3), pair[1], pair[0]).astype(f32)

    def hold(pair, *earlier):
        return (pair[0], after(pair[1], *earlier)) if isinstance(pair, tuple) else after(pair, *earlier)

    def step(*pairs):
        if not two:
            return [join(pair) if isinstance(pair, tuple) else pair for pair in pairs]
        return join_call(*pairs)

    own_tokens = tokens[:, 0, :]
    token_x = over_x(own_tokens)
    token_core = over_core(own_tokens)
    gains = jnp.stack([gain_attn, gain_ffn])
    if two:
        gains = jnp.concatenate([gains, over_fsdp(gains)], axis=1)
    else:
        gains = lax.all_gather(gains, "fsdp", axis=1, tiled=True)
    attention_gain = gains[0].reshape(1, width).astype(f32)
    ffn_gain = gains[1].reshape(1, width).astype(f32)
    three = (w_query, w_key, w_value)
    if two:
        own_three = stack_call(*three)
        qkv_weight = [own_three, over_fsdp(own_three)]
    else:
        qkv_weight = [stack_call(*(lax.all_gather(w, "fsdp", axis=0, tiled=True) for w in three))]
    count = len(qkv_weight)

    place = jnp.stack([x_at, core_at, ctx_at, fsdp_at]).astype(jnp.int32)
    position, query_extra, key_extra, seg_bits, need_bits = layout_call(parents, seg_lengths, tree_len, chip_rows)
    frequency = jnp.exp(-math.log(10000.0) * jnp.arange(HALF, dtype=f32) / HALF)
    angles = frequency[None, :, None] * position
    cosine, sine = jnp.cos(angles), jnp.sin(angles)

    def normalize(rows_f32):
        return lax.rsqrt(jnp.mean(rows_f32 * rows_f32, axis=-1, keepdims=True) + epsilon)

    first_flat = first_values[:, 0, :]

    def spread(pieces):
        return [over_ctx(piece, flip) if flip else piece for flip, piece in enumerate(pieces)]

    others = (w_gate, w_up, w_down, w_out)
    if two:
        feed_own = stack_call(*(after(w.T, own_three) for w in others))
    near_normed = norm_call(after(place, feed_own) if two else place, own_tokens, token_core, attention_gain, two)
    far_normed = norm_call(after(place, near_normed), token_x, over_core(token_x), attention_gain, two)
    if two:
        feed_weight = [feed_own, over_fsdp(feed_own)]
    else:
        feed_weight = [stack_call(*(lax.all_gather(w, "fsdp", axis=0, tiled=True).T for w in others))]
    by_head = project_call(place, near_normed, far_normed, cosine, sine, first_flat, qkv_weight)
    own_cot = relative(after(cotangent[:, 0, :], by_head))
    arrived = after(place, own_cot)
    keys, key_lanes, value_lanes, values, queries = prep_call(arrived, query_extra, key_extra, exchange(by_head))
    cot_x = over_x(after(own_cot, keys))
    out_weight = pick_call([after(w, keys) for w in feed_weight], head_width)
    out_weight_x = over_x(out_weight)
    cot_core = over_core(after(own_cot, keys))
    cot_x_core = over_core(cot_x)

    half_places = jnp.arange(ctx_count, dtype=jnp.int32) * 2
    far_out, far_full, far_lse = fwd_call(
        after(half_places + (1 - x_at), cot_core), seg_bits, need_bits, keys, value_lanes, queries
    )
    near_out, near_full, near_lse = fwd_call(
        after(half_places + x_at, far_out, out_weight, cot_x), seg_bits, need_bits, keys, value_lanes, queries
    )
    far_mixed = after(exchange(far_out), near_out).reshape(head_width, chip_rows)
    far_mixed_got = over_x(far_mixed)
    near_mixed = exchange(after(near_out, far_mixed)).reshape(head_width, chip_rows)

    mine, other = output_call(place, near_mixed, far_mixed_got, out_weight, out_weight_x)
    own_single = relative(own_tokens).astype(f32)
    middle = own_single + mine + over_core(other).astype(f32)

    middle_scale = normalize(middle)
    ffn_own = (middle * middle_scale * ffn_gain).astype(bf16)
    ffn_x = over_x(ffn_own)
    ffn_core = over_core(ffn_own)
    ffn_x_core = over_core(ffn_x)
    near_hidden, near_gate, near_up, near_mine, near_sent = feed_call(
        ffn_own, ffn_core, own_cot, cot_core, feed_weight, hidden
    )
    far_hidden, far_gate, far_up, far_mine, far_sent = feed_call(
        after(ffn_x, near_mine), ffn_x_core, cot_x, cot_x_core, feed_weight, hidden
    )
    far_sum = (far_mine + over_core(far_sent).astype(f32)).astype(bf16)
    far_sum_got = over_x(far_sum)
    near_sum = near_mine + over_core(near_sent).astype(f32)

    all_cot = (after(own_cot, far_sum), cot_core, cot_x, cot_x_core)
    all_ffn = (after(ffn_own, far_sum), ffn_core, ffn_x, ffn_x_core)
    first_parts, second_parts = feed_grads_call(
        (near_gate, far_gate, near_up, far_up), (near_hidden, far_hidden), all_ffn, all_cot, count
    )
    first_sum = fsdp_sum(first_parts, 1)
    second_sum = fsdp_sum(second_parts, 1)
    ffn_grad = near_sum + after(far_sum_got, first_parts[0]).astype(f32)

    weighted = ffn_grad * ffn_gain
    middle_grad = (
        own_cot.astype(f32)
        + middle_scale * weighted
        - middle * (middle_scale**3 * jnp.mean(weighted * middle, axis=-1, keepdims=True))
    )
    middle_low = middle_grad.astype(bf16)
    near_heads, far_heads, chip_low = heads_call(place, middle_low, over_core(middle_low), out_weight, out_weight_x)
    far_out_grad = over_x(far_heads)
    near_grads = exchange(near_heads.reshape(heads, HEAD, chip_rows))
    far_grads = exchange(after(far_out_grad, near_grads).reshape(heads, HEAD, chip_rows))

    ffn_gain_part = jnp.sum(after(ffn_grad, near_heads) * middle * middle_scale, axis=0)
    low_x = over_x(after(middle_low, far_out_grad))
    low_x_core = over_core(low_x)
    near_result, far_result, sent = result_call(after(near_hidden, near_heads), far_hidden, feed_weight)
    sent_got = over_core(sent)
    far_result_low = (far_result + sent_got[1].astype(f32)).astype(bf16)
    far_result_got = over_x(far_result_low)

    (first_low,) = step(hold(first_sum, far_grads))
    first_in = inward(first_low)
    back_queries, grads = prep_back_call(
        after(place, far_result_low, first_low), queries, query_extra.shape[1], near_grads, far_grads, near_full, far_full, near_lse, far_lse
    )

    def back(stage, places, kept, query_sum, *earlier):
        return bwd_call(
            stage, after(jnp.stack(places).astype(jnp.int32), *earlier), place, seg_bits, need_bits, cosine, sine,
            keys, key_lanes, values, back_queries, grads, kept, query_sum,
        )

    far_at, near_at = [2 * i + 1 - x_at for i in range(4)], [2 * i + x_at for i in range(4)]
    first_kv, query_sum = back(0, far_at[:2], None, None, first_low)

    first_low, second_low = step(hold(first_in, first_kv), hold(second_sum, first_kv))
    first_across, second_in = across(first_low), inward(second_low)
    far_kv, near_kv, query_sum = back(1, far_at[2:] + near_at[2:], first_kv, query_sum, first_low)

    first_low, second_low = step(hold(first_across, far_kv), hold(second_in, far_kv))
    first_done, second_across = outward(first_low), across(second_low)
    far_kv_got = exchange(after(far_kv, first_low))
    last = back(2, near_at[:2], near_kv, query_sum, first_low)

    (second_low,) = step(hold(second_across, last))
    second_done = outward(second_low)
    last_got = exchange(after(last, second_low, first_done[1]))
    far_kv_got = after(far_kv_got, last)
    out_parts = out_grads_call(after(place, last), chip_low, low_x, low_x_core, near_mixed, far_mixed, count)
    out_sum = fsdp_sum(out_parts)
    second_all = finish(hold(second_done, out_parts[0]))
    layer_out = relative((after(middle, second_all) + near_result + sent_got[0].astype(f32) + far_result_got.astype(f32)).astype(bf16))
    first_all = finish(hold(first_done, second_low))
    (out_low,) = step(hold(out_sum, layer_out))
    last_got = after(last_got, first_all, out_low)
    out_in = inward(out_low)

    far_mine, far_other, far_gain = rows_call(place, far_normed, far_kv_got, last_got, qkv_weight, 1)
    far_rows_got = over_x((far_mine + over_core(far_other).astype(f32)).astype(bf16))
    near_mine, near_other, near_gain = rows_call(
        after(place, far_mine), near_normed, far_kv_got, last_got, qkv_weight, 0
    )
    near_rows_got = over_core(near_other)
    qkv_parts = weights_call(after(near_normed, near_mine), far_normed, far_kv_got, last_got, count)
    qkv_sum = fsdp_sum(qkv_parts)
    gain_sum = jnp.concatenate([(far_gain + near_gain) / attention_gain, ffn_gain_part[None]], axis=0)
    if two:
        gain_sum = gain_sum + over_core(gain_sum)
        gain_sum = gain_sum + over_x(gain_sum)
    qkv_low, out_low = step(hold(qkv_sum, gain_sum), hold(out_in, gain_sum))
    qkv_in, out_across = inward(qkv_low), across(out_low)
    near_value = after(last_got, qkv_low)[:, HEAD : 2 * HEAD].reshape(head_width, chip_rows)
    far_value = far_kv_got[:, HEAD:].reshape(head_width, chip_rows)
    grad_values = by_x(near_value.T, far_value.T).astype(f32)
    if two:
        gain_sum = gain_sum[:, :weight_rows] + over_fsdp(after(gain_sum, qkv_low)[:, weight_rows:])
        gain_sum = gain_sum + over_ctx(gain_sum, 1)
    qkv_low, out_low = step(hold(qkv_in, gain_sum, grad_values), hold(out_across, gain_sum))
    lows = [qkv_low]
    qkv_across, out_done = across(qkv_low), outward(out_low)
    if two:
        gain_sum = gain_sum + over_ctx(after(gain_sum, qkv_low), 2)
    else:
        gain_sum = lax.psum(gain_sum, ("fsdp", "ctx", "tp"))
        gain_sum = lax.dynamic_slice_in_dim(gain_sum, fsdp_at * weight_rows, weight_rows, 1)
    (qkv_low,) = step(hold(qkv_across, gain_sum, out_done[1]))
    grad_query, grad_key, grad_value = jnp.split(finish(outward(qkv_low)), 3)
    grad_out = finish(out_done)
    grad_gate, grad_up, grad_down = first_all[:hidden].T, first_all[hidden:].T, second_all.T

    normed_grad = after(near_mine, lows[0]) + near_rows_got.astype(f32) + far_rows_got.astype(f32)
    scale = normalize(own_single)
    weighted = normed_grad * attention_gain
    grad_tokens = (
        middle_grad + scale * weighted - own_single * (scale**3 * jnp.mean(weighted * own_single, axis=-1, keepdims=True))
    )
    return (
        layer_out[:, None, :],
        relative(grad_tokens)[:, None, :],
        grad_values[:, None, :],
        grad_query,
        grad_key,
        grad_value,
        grad_out,
        grad_gate,
        grad_up,
        grad_down,
        gain_sum[0],
        gain_sum[1],
    )

def solution(mesh):
    rows, columns = P(("ctx", "tp"), "fsdp", None), P("ctx", "fsdp", "tp")
    weight, gain = P("fsdp", "tp"), P("fsdp")
    return jax.shard_map(
        on_device,
        mesh=mesh,
        in_specs=(rows, columns, rows, P("fsdp", None), P("fsdp", None)) + (weight,) * 7 + (gain,) * 2,
        out_specs=(rows, rows, columns) + (weight,) * 7 + (gain,) * 2,
        check_vma=False,
    )
```

```python
import functools
import math

import jax
import jax.numpy as jnp
from jax import lax
from jax.experimental import pallas as pl
from jax.experimental.pallas import tpu as pltpu
from jax.sharding import PartitionSpec as P

HEAD = 64
HALF = HEAD // 2
BIG = 1e30
LOG2E = 1.4426950408889634
SCORE_SCALE = HEAD**-0.5
QUERY_SCALE = SCORE_SCALE * LOG2E
epsilon = 1e-05
f32 = jnp.float32
bf16 = jnp.bfloat16


def dot(a, b, ca, cb):
    return lax.dot_general(a, b, (((ca,), (cb,)), ((), ())), preferred_element_type=f32)


def layout_kernel(par_ref, len_ref, pos_ref, qx_ref, kx_ref, seg_ref, need_ref, anc_sc, above_sc, *, segs, tokens, piece):
    token = lax.broadcasted_iota(jnp.int32, (1, tokens), 1)
    pos = jnp.zeros((1, tokens), jnp.int32)
    seg_of = jnp.full((1, tokens), -1, jnp.int32)
    bits = jnp.zeros((1, tokens), jnp.int32)
    for b in range(tokens // piece):
        seg_ref[b] = 0
        need_ref[b] = 0
    off = jnp.int32(0)
    for s in range(segs):
        length = len_ref[0, s]
        if s == 0:
            anc, above = jnp.int32(1), jnp.int32(0)
        else:
            parent = par_ref[0, s]
            anc = anc_sc[parent] | jnp.int32(1 << s)
            above = above_sc[parent] + len_ref[0, parent]
        anc_sc[s] = anc
        above_sc[s] = above
        started = token >= off
        seg_of = jnp.where(started, s, seg_of)
        pos = jnp.where(started, token - off + above, pos)
        bits = jnp.where(started, anc, bits)

        def mark(b, carry, anc=anc, s=s):
            seg_ref[b] = seg_ref[b] | jnp.int32(1 << s)
            need_ref[b] = need_ref[b] | anc
            return carry

        lax.fori_loop(off // piece, (off + length - 1) // piece + 1, mark, 0)
        off = off + length
    row = lax.broadcasted_iota(jnp.int32, (kx_ref.shape[1], tokens), 0)
    key_extra = jnp.where(row == seg_of, -BIG, 0.0).astype(bf16)
    linked = lax.shift_right_logical(jnp.broadcast_to(bits, row.shape), row) & 1
    query_extra = jnp.where(linked == 1, 0.0, 1.0).astype(bf16)
    for p in range(tokens // piece):
        lanes = slice(p * piece, (p + 1) * piece)
        pos_ref[p] = pos[:, lanes].astype(f32)
        kx_ref[p] = key_extra[:, lanes]
        qx_ref[p] = query_extra[:, lanes]


SMEM = pl.BlockSpec(memory_space=pltpu.SMEM)
VMEM = pl.BlockSpec(memory_space=pltpu.VMEM)


def layout_call(parents, lengths, tokens, piece):
    segs = parents.shape[-1]
    rows = -(-segs // 16) * 16
    return pl.pallas_call(
        functools.partial(layout_kernel, segs=segs, tokens=tokens, piece=piece),
        out_shape=(
            jax.ShapeDtypeStruct((tokens // piece, 1, piece), f32),
            jax.ShapeDtypeStruct((tokens // piece, rows, piece), bf16),
            jax.ShapeDtypeStruct((tokens // piece, rows, piece), bf16),
            jax.ShapeDtypeStruct((tokens // piece,), jnp.int32),
            jax.ShapeDtypeStruct((tokens // piece,), jnp.int32),
        ),
        in_specs=[SMEM, SMEM],
        out_specs=(VMEM, VMEM, VMEM, SMEM, SMEM),
        scratch_shapes=[pltpu.SMEM((segs,), jnp.int32), pltpu.SMEM((segs,), jnp.int32)],
        cost_estimate=pl.CostEstimate(flops=0, bytes_accessed=1 << 16, transcendentals=0),
        name="layout",
    )(parents, lengths)


def causal(scores):
    key_at = lax.broadcasted_iota(jnp.int32, scores.shape, 0)
    query_at = lax.broadcasted_iota(jnp.int32, scores.shape, 1)
    return jnp.where(key_at <= query_at, scores, -BIG)


def three_parts(row):
    at = lax.broadcasted_iota(jnp.int32, (16, row.shape[1]), 0)
    high = row.astype(bf16).astype(f32)
    rest = row - high
    mid = rest.astype(bf16).astype(f32)
    low = rest - mid
    return jnp.where(at == 0, high, jnp.where(at == 1, mid, jnp.where(at == 2, low, 0.0))).astype(bf16)


def unrotate(values, cosine, sine):
    a, b = values[:HALF], values[HALF:]
    return jnp.concatenate([a * cosine + b * sine, b * cosine - a * sine], axis=0)


def prep_kernel(place_ref, qx_ref, kx_ref, got_ref, keys, key_lanes, value_lanes, values, queries):
    piece = got_ref.shape[2] // 2
    extra = qx_ref.shape[1]
    minus = jnp.full((16, piece), -1.0, bf16)
    pad_key = jnp.zeros((128 - HEAD - extra - 16, piece), bf16)
    pad_value = jnp.zeros((128 - HEAD - 16, piece), bf16)
    for half in (0, 1):
        for p in range(got_ref.shape[0]):
            at = 2 * p + (place_ref[0] ^ half)
            got = got_ref[p, :, half * piece : (half + 1) * piece]
            query, key, value = got[:HEAD, :], got[HEAD : 2 * HEAD, :], got[2 * HEAD :, :]
            key_lanes[at] = key
            keys[at] = jnp.concatenate([key, kx_ref[at], minus, pad_key], axis=0).T
            value_lanes[at] = jnp.concatenate([value, -minus], axis=0)
            values[at] = jnp.concatenate([value, minus, pad_value], axis=0).T
            queries[at] = jnp.concatenate([query, qx_ref[at], jnp.zeros((128 - HEAD - extra, piece), bf16)], axis=0)


def shape_of(*sizes, dtype=bf16):
    return jax.ShapeDtypeStruct(sizes, dtype)


def call(kernel, name, out_shape, operands, scratch=(), scalars=1, mib=20, late=()):
    outs = out_shape if isinstance(out_shape, tuple) else (out_shape,)
    arrays = operands[scalars:]
    count, total = len(arrays), len(arrays) + len(outs)

    def body(*refs):
        first, rest = refs[:scalars], refs[scalars:]
        outside, inside, sems, rest = rest[:total], rest[total : 2 * total], rest[2 * total], rest[2 * total + 1 :]
        copies = [pltpu.make_async_copy(outside[i], inside[i], sems.at[i]) for i in range(count)]
        for copy in copies:
            copy.start()
        for i in range(count):
            if i not in late:
                copies[i].wait()
        more = {"ready": lambda: [copies[i].wait() for i in late]} if late else {}
        kernel(*first, *inside, *rest, **more)
        copies = [pltpu.make_async_copy(inside[i], outside[i], sems.at[i]) for i in range(count, total)]
        for copy in copies:
            copy.start()
        for copy in copies:
            copy.wait()

    got = pl.pallas_call(
        body,
        out_shape=outs,
        in_specs=[SMEM] * scalars + [pl.BlockSpec(memory_space=pltpu.HBM)] * count,
        out_specs=(pl.BlockSpec(memory_space=pltpu.HBM),) * len(outs),
        scratch_shapes=[pltpu.VMEM(x.shape, x.dtype) for x in (*arrays, *outs)]
        + [pltpu.SemaphoreType.DMA((total,))]
        + list(scratch),
        compiler_params=pltpu.CompilerParams(vmem_limit_bytes=60 << 20),
        cost_estimate=pl.CostEstimate(flops=0, bytes_accessed=1 << 16, transcendentals=0),
        name=name,
    )(*operands)
    return got if isinstance(out_shape, tuple) else got[0]


def cut(ref, count):
    size = ref.shape[1] // count
    return [ref[:, i * size : (i + 1) * size] for i in range(count)]


def project_kernel(place_ref, near_own, near_other, far_own, far_other, gain_ref, cos_ref, sin_ref, first_ref, *rest, count, swap):
    weights, (out, near_out, far_out, raw) = rest[:count], rest[count:]
    heads_width = raw.shape[0] // 3
    size, width = near_own.shape
    block = width // count
    for refs, normed in (((near_own, near_other), near_out), ((far_own, far_other), far_out)):
        for half, ref in enumerate(refs):
            single = ref[...].astype(f32)
            scale = lax.rsqrt(jnp.mean(single * single, axis=-1, keepdims=True) + epsilon)
            if swap:
                turned = jnp.concatenate([single[:, block:], single[:, :block]], axis=1)
                single = jnp.where(place_ref[3] == 0, single, turned)
            at = pl.multiple_of((place_ref[1] ^ half) * size, size)
            normed[pl.ds(at, size), :] = (single * scale * gain_ref[...]).astype(bf16)
    piece = 2 * size
    turned = [[w[i * block : (i + 1) * block, :].T for w in weights] for i in range(3)]
    for half, rows_ref in enumerate((near_out, far_out)):
        rows = cut(rows_ref, count)
        for i in range(3):
            raw[i * heads_width : (i + 1) * heads_width, :] = sum(dot(w, r, 1, 1) for w, r in zip(turned[i], rows))
        x_half = place_ref[0] ^ half
        at = 2 * place_ref[2] + x_half
        cosine, sine = cos_ref[at], sin_ref[at]
        start = pl.multiple_of(x_half * piece, piece)
        first = first_ref[pl.ds(start, piece), :].astype(f32).T

        def turn(values):
            a, b = values[:HALF], values[HALF:]
            return jnp.concatenate([a * cosine - b * sine, b * cosine + a * sine], axis=0)

        lanes = slice(half * piece, (half + 1) * piece)
        for at in range(heads_width // HEAD):
            rows_at = [slice(i * heads_width + at * HEAD, i * heads_width + (at + 1) * HEAD) for i in range(3)]
            value = 0.5 * raw[rows_at[2], :] + 0.5 * first[at * HEAD : (at + 1) * HEAD]
            out[at, :HEAD, lanes] = (turn(raw[rows_at[0], :]) * QUERY_SCALE).astype(bf16)
            out[at, HEAD : 2 * HEAD, lanes] = turn(raw[rows_at[1], :]).astype(bf16)
            out[at, 2 * HEAD :, lanes] = value.astype(bf16)


def project_call(place, rows, gain, cosine, sine, first, weights, swap):
    (size, width), columns = rows[0].shape, weights[0].shape[1]
    return call(
        functools.partial(project_kernel, count=len(weights), swap=swap), "project",
        (shape_of(columns // HEAD, 3 * HEAD, 4 * size), shape_of(2 * size, width), shape_of(2 * size, width)),
        (place, *rows, gain, cosine, sine, first, *weights),
        scratch=[pltpu.VMEM((3 * columns, 2 * size), f32)],
    )


def stack_kernel(*refs):
    out, at = refs[-1], 0
    for ref in refs[:-1]:
        rows = ref.shape[0]
        out[at : at + rows, :] = ref[...]
        at += rows


def pick_kernel(*refs):
    out = refs[-1]
    rows = out.shape[0]
    size = out.shape[1] // (len(refs) - 1)
    for i, ref in enumerate(refs[:-1]):
        out[:, i * size : (i + 1) * size] = ref[ref.shape[0] - rows :, :]


def pick_call(blocks, rows):
    return call(pick_kernel, "pick", shape_of(rows, blocks[0].shape[1] * len(blocks)), tuple(blocks), scalars=0)


def stack_call(*arrays):
    rows = sum(a.shape[0] for a in arrays)
    return call(stack_kernel, "stack", shape_of(rows, arrays[0].shape[1]), arrays, scalars=0, mib=16)


def split_core(place_ref, total, mine_ref, other_ref):
    rows = mine_ref.shape[0]
    mine_ref[...] = total[pl.ds(pl.multiple_of(place_ref[1] * rows, rows), rows), :]
    other_ref[...] = total[pl.ds(pl.multiple_of((1 - place_ref[1]) * rows, rows), rows), :].astype(bf16)


def output_kernel(place_ref, near_ref, far_ref, *rest):
    near_weight, far_weight, mine_ref, other_ref, total = rest
    total[...] = dot(near_ref[...].T, near_weight[...], 1, 0) + dot(far_ref[...].T, far_weight[...], 1, 0)
    split_core(place_ref, total, mine_ref, other_ref)


def output_call(place, near, far, near_weight, far_weight):
    rows, width = near.shape[1], near_weight.shape[1]
    return call(
        output_kernel, "out_project",
        (shape_of(rows // 2, width, dtype=f32), shape_of(rows // 2, width)),
        (place, near, far, near_weight, far_weight),
        scratch=[pltpu.VMEM((rows, width), f32)],
    )


def heads_kernel(place_ref, own_ref, other_ref, near_weight, far_weight, near_out, far_out, chip):
    rows = own_ref.shape[0]
    for half, ref in enumerate((own_ref, other_ref)):
        chip[pl.ds(pl.multiple_of((place_ref[1] ^ half) * rows, rows), rows), :] = ref[...]
    far_out[...] = dot(far_weight[...], chip[...], 1, 1).astype(bf16)
    near_out[...] = dot(near_weight[...], chip[...], 1, 1).astype(bf16)


def heads_call(place, own, other, near_weight, far_weight):
    rows, columns = 2 * own.shape[0], near_weight.shape[0]
    return call(
        heads_kernel, "out_back",
        (shape_of(columns, rows), shape_of(columns, rows), shape_of(rows, own.shape[1])),
        (place, own, other, near_weight, far_weight),
    )


def feed_kernel(rows_ref, other_ref, cot_ref, cot_other_ref, *rest, count):
    hidden = rest[count].shape[2]
    gate_w, up_w, down_w = ([w.at[i * hidden : (i + 1) * hidden] for w in rest[:count]] for i in range(3))
    hidden_ref, gate_ref, up_ref, mine_ref, sent_ref, rows_sc, cot_sc, back_sc = rest[count:]
    size = rows_ref.shape[0]
    rows_sc[0], rows_sc[1] = rows_ref[...], other_ref[...]
    cot_sc[0], cot_sc[1] = cot_ref[...], cot_other_ref[...]
    block = rows_ref.shape[1] // count

    def step(at, carry):
        lanes = [slice(i * block, (i + 1) * block) for i in range(count)]
        rows, cots = [rows_sc[at, :, s] for s in lanes], [cot_sc[at, :, s] for s in lanes]
        gate = sum(dot(r, w[...], 1, 1) for r, w in zip(rows, gate_w))
        up = sum(dot(r, w[...], 1, 1) for r, w in zip(rows, up_w))
        hidden_grad = sum(dot(r, w[...], 1, 1) for r, w in zip(cots, down_w))
        sig = 1.0 / (1.0 + jnp.exp(-gate))
        act = gate * sig
        hidden_ref[at] = (act * up).astype(bf16)
        gate_grad = (hidden_grad * up * (sig * (1.0 + gate * (1.0 - sig)))).astype(bf16)
        up_grad = (hidden_grad * act).astype(bf16)
        gate_ref[at] = gate_grad
        up_ref[at] = up_grad
        for i in range(count):
            back_sc[at, :, lanes[i]] = dot(gate_grad, gate_w[i][...], 1, 0) + dot(up_grad, up_w[i][...], 1, 0)
        return carry

    lax.fori_loop(0, 2, step, 0)
    mine_ref[...] = back_sc[0]
    sent_ref[...] = back_sc[1].astype(bf16)


def feed_call(rows, other, cot, cot_other, weights, hidden):
    size, width = rows.shape
    count = len(weights)
    return call(
        functools.partial(feed_kernel, count=count), "feed",
        (shape_of(2, size, hidden),) * 3 + (shape_of(size, width, dtype=f32), shape_of(size, width)),
        (rows, other, cot, cot_other, *weights),
        scratch=[pltpu.VMEM((2, size, width), bf16)] * 2 + [pltpu.VMEM((2, size, width), f32)],
        scalars=0, mib=40,
    )


def prep_back(place_ref, queries, near_grad, far_grad, near_full, far_full, near_lse, far_lse, queries_out, grads_out, extra):
    places, _, piece = near_grad.shape
    queries_out[...] = queries[...]
    pad = jnp.zeros((128 - HEAD - 16, piece), bf16)
    for half, (grad, full, lse) in enumerate(((near_grad, near_full, near_lse), (far_grad, far_full, far_lse))):
        for p in range(places):
            at = 2 * p + (place_ref[0] ^ half)
            queries_out[at, HEAD + extra : HEAD + extra + 16, :] = lse[p]
            delta = jnp.sum(grad[p].astype(f32) * full[p], axis=0, keepdims=True)
            grads_out[at] = jnp.concatenate([grad[p], three_parts(delta), pad], axis=0)


def last_kernel(place_ref, near_rows, far_rows, kv, last, *rest, count):
    weights, rest = rest[:count], rest[count:]
    parts, (near_mine, near_other, far_mine, far_other, gain_ref, total) = rest[:count], rest[count:]
    size = near_rows.shape[1] // count
    columns = kv.shape[0] * HEAD
    flat = lambda ref, at: ref[:, at * HEAD : (at + 1) * HEAD, :].reshape(columns, ref.shape[2])
    near = flat(last, 2), flat(last, 0), flat(last, 1)
    far = flat(last, 3), flat(kv, 0), flat(kv, 1)
    for i in range(3):
        for b in range(count):
            lanes = slice(b * size, (b + 1) * size)
            sums = dot(near[i], near_rows[:, lanes], 1, 0) + dot(far[i], far_rows[:, lanes], 1, 0)
            parts[b][i * size : (i + 1) * size, :] = sums.T.astype(bf16)
    gain_ref[...] = jnp.zeros(gain_ref.shape, f32)
    for grads, rows, mine, other in ((far, far_rows, far_mine, far_other), (near, near_rows, near_mine, near_other)):
        turned = [g.T for g in grads]
        for b in range(count):
            lanes = slice(b * size, (b + 1) * size)
            part = sum(dot(g, weights[b][i * size : (i + 1) * size, :], 1, 1) for i, g in enumerate(turned))
            total[:, lanes] = part
            gain_ref[:, lanes] += jnp.sum(part * rows[:, lanes].astype(f32), axis=0, keepdims=True)
        split_core(place_ref, total, mine, other)


def last_call(place, near_rows, far_rows, kv, last, weights):
    (size, width), count, columns = near_rows.shape, len(weights), kv.shape[0] * HEAD
    rows = (shape_of(size // 2, width, dtype=f32), shape_of(size // 2, width))
    outs = call(
        functools.partial(last_kernel, count=count), "project_back",
        tuple(shape_of(3 * width // count, columns) for _ in range(count)) + rows + rows + (shape_of(1, width, dtype=f32),),
        (place, near_rows, far_rows, kv, last, *weights),
        scratch=[pltpu.VMEM((size, width), f32)],
    )
    return outs[:count], *outs[count:]


def feed_grads_kernel(near_gate, far_gate, near_up, far_up, near_hidden, far_hidden, *refs):
    rows, cots, outs = refs[:4], refs[4:8], refs[8:]
    count = len(outs) // 2
    size = rows[0].shape[1] // count
    hidden = near_gate.shape[2]
    pairs = ((near_gate, far_gate, rows), (near_up, far_up, rows), (near_hidden, far_hidden, cots))
    for b in range(count):
        lanes = slice(b * size, (b + 1) * size)
        for i, (near, far, right) in enumerate(pairs):
            near, far = (ref[...].reshape(2 * ref.shape[1], hidden) for ref in (near, far))
            near_right, far_right = (jnp.concatenate([right[j][:, lanes], right[j + 1][:, lanes]], axis=0) for j in (0, 2))
            total = (dot(near, near_right, 0, 0) + dot(far, far_right, 0, 0)).astype(bf16)
            if i < 2:
                outs[b][i * hidden : (i + 1) * hidden, :] = total
            else:
                outs[count + b][...] = total


def feed_grads_call(lefts, hiddens, rows, cots, count):
    hidden, size = lefts[0].shape[2], rows[0].shape[1] // count
    outs = call(
        feed_grads_kernel, "feed_grads",
        (shape_of(2 * hidden, size),) * count + (shape_of(hidden, size),) * count,
        (*lefts, *hiddens, *rows, *cots), scalars=0, mib=40,
    )
    return outs[:count], outs[count:]


def result_kernel(near_hidden, far_hidden, *rest, count):
    weights, (near_mine, far_mine, sent) = rest[:count], rest[count:]
    size = near_mine.shape[1] // count
    for at, (ref, mine) in enumerate(((near_hidden, near_mine), (far_hidden, far_mine))):
        for i in range(count):
            lanes = slice(i * size, (i + 1) * size)
            weight = weights[i][2 * ref.shape[2] : 3 * ref.shape[2], :]
            mine[:, lanes] = dot(ref[0], weight, 1, 0)
            sent[at, :, lanes] = dot(ref[1], weight, 1, 0).astype(bf16)


def result_call(near_hidden, far_hidden, weights):
    _, size, _ = near_hidden.shape
    count = len(weights)
    width = weights[0].shape[1] * count
    return call(
        functools.partial(result_kernel, count=count), "result",
        (shape_of(size, width, dtype=f32), shape_of(size, width, dtype=f32), shape_of(2, size, width)),
        (near_hidden, far_hidden, *weights), scalars=0, mib=24,
    )


def out_grads_kernel(place_ref, chip_low, far_own, far_other, near_mixed, far_mixed, *rest):
    outs, far_low = rest[:-1], rest[-1]
    count = len(outs)
    rows = far_own.shape[0]
    for half, ref in enumerate((far_own, far_other)):
        far_low[pl.ds(pl.multiple_of((place_ref[1] ^ half) * rows, rows), rows), :] = ref[...]
    near, far = near_mixed[...], far_mixed[...]
    for out, near_rows, far_rows in zip(outs, cut(chip_low, count), cut(far_low, count)):
        out[...] = (dot(near, near_rows, 1, 0) + dot(far, far_rows, 1, 0)).T.astype(bf16)


def out_grads_call(place, chip_low, far_own, far_other, near_mixed, far_mixed, count):
    width, columns = chip_low.shape[1] // count, near_mixed.shape[0]
    return call(
        out_grads_kernel, "out_grads", tuple(shape_of(width, columns) for _ in range(count)),
        (place, chip_low, far_own, far_other, near_mixed, far_mixed),
        scratch=[pltpu.VMEM(chip_low.shape, bf16)],
    )


def join_kernel(*refs):
    count = len(refs) // 3
    for i in range(count):
        a, b, out = refs[2 * i], refs[2 * i + 1], refs[2 * count + i]
        out[...] = (a[...].astype(f32) + b[...].astype(f32)).astype(bf16)


def join_call(*pairs):
    outs = call(
        join_kernel, "join", tuple(shape_of(*a.shape) for a, _ in pairs), [x for pair in pairs for x in pair],
        scalars=0, mib=16,
    )
    return list(outs)


def collect(first, last, hit, todo):
    def step(at, count):
        todo[count] = at
        return count + hit(at).astype(jnp.int32)

    return lax.fori_loop(first, last, step, jnp.int32(0))


def two_ahead(count, todo, first, fill, work):
    def step(j, now):
        middle, after = todo[2 * j], todo[2 * j + 1]
        fill(1, middle)
        work(0, now)
        fill(0, after)
        work(1, middle)
        return after

    last = lax.fori_loop(0, count // 2, step, first)

    @pl.when(lax.rem(count, 2) == 0)
    def _():
        work(0, last)

    @pl.when(lax.rem(count, 2) == 1)
    def _():
        final = todo[count - 1]
        fill(1, final)
        work(0, last)
        work(1, final)


def fwd_kernel(todo_ref, place_ref, seg_ref, need_ref, *refs, first):
    outs, (score_a, score_b, top, total, todo) = refs[:-5], refs[-5:]
    if first:
        got_ref, qx_ref, kx_ref, out_ref, full_ref, lse_ref, keys, key_lanes, values, plain_values, queries = outs
        prep_kernel(place_ref, qx_ref, kx_ref, got_ref, keys, key_lanes, values, plain_values, queries)
    else:
        keys, values, queries, out_ref, full_ref, lse_ref = outs
    scores = (score_a, score_b)

    def attend(i, carry):
        at = todo_ref[i]
        need = need_ref[at]
        count = collect(0, at, lambda k: (seg_ref[k] & need) != 0, todo)
        query = queries[at]
        score_a[...] = causal(dot(keys[at], query, 1, 0))
        top[...] = jnp.full(top.shape, -BIG, f32)
        total[...] = jnp.zeros(total.shape, f32)

        def fill(slot, key_at):
            scores[slot][...] = dot(keys[key_at], query, 1, 0)

        def work(slot, key_at):
            score = scores[slot][...]
            old_top = top[...]
            new_top = jnp.maximum(old_top, jnp.max(score, axis=0, keepdims=True))
            weights = jnp.exp2(score - new_top).astype(bf16)
            total[...] = total[...] * jnp.exp2(old_top - new_top) + dot(values[key_at], weights, 1, 0)
            top[...] = new_top

        two_ahead(count, todo, at, fill, work)
        final = total[...]
        weight_sum = final[HEAD : HEAD + 1, :]
        mixed = final[:HEAD, :] * (1.0 / weight_sum)
        out_ref[i] = mixed.astype(bf16)
        full_ref[i] = mixed
        lse_ref[i] = three_parts(top[...] + jnp.log2(weight_sum))
        return carry

    lax.fori_loop(0, out_ref.shape[0], attend, 0)


def fwd_call(todo, place, seg, need, operands, first=False):
    count = todo.shape[0]
    if first:
        pieces, piece = 2 * operands[0].shape[0], operands[0].shape[2] // 2
        more = (
            shape_of(pieces, piece, 128),
            shape_of(pieces, HEAD, piece),
            shape_of(pieces, HEAD + 16, piece),
            shape_of(pieces, piece, 128),
            shape_of(pieces, 128, piece),
        )
    else:
        (pieces, _, piece), more = operands[2].shape, ()
    return call(
        functools.partial(fwd_kernel, first=first), "attend",
        (shape_of(count, HEAD, piece), shape_of(count, HEAD, piece, dtype=f32), shape_of(count, 16, piece)) + more,
        (todo, place, seg, need, *operands),
        scratch=[pltpu.VMEM((piece, piece), f32)] * 2
        + [pltpu.VMEM((1, piece), f32), pltpu.VMEM((HEAD + 16, piece), f32), pltpu.SMEM((pieces,), jnp.int32)],
        scalars=4,
    )


def bwd_kernel(todo_ref, place_ref, seg_ref, need_ref, cos_ref, sin_ref, keys, key_lanes, values, queries, *rest, stage, todo_count, extra, ready):
    if stage:
        grads, kept, sum_in, rest = rest[0], rest[1], rest[2], rest[3:]
    else:
        before, rest = rest[:6], rest[6:]
    outs, rest = rest[: (4, 3, 1)[stage]], rest[(4, 3, 1)[stage] :]
    if not stage:
        prep_back(place_ref, queries, *before, outs[1], outs[2], extra)
        queries, grads = outs[1], outs[2]
    score_a, grad_a, score_b, grad_b, key_sum, value_sum, todo = rest[:7]
    sums = rest[7] if stage == 2 else outs[-1]
    pieces = queries.shape[0]
    scores, prob_grads = (score_a, score_b), (grad_a, grad_b)
    sums[...] = sum_in[...] if stage else jnp.zeros(sums.shape, f32)
    if stage == 1:
        outs[0][:2] = kept[...]
    if stage == 2:
        outs[0][2:, : 2 * HEAD, :] = kept[...]
    ready()

    def attend(i, carry):
        at = todo_ref[i]
        seg = seg_ref[at]
        count = collect(at + 1, pieces, lambda q: (need_ref[q] & seg) != 0, todo)
        key, value, key_lane = keys[at], values[at], key_lanes[at]
        score_a[...] = causal(dot(key, queries[at], 1, 0))
        grad_a[...] = dot(value, grads[at], 1, 0)
        key_sum[...] = jnp.zeros(key_sum.shape, f32)
        value_sum[...] = jnp.zeros(value_sum.shape, f32)

        def fill(slot, query_at):
            scores[slot][...] = dot(key, queries[query_at], 1, 0)
            prob_grads[slot][...] = dot(value, grads[query_at], 1, 0)

        def work(slot, query_at):
            probs = jnp.exp2(scores[slot][...])
            score_grad = (probs * prob_grads[slot][...]).astype(bf16)
            value_sum[...] += dot(grads[query_at, :HEAD, :], probs.astype(bf16), 1, 1)
            key_sum[...] += dot(queries[query_at, :HEAD, :], score_grad, 1, 1)
            sums[query_at] += dot(key_lane, score_grad, 1, 0)

        two_ahead(count, todo, at, fill, work)
        key_grad = unrotate(key_sum[...] * (1.0 / LOG2E), cos_ref[at], sin_ref[at]).astype(bf16)
        value_grad = (0.5 * value_sum[...]).astype(bf16)

        def write(ref, place):
            ref[place, :HEAD, :] = key_grad
            ref[place, HEAD : 2 * HEAD, :] = value_grad

        if stage == 1:
            pl.when(i < 2)(lambda: write(outs[0], 2 + i))
            pl.when(i >= 2)(lambda: write(outs[1], i - 2))
        else:
            write(outs[0], i)
        return carry

    lax.fori_loop(0, todo_count, attend, 0)
    if stage == 2:
        for p in range(pieces):
            grad = unrotate(sums[p] * SCORE_SCALE, cos_ref[p], sin_ref[p]).astype(bf16)
            start = pl.multiple_of((2 + ((p % 2) ^ place_ref[0])) * HEAD, HEAD)
            outs[0][p // 2, pl.ds(start, HEAD), :] = grad


def bwd_call(stage, todo, place, seg, need, cosine, sine, keys, key_lanes, values, queries, more, extra):
    count, (pieces, _, piece) = todo.shape[0], queries.shape
    places = pieces // 2
    sums = shape_of(pieces, HEAD, piece, dtype=f32)
    outs = (
        (shape_of(2, 2 * HEAD, piece), shape_of(*queries.shape), shape_of(*queries.shape), sums),
        (shape_of(places, 2 * HEAD, piece), shape_of(2, 2 * HEAD, piece), sums),
        (shape_of(places, 4 * HEAD, piece),),
    )[stage]
    operands = (cosine, sine, keys, key_lanes, values, queries, *more)
    got = call(
        functools.partial(bwd_kernel, stage=stage, todo_count=count, extra=extra), "attend_back", outs,
        (todo, place, seg, need, *operands),
        scratch=[pltpu.VMEM((piece, piece), f32)] * 4
        + [pltpu.VMEM((HEAD, piece), f32)] * 2
        + [pltpu.SMEM((pieces,), jnp.int32)]
        + ([pltpu.VMEM(sums.shape, f32)] if stage == 2 else []),
        scalars=4, mib=36, late=(0, 1),
    )
    return got[0] if stage == 2 else got


def after(value, *earlier):
    return lax.optimization_barrier((value,) + earlier)[0]


def on_device(
    tokens, first_values, cotangent, parents, seg_lengths,
    w_query, w_key, w_value, w_out, w_gate, w_up, w_down, gain_attn, gain_ffn,
):
    assert tokens.shape[1] == 1
    fsdp_count, ctx_count, tp_count = (lax.axis_size(a) for a in ("fsdp", "ctx", "tp"))
    assert tp_count == 4 and ctx_count == 4
    fsdp_at, ctx_at, tp_at = (lax.axis_index(a) for a in ("fsdp", "ctx", "tp"))
    core_at, x_at = tp_at % 2, tp_at // 2
    own_rows, width = tokens.shape[0], tokens.shape[2]
    chip_rows = 2 * own_rows
    heads = w_query.shape[1] // HEAD
    head_width = heads * HEAD
    assert heads == ctx_count
    tree_len = own_rows * tp_count * ctx_count
    weight_rows, hidden = w_query.shape[0], w_gate.shape[1]
    two = fsdp_count == 2

    def over_core(value):
        return lax.ppermute(value, "tp", [(i, i ^ 1) for i in range(tp_count)])

    def over_x(value):
        return lax.ppermute(value, "tp", [(i, i ^ 2) for i in range(tp_count)])

    def over_fsdp(value):
        return lax.ppermute(value, "fsdp", [(0, 1), (1, 0)])

    def over_ctx(value, flip):
        return lax.ppermute(value, "ctx", [(i, i ^ flip) for i in range(ctx_count)])

    def exchange(by_place):
        return lax.all_to_all(by_place, "ctx", 0, 0, tiled=True)

    def relative(rows):
        if not two:
            return rows
        swapped = jnp.concatenate([rows[..., weight_rows:], rows[..., :weight_rows]], axis=-1)
        return jnp.where(fsdp_at == 0, rows, swapped)

    def by_x(near, far):
        return jnp.where(x_at == 0, jnp.concatenate([near, far], axis=0), jnp.concatenate([far, near], axis=0))

    def fsdp_sum(parts, axis=0):
        if not two:
            return lax.psum_scatter(parts[0], "fsdp", scatter_dimension=axis, tiled=True)
        return parts[0], over_fsdp(parts[1])

    def inward(low):
        return low, lax.ppermute(low, "ctx", [(0, 1), (3, 2)])

    def across(low):
        return low, lax.ppermute(low, "ctx", [(1, 2), (2, 1)])

    def outward(low):
        return low, lax.ppermute(low, "ctx", [(1, 0), (2, 3)])

    def join(pair):
        return (pair[0].astype(f32) + pair[1].astype(f32)).astype(bf16)

    def finish(pair):
        return jnp.where((ctx_at == 0) | (ctx_at == 3), pair[1], pair[0]).astype(f32)

    def hold(pair, *earlier):
        return (pair[0], after(pair[1], *earlier)) if isinstance(pair, tuple) else after(pair, *earlier)

    def step(*pairs):
        if not two:
            return [join(pair) if isinstance(pair, tuple) else pair for pair in pairs]
        return join_call(*pairs)

    own_tokens = tokens[:, 0, :]
    token_x = over_x(own_tokens)
    token_core = over_core(own_tokens)
    gains = jnp.stack([gain_attn, gain_ffn])
    if two:
        gains = jnp.concatenate([gains, over_fsdp(gains)], axis=1)
    else:
        gains = lax.all_gather(gains, "fsdp", axis=1, tiled=True)
    attention_gain = gains[0].reshape(1, width).astype(f32)
    ffn_gain = gains[1].reshape(1, width).astype(f32)
    three = (w_query, w_key, w_value)
    if two:
        own_three = stack_call(*three)
        qkv_weight = [own_three, over_fsdp(own_three)]
    else:
        qkv_weight = [stack_call(*(lax.all_gather(w, "fsdp", axis=0, tiled=True) for w in three))]
    count = len(qkv_weight)

    place = jnp.stack([x_at, core_at, ctx_at, fsdp_at]).astype(jnp.int32)
    position, query_extra, key_extra, seg_bits, need_bits = layout_call(parents, seg_lengths, tree_len, chip_rows)
    frequency = jnp.exp(-math.log(10000.0) * jnp.arange(HALF, dtype=f32) / HALF)
    angles = frequency[None, :, None] * position
    cosine, sine = jnp.cos(angles), jnp.sin(angles)

    def normalize(rows_f32):
        return lax.rsqrt(jnp.mean(rows_f32 * rows_f32, axis=-1, keepdims=True) + epsilon)

    first_flat = first_values[:, 0, :]

    def spread(pieces):
        return [over_ctx(piece, flip) if flip else piece for flip, piece in enumerate(pieces)]

    by_head, near_normed, far_normed = project_call(
        place, (own_tokens, token_core, token_x, over_core(token_x)), attention_gain, cosine, sine, first_flat, qkv_weight, two
    )
    got = exchange(by_head)
    others = (w_gate, w_up, w_down, w_out)
    if two:
        feed_own = stack_call(*(after(w.T, by_head) for w in others))
        feed_weight = [feed_own, over_fsdp(feed_own)]
    else:
        feed_weight = [stack_call(*(lax.all_gather(w, "fsdp", axis=0, tiled=True).T for w in others))]
    own_cot = relative(after(cotangent[:, 0, :], by_head))
    half_places = jnp.arange(ctx_count, dtype=jnp.int32) * 2
    far_out, far_full, far_lse, keys, key_lanes, value_lanes, values, queries = fwd_call(
        after(half_places + (1 - x_at), own_cot), place, seg_bits, need_bits, (got, query_extra, key_extra), True
    )
    cot_x = over_x(after(own_cot, got))
    out_weight = pick_call([after(w, far_out) for w in feed_weight], head_width)
    out_weight_x = over_x(out_weight)
    cot_core = over_core(after(own_cot, got))
    cot_x_core = over_core(cot_x)

    near_out, near_full, near_lse = fwd_call(
        after(half_places + x_at, far_out, out_weight, cot_x), place, seg_bits, need_bits, (keys, value_lanes, queries)
    )
    far_mixed = after(exchange(far_out), near_out).reshape(head_width, chip_rows)
    far_mixed_got = over_x(far_mixed)
    near_mixed = exchange(after(near_out, far_mixed)).reshape(head_width, chip_rows)

    mine, other = output_call(place, near_mixed, far_mixed_got, out_weight, out_weight_x)
    own_single = relative(own_tokens).astype(f32)
    middle = own_single + mine + over_core(other).astype(f32)

    middle_scale = normalize(middle)
    ffn_own = (middle * middle_scale * ffn_gain).astype(bf16)
    ffn_x = over_x(ffn_own)
    ffn_core = over_core(ffn_own)
    near_hidden, near_gate, near_up, near_mine, near_sent = feed_call(
        ffn_own, ffn_core, own_cot, cot_core, feed_weight, hidden
    )
    ffn_x = after(ffn_x, near_mine)
    ffn_x_core = over_core(ffn_x)
    far_hidden, far_gate, far_up, far_mine, far_sent = feed_call(
        ffn_x, ffn_x_core, cot_x, cot_x_core, feed_weight, hidden
    )
    far_sum = (far_mine + over_core(far_sent).astype(f32)).astype(bf16)
    far_sum_got = over_x(far_sum)
    near_sum = near_mine + over_core(near_sent).astype(f32)

    all_cot = (after(own_cot, far_sum), cot_core, cot_x, cot_x_core)
    all_ffn = (after(ffn_own, far_sum), ffn_core, ffn_x, ffn_x_core)
    first_parts, second_parts = feed_grads_call(
        (near_gate, far_gate, near_up, far_up), (near_hidden, far_hidden), all_ffn, all_cot, count
    )
    first_sum = fsdp_sum(first_parts, 1)
    second_sum = fsdp_sum(second_parts, 1)
    ffn_grad = near_sum + after(far_sum_got, first_parts[0]).astype(f32)

    weighted = ffn_grad * ffn_gain
    middle_grad = (
        own_cot.astype(f32)
        + middle_scale * weighted
        - middle * (middle_scale**3 * jnp.mean(weighted * middle, axis=-1, keepdims=True))
    )
    middle_low = middle_grad.astype(bf16)
    near_heads, far_heads, chip_low = heads_call(place, middle_low, over_core(middle_low), out_weight, out_weight_x)
    far_out_grad = over_x(far_heads)
    near_grads = exchange(near_heads.reshape(heads, HEAD, chip_rows))
    far_grads = exchange(after(far_out_grad, near_grads).reshape(heads, HEAD, chip_rows))

    ffn_gain_part = jnp.sum(after(ffn_grad, near_heads) * middle * middle_scale, axis=0)
    low_x = over_x(after(middle_low, far_out_grad))
    low_x_core = over_core(low_x)
    near_result, far_result, sent = result_call(after(near_hidden, near_heads), far_hidden, feed_weight)
    sent_got = over_core(sent)
    (first_low,) = step(hold(first_sum, far_grads, sent))
    first_in = inward(first_low)
    def back(stage, places, more, *earlier):
        return bwd_call(
            stage, after(jnp.stack(places).astype(jnp.int32), *earlier), place, seg_bits, need_bits, cosine, sine,
            keys, key_lanes, values, more[0], more[1:], query_extra.shape[1],
        )

    far_at, near_at = [2 * i + 1 - x_at for i in range(4)], [2 * i + x_at for i in range(4)]
    first_kv, back_queries, grads, query_sum = back(
        0, far_at[:2], (queries, near_grads, far_grads, near_full, far_full, near_lse, far_lse), first_low
    )

    first_low, second_low = step(hold(first_in, first_kv), hold(second_sum, first_kv))
    first_across, second_in = across(first_low), inward(second_low)
    far_kv, near_kv, query_sum = back(
        1, far_at[2:] + near_at[2:], (back_queries, grads, first_kv, query_sum), first_low
    )

    first_low, second_low = step(hold(first_across, far_kv), hold(second_in, far_kv))
    first_done, second_across = outward(first_low), across(second_low)
    far_kv_got = exchange(after(far_kv, first_low))
    last = back(2, near_at[:2], (back_queries, grads, near_kv, query_sum), first_low)

    (second_low,) = step(hold(second_across, last))
    second_done = outward(second_low)
    last_got = exchange(after(last, second_low, first_done[1]))
    far_kv_got = after(far_kv_got, last)
    out_parts = out_grads_call(after(place, last), chip_low, low_x, low_x_core, near_mixed, far_mixed, count)
    out_sum = fsdp_sum(out_parts)
    far_result_got = over_x((after(far_result, out_parts[0]) + sent_got[1].astype(f32)).astype(bf16))
    second_all = finish(hold(second_done, out_parts[0]))
    layer_out = relative((after(middle, second_all) + near_result + sent_got[0].astype(f32) + far_result_got.astype(f32)).astype(bf16))
    first_all = finish(hold(first_done, second_low))
    (out_low,) = step(hold(out_sum, layer_out))
    last_got = after(last_got, first_all, out_low)
    out_in = inward(out_low)

    qkv_parts, near_mine, near_other, far_mine, far_other, gain_part = last_call(
        place, near_normed, far_normed, far_kv_got, last_got, qkv_weight
    )
    far_rows_got = over_x((far_mine + over_core(far_other).astype(f32)).astype(bf16))
    near_rows_got = over_core(near_other)
    qkv_sum = fsdp_sum(qkv_parts)
    gain_sum = jnp.concatenate([gain_part / attention_gain, ffn_gain_part[None]], axis=0)
    if two:
        gain_sum = gain_sum + over_core(gain_sum)
        gain_sum = gain_sum + over_x(gain_sum)
    qkv_low, out_low = step(hold(qkv_sum, gain_sum), hold(out_in, gain_sum))
    qkv_in, out_across = inward(qkv_low), across(out_low)
    near_value = after(last_got, qkv_low)[:, HEAD : 2 * HEAD].reshape(head_width, chip_rows)
    far_value = far_kv_got[:, HEAD:].reshape(head_width, chip_rows)
    grad_values = by_x(near_value.T, far_value.T).astype(f32)
    if two:
        gain_sum = gain_sum[:, :weight_rows] + over_fsdp(after(gain_sum, qkv_low)[:, weight_rows:])
        gain_sum = gain_sum + over_ctx(gain_sum, 1)
    qkv_low, out_low = step(hold(qkv_in, gain_sum, grad_values), hold(out_across, gain_sum))
    lows = [qkv_low]
    qkv_across, out_done = across(qkv_low), outward(out_low)
    if two:
        gain_sum = gain_sum + over_ctx(after(gain_sum, qkv_low), 2)
    else:
        gain_sum = lax.psum(gain_sum, ("fsdp", "ctx", "tp"))
        gain_sum = lax.dynamic_slice_in_dim(gain_sum, fsdp_at * weight_rows, weight_rows, 1)
    (qkv_low,) = step(hold(qkv_across, gain_sum, out_done[1]))
    grad_query, grad_key, grad_value = jnp.split(finish(outward(qkv_low)), 3)
    grad_out = finish(out_done)
    grad_gate, grad_up, grad_down = first_all[:hidden].T, first_all[hidden:].T, second_all.T

    normed_grad = after(near_mine, lows[0]) + near_rows_got.astype(f32) + far_rows_got.astype(f32)
    scale = normalize(own_single)
    weighted = normed_grad * attention_gain
    grad_tokens = (
        middle_grad + scale * weighted - own_single * (scale**3 * jnp.mean(weighted * own_single, axis=-1, keepdims=True))
    )
    return (
        layer_out[:, None, :],
        relative(grad_tokens)[:, None, :],
        grad_values[:, None, :],
        grad_query,
        grad_key,
        grad_value,
        grad_out,
        grad_gate,
        grad_up,
        grad_down,
        gain_sum[0],
        gain_sum[1],
    )

def solution(mesh):
    rows, columns = P(("ctx", "tp"), "fsdp", None), P("ctx", "fsdp", "tp")
    weight, gain = P("fsdp", "tp"), P("fsdp")
    return jax.shard_map(
        on_device,
        mesh=mesh,
        in_specs=(rows, columns, rows, P("fsdp", None), P("fsdp", None)) + (weight,) * 7 + (gain,) * 2,
        out_specs=(rows, rows, columns) + (weight,) * 7 + (gain,) * 2,
        check_vma=False,
    )
```

```python
import functools
import math

import jax
import jax.numpy as jnp
from jax import lax
from jax.experimental import pallas as pl
from jax.experimental.pallas import tpu as pltpu
from jax.sharding import PartitionSpec as P

HEAD = 64
HALF = HEAD // 2
BIG = 1e30
LOG2E = 1.4426950408889634
SCORE_SCALE = HEAD**-0.5
QUERY_SCALE = SCORE_SCALE * LOG2E
epsilon = 1e-05
f32 = jnp.float32
bf16 = jnp.bfloat16


def dot(a, b, ca, cb):
    return lax.dot_general(a, b, (((ca,), (cb,)), ((), ())), preferred_element_type=f32)


def layout_kernel(par_ref, len_ref, pos_ref, qx_ref, kx_ref, seg_ref, need_ref, anc_sc, above_sc, *, segs, tokens, piece):
    token = lax.broadcasted_iota(jnp.int32, (1, tokens), 1)
    pos = jnp.zeros((1, tokens), jnp.int32)
    seg_of = jnp.full((1, tokens), -1, jnp.int32)
    bits = jnp.zeros((1, tokens), jnp.int32)
    for b in range(tokens // piece):
        seg_ref[b] = 0
        need_ref[b] = 0
    off = jnp.int32(0)
    for s in range(segs):
        length = len_ref[0, s]
        if s == 0:
            anc, above = jnp.int32(1), jnp.int32(0)
        else:
            parent = par_ref[0, s]
            anc = anc_sc[parent] | jnp.int32(1 << s)
            above = above_sc[parent] + len_ref[0, parent]
        anc_sc[s] = anc
        above_sc[s] = above
        started = token >= off
        seg_of = jnp.where(started, s, seg_of)
        pos = jnp.where(started, token - off + above, pos)
        bits = jnp.where(started, anc, bits)

        def mark(b, carry, anc=anc, s=s):
            seg_ref[b] = seg_ref[b] | jnp.int32(1 << s)
            need_ref[b] = need_ref[b] | anc
            return carry

        lax.fori_loop(off // piece, (off + length - 1) // piece + 1, mark, 0)
        off = off + length
    row = lax.broadcasted_iota(jnp.int32, (kx_ref.shape[1], tokens), 0)
    key_extra = jnp.where(row == seg_of, -BIG, 0.0).astype(bf16)
    linked = lax.shift_right_logical(jnp.broadcast_to(bits, row.shape), row) & 1
    query_extra = jnp.where(linked == 1, 0.0, 1.0).astype(bf16)
    for p in range(tokens // piece):
        lanes = slice(p * piece, (p + 1) * piece)
        pos_ref[p] = pos[:, lanes].astype(f32)
        kx_ref[p] = key_extra[:, lanes]
        qx_ref[p] = query_extra[:, lanes]


SMEM = pl.BlockSpec(memory_space=pltpu.SMEM)
VMEM = pl.BlockSpec(memory_space=pltpu.VMEM)


def layout_call(parents, lengths, tokens, piece):
    segs = parents.shape[-1]
    rows = -(-segs // 16) * 16
    return pl.pallas_call(
        functools.partial(layout_kernel, segs=segs, tokens=tokens, piece=piece),
        out_shape=(
            jax.ShapeDtypeStruct((tokens // piece, 1, piece), f32),
            jax.ShapeDtypeStruct((tokens // piece, rows, piece), bf16),
            jax.ShapeDtypeStruct((tokens // piece, rows, piece), bf16),
            jax.ShapeDtypeStruct((tokens // piece,), jnp.int32),
            jax.ShapeDtypeStruct((tokens // piece,), jnp.int32),
        ),
        in_specs=[SMEM, SMEM],
        out_specs=(VMEM, VMEM, VMEM, SMEM, SMEM),
        scratch_shapes=[pltpu.SMEM((segs,), jnp.int32), pltpu.SMEM((segs,), jnp.int32)],
        cost_estimate=pl.CostEstimate(flops=0, bytes_accessed=1 << 16, transcendentals=0),
        name="layout",
    )(parents, lengths)


def causal(scores):
    key_at = lax.broadcasted_iota(jnp.int32, scores.shape, 0)
    query_at = lax.broadcasted_iota(jnp.int32, scores.shape, 1)
    return jnp.where(key_at <= query_at, scores, -BIG)


def three_parts(row):
    at = lax.broadcasted_iota(jnp.int32, (16, row.shape[1]), 0)
    high = row.astype(bf16).astype(f32)
    rest = row - high
    mid = rest.astype(bf16).astype(f32)
    low = rest - mid
    return jnp.where(at == 0, high, jnp.where(at == 1, mid, jnp.where(at == 2, low, 0.0))).astype(bf16)


def unrotate(values, cosine, sine):
    a, b = values[:HALF], values[HALF:]
    return jnp.concatenate([a * cosine + b * sine, b * cosine - a * sine], axis=0)


def prep_kernel(place_ref, qx_ref, kx_ref, got_ref, keys, key_lanes, value_lanes, values, queries):
    piece = got_ref.shape[2] // 2
    extra = qx_ref.shape[1]
    minus = jnp.full((16, piece), -1.0, bf16)
    pad_key = jnp.zeros((128 - HEAD - extra - 16, piece), bf16)
    pad_value = jnp.zeros((128 - HEAD - 16, piece), bf16)
    for half in (0, 1):
        for p in range(got_ref.shape[0]):
            at = 2 * p + (place_ref[0] ^ half)
            got = got_ref[p, :, half * piece : (half + 1) * piece]
            query, key, value = got[:HEAD, :], got[HEAD : 2 * HEAD, :], got[2 * HEAD :, :]
            key_lanes[at] = key
            keys[at] = jnp.concatenate([key, kx_ref[at], minus, pad_key], axis=0).T
            value_lanes[at] = jnp.concatenate([value, -minus], axis=0)
            values[at] = jnp.concatenate([value, minus, pad_value], axis=0).T
            queries[at] = jnp.concatenate([query, qx_ref[at], jnp.zeros((128 - HEAD - extra, piece), bf16)], axis=0)


def shape_of(*sizes, dtype=bf16):
    return jax.ShapeDtypeStruct(sizes, dtype)


def call(kernel, name, out_shape, operands, scratch=(), scalars=1, mib=20, late=()):
    outs = out_shape if isinstance(out_shape, tuple) else (out_shape,)
    arrays = operands[scalars:]
    count, total = len(arrays), len(arrays) + len(outs)

    def body(*refs):
        first, rest = refs[:scalars], refs[scalars:]
        outside, inside, sems, rest = rest[:total], rest[total : 2 * total], rest[2 * total], rest[2 * total + 1 :]
        copies = [pltpu.make_async_copy(outside[i], inside[i], sems.at[i]) for i in range(count)]
        for copy in copies:
            copy.start()
        for i in range(count):
            if i not in late:
                copies[i].wait()
        more = {"ready": lambda: [copies[i].wait() for i in late]} if late else {}
        kernel(*first, *inside, *rest, **more)
        copies = [pltpu.make_async_copy(inside[i], outside[i], sems.at[i]) for i in range(count, total)]
        for copy in copies:
            copy.start()
        for copy in copies:
            copy.wait()

    got = pl.pallas_call(
        body,
        out_shape=outs,
        in_specs=[SMEM] * scalars + [pl.BlockSpec(memory_space=pltpu.HBM)] * count,
        out_specs=(pl.BlockSpec(memory_space=pltpu.HBM),) * len(outs),
        scratch_shapes=[pltpu.VMEM(x.shape, x.dtype) for x in (*arrays, *outs)]
        + [pltpu.SemaphoreType.DMA((total,))]
        + list(scratch),
        compiler_params=pltpu.CompilerParams(vmem_limit_bytes=60 << 20),
        cost_estimate=pl.CostEstimate(flops=0, bytes_accessed=1 << 16, transcendentals=0),
        name=name,
    )(*operands)
    return got if isinstance(out_shape, tuple) else got[0]


def cut(ref, count):
    size = ref.shape[1] // count
    return [ref[:, i * size : (i + 1) * size] for i in range(count)]


def project_kernel(place_ref, near_own, near_other, far_own, far_other, gain_ref, cos_ref, sin_ref, first_ref, *rest, count, swap):
    weights, (out, near_out, far_out, raw) = rest[:count], rest[count:]
    heads_width = raw.shape[0] // 3
    size, width = near_own.shape
    block = width // count
    for refs, normed in (((near_own, near_other), near_out), ((far_own, far_other), far_out)):
        for half, ref in enumerate(refs):
            single = ref[...].astype(f32)
            scale = lax.rsqrt(jnp.mean(single * single, axis=-1, keepdims=True) + epsilon)
            if swap:
                turned = jnp.concatenate([single[:, block:], single[:, :block]], axis=1)
                single = jnp.where(place_ref[3] == 0, single, turned)
            at = pl.multiple_of((place_ref[1] ^ half) * size, size)
            normed[pl.ds(at, size), :] = (single * scale * gain_ref[...]).astype(bf16)
    piece = 2 * size
    turned = [[w[i * block : (i + 1) * block, :].T for w in weights] for i in range(3)]
    for half, rows_ref in enumerate((near_out, far_out)):
        rows = cut(rows_ref, count)
        for i in range(3):
            raw[i * heads_width : (i + 1) * heads_width, :] = sum(dot(w, r, 1, 1) for w, r in zip(turned[i], rows))
        x_half = place_ref[0] ^ half
        at = 2 * place_ref[2] + x_half
        cosine, sine = cos_ref[at], sin_ref[at]
        start = pl.multiple_of(x_half * piece, piece)
        first = first_ref[pl.ds(start, piece), :].astype(f32).T

        def turn(values):
            a, b = values[:HALF], values[HALF:]
            return jnp.concatenate([a * cosine - b * sine, b * cosine + a * sine], axis=0)

        lanes = slice(half * piece, (half + 1) * piece)
        for at in range(heads_width // HEAD):
            rows_at = [slice(i * heads_width + at * HEAD, i * heads_width + (at + 1) * HEAD) for i in range(3)]
            value = 0.5 * raw[rows_at[2], :] + 0.5 * first[at * HEAD : (at + 1) * HEAD]
            out[at, :HEAD, lanes] = (turn(raw[rows_at[0], :]) * QUERY_SCALE).astype(bf16)
            out[at, HEAD : 2 * HEAD, lanes] = turn(raw[rows_at[1], :]).astype(bf16)
            out[at, 2 * HEAD :, lanes] = value.astype(bf16)


def project_call(place, rows, gain, cosine, sine, first, weights, swap):
    (size, width), columns = rows[0].shape, weights[0].shape[1]
    return call(
        functools.partial(project_kernel, count=len(weights), swap=swap), "project",
        (shape_of(columns // HEAD, 3 * HEAD, 4 * size), shape_of(2 * size, width), shape_of(2 * size, width)),
        (place, *rows, gain, cosine, sine, first, *weights),
        scratch=[pltpu.VMEM((3 * columns, 2 * size), f32)],
    )


def stack_kernel(*refs):
    out, at = refs[-1], 0
    for ref in refs[:-1]:
        rows = ref.shape[0]
        out[at : at + rows, :] = ref[...]
        at += rows


def pick_kernel(*refs):
    out = refs[-1]
    rows = out.shape[0]
    size = out.shape[1] // (len(refs) - 1)
    for i, ref in enumerate(refs[:-1]):
        out[:, i * size : (i + 1) * size] = ref[ref.shape[0] - rows :, :]


def pick_call(blocks, rows):
    return call(pick_kernel, "pick", shape_of(rows, blocks[0].shape[1] * len(blocks)), tuple(blocks), scalars=0)


def stack_call(*arrays):
    rows = sum(a.shape[0] for a in arrays)
    return call(stack_kernel, "stack", shape_of(rows, arrays[0].shape[1]), arrays, scalars=0, mib=16)


def split_core(place_ref, total, mine_ref, other_ref):
    rows = mine_ref.shape[0]
    mine_ref[...] = total[pl.ds(pl.multiple_of(place_ref[1] * rows, rows), rows), :]
    other_ref[...] = total[pl.ds(pl.multiple_of((1 - place_ref[1]) * rows, rows), rows), :].astype(bf16)


def output_kernel(place_ref, near_ref, far_ref, *rest):
    near_weight, far_weight, mine_ref, other_ref, total = rest
    total[...] = dot(near_ref[...].T, near_weight[...], 1, 0) + dot(far_ref[...].T, far_weight[...], 1, 0)
    split_core(place_ref, total, mine_ref, other_ref)


def output_call(place, near, far, near_weight, far_weight):
    rows, width = near.shape[1], near_weight.shape[1]
    return call(
        output_kernel, "out_project",
        (shape_of(rows // 2, width, dtype=f32), shape_of(rows // 2, width)),
        (place, near, far, near_weight, far_weight),
        scratch=[pltpu.VMEM((rows, width), f32)],
    )


def heads_kernel(place_ref, own_ref, other_ref, near_weight, far_weight, near_out, far_out, chip):
    rows = own_ref.shape[0]
    for half, ref in enumerate((own_ref, other_ref)):
        chip[pl.ds(pl.multiple_of((place_ref[1] ^ half) * rows, rows), rows), :] = ref[...]
    far_out[...] = dot(far_weight[...], chip[...], 1, 1).astype(bf16)
    near_out[...] = dot(near_weight[...], chip[...], 1, 1).astype(bf16)


def heads_call(place, own, other, near_weight, far_weight):
    rows, columns = 2 * own.shape[0], near_weight.shape[0]
    return call(
        heads_kernel, "out_back",
        (shape_of(columns, rows), shape_of(columns, rows), shape_of(rows, own.shape[1])),
        (place, own, other, near_weight, far_weight),
    )


def feed_kernel(rows_ref, other_ref, cot_ref, cot_other_ref, *rest, count):
    hidden = rest[count].shape[2]
    gate_w, up_w, down_w = ([w.at[i * hidden : (i + 1) * hidden] for w in rest[:count]] for i in range(3))
    hidden_ref, gate_ref, up_ref, mine_ref, sent_ref, rows_sc, cot_sc, back_sc = rest[count:]
    size = rows_ref.shape[0]
    rows_sc[0], rows_sc[1] = rows_ref[...], other_ref[...]
    cot_sc[0], cot_sc[1] = cot_ref[...], cot_other_ref[...]
    block = rows_ref.shape[1] // count

    def step(at, carry):
        lanes = [slice(i * block, (i + 1) * block) for i in range(count)]
        rows, cots = [rows_sc[at, :, s] for s in lanes], [cot_sc[at, :, s] for s in lanes]
        gate = sum(dot(r, w[...], 1, 1) for r, w in zip(rows, gate_w))
        up = sum(dot(r, w[...], 1, 1) for r, w in zip(rows, up_w))
        hidden_grad = sum(dot(r, w[...], 1, 1) for r, w in zip(cots, down_w))
        sig = 1.0 / (1.0 + jnp.exp(-gate))
        act = gate * sig
        hidden_ref[at] = (act * up).astype(bf16)
        gate_grad = (hidden_grad * up * (sig * (1.0 + gate * (1.0 - sig)))).astype(bf16)
        up_grad = (hidden_grad * act).astype(bf16)
        gate_ref[at] = gate_grad
        up_ref[at] = up_grad
        for i in range(count):
            back_sc[at, :, lanes[i]] = dot(gate_grad, gate_w[i][...], 1, 0) + dot(up_grad, up_w[i][...], 1, 0)
        return carry

    lax.fori_loop(0, 2, step, 0)
    mine_ref[...] = back_sc[0]
    sent_ref[...] = back_sc[1].astype(bf16)


def feed_call(rows, other, cot, cot_other, weights, hidden):
    size, width = rows.shape
    count = len(weights)
    return call(
        functools.partial(feed_kernel, count=count), "feed",
        (shape_of(2, size, hidden),) * 3 + (shape_of(size, width, dtype=f32), shape_of(size, width)),
        (rows, other, cot, cot_other, *weights),
        scratch=[pltpu.VMEM((2, size, width), bf16)] * 2 + [pltpu.VMEM((2, size, width), f32)],
        scalars=0, mib=40,
    )


def prep_back(place_ref, queries, near_grad, far_grad, near_full, far_full, near_lse, far_lse, queries_out, grads_out, extra):
    places, _, piece = near_grad.shape
    queries_out[...] = queries[...]
    pad = jnp.zeros((128 - HEAD - 16, piece), bf16)
    for half, (grad, full, lse) in enumerate(((near_grad, near_full, near_lse), (far_grad, far_full, far_lse))):
        for p in range(places):
            at = 2 * p + (place_ref[0] ^ half)
            queries_out[at, HEAD + extra : HEAD + extra + 16, :] = lse[p]
            delta = jnp.sum(grad[p].astype(f32) * full[p], axis=0, keepdims=True)
            grads_out[at] = jnp.concatenate([grad[p], three_parts(delta), pad], axis=0)


def by_projection(kv, last):
    columns = kv.shape[0] * HEAD
    flat = lambda ref, at: ref[:, at * HEAD : (at + 1) * HEAD, :].reshape(columns, ref.shape[2])
    return (flat(last, 2), flat(last, 0), flat(last, 1)), (flat(last, 3), flat(kv, 0), flat(kv, 1))


def weights_kernel(near_rows, far_rows, kv, last, *parts):
    size = near_rows.shape[1] // len(parts)
    near, far = by_projection(kv, last)
    for i in range(3):
        for b, part in enumerate(parts):
            lanes = slice(b * size, (b + 1) * size)
            sums = dot(near[i], near_rows[:, lanes], 1, 0) + dot(far[i], far_rows[:, lanes], 1, 0)
            part[i * size : (i + 1) * size, :] = sums.T.astype(bf16)


def weights_call(near_rows, far_rows, kv, last, count):
    width, columns = near_rows.shape[1], kv.shape[0] * HEAD
    return call(
        weights_kernel, "weight_grads", tuple(shape_of(3 * width // count, columns) for _ in range(count)),
        (near_rows, far_rows, kv, last), scalars=0,
    )


def rows_kernel(place_ref, near_rows, far_rows, kv, last, *rest, count):
    weights, (near_mine, near_other, far_mine, far_other, gain_ref, value_ref, total) = rest[:count], rest[count:]
    size = near_rows.shape[1] // count
    near, far = by_projection(kv, last)
    for half, grads in enumerate((near, far)):
        value = grads[2].T.astype(f32)
        tokens, columns = value.shape
        folds = columns // 128
        for j in range(folds):
            rows_at = pl.ds((place_ref[0] ^ half) * tokens * folds + j, tokens, stride=folds)
            value_ref[rows_at, :] = value[:, j * 128 : (j + 1) * 128]
    gain_ref[...] = jnp.zeros(gain_ref.shape, f32)
    for grads, rows, mine, other in ((far, far_rows, far_mine, far_other), (near, near_rows, near_mine, near_other)):
        turned = [g.T for g in grads]
        for b in range(count):
            lanes = slice(b * size, (b + 1) * size)
            part = sum(dot(g, weights[b][i * size : (i + 1) * size, :], 1, 1) for i, g in enumerate(turned))
            total[:, lanes] = part
            gain_ref[:, lanes] += jnp.sum(part * rows[:, lanes].astype(f32), axis=0, keepdims=True)
        split_core(place_ref, total, mine, other)


def rows_call(place, near_rows, far_rows, kv, last, weights):
    size, width = near_rows.shape
    rows = (shape_of(size // 2, width, dtype=f32), shape_of(size // 2, width))
    values = shape_of(2 * size * kv.shape[0] * HEAD // 128, 128, dtype=f32)
    return call(
        functools.partial(rows_kernel, count=len(weights)), "rows_back",
        rows + rows + (shape_of(1, width, dtype=f32), values),
        (place, near_rows, far_rows, kv, last, *weights),
        scratch=[pltpu.VMEM((size, width), f32)],
    )


def feed_grads_kernel(near_gate, far_gate, near_up, far_up, near_hidden, far_hidden, *refs):
    rows, cots, outs = refs[:4], refs[4:8], refs[8:]
    count = len(outs) // 2
    size = rows[0].shape[1] // count
    hidden = near_gate.shape[2]
    pairs = ((near_gate, far_gate, rows), (near_up, far_up, rows), (near_hidden, far_hidden, cots))
    for b in range(count):
        lanes = slice(b * size, (b + 1) * size)
        for i, (near, far, right) in enumerate(pairs):
            near, far = (ref[...].reshape(2 * ref.shape[1], hidden) for ref in (near, far))
            near_right, far_right = (jnp.concatenate([right[j][:, lanes], right[j + 1][:, lanes]], axis=0) for j in (0, 2))
            total = (dot(near, near_right, 0, 0) + dot(far, far_right, 0, 0)).astype(bf16)
            if i < 2:
                outs[b][i * hidden : (i + 1) * hidden, :] = total
            else:
                outs[count + b][...] = total


def feed_grads_call(lefts, hiddens, rows, cots, count):
    hidden, size = lefts[0].shape[2], rows[0].shape[1] // count
    outs = call(
        feed_grads_kernel, "feed_grads",
        (shape_of(2 * hidden, size),) * count + (shape_of(hidden, size),) * count,
        (*lefts, *hiddens, *rows, *cots), scalars=0, mib=40,
    )
    return outs[:count], outs[count:]


def result_kernel(near_hidden, far_hidden, *rest, count):
    weights, (near_mine, far_mine, sent) = rest[:count], rest[count:]
    size = near_mine.shape[1] // count
    for at, (ref, mine) in enumerate(((near_hidden, near_mine), (far_hidden, far_mine))):
        for i in range(count):
            lanes = slice(i * size, (i + 1) * size)
            weight = weights[i][2 * ref.shape[2] : 3 * ref.shape[2], :]
            mine[:, lanes] = dot(ref[0], weight, 1, 0)
            sent[at, :, lanes] = dot(ref[1], weight, 1, 0).astype(bf16)


def result_call(near_hidden, far_hidden, weights):
    _, size, _ = near_hidden.shape
    count = len(weights)
    width = weights[0].shape[1] * count
    return call(
        functools.partial(result_kernel, count=count), "result",
        (shape_of(size, width, dtype=f32), shape_of(size, width, dtype=f32), shape_of(2, size, width)),
        (near_hidden, far_hidden, *weights), scalars=0, mib=24,
    )


def out_grads_kernel(place_ref, chip_low, far_own, far_other, near_mixed, far_mixed, *rest):
    outs, far_low = rest[:-1], rest[-1]
    count = len(outs)
    rows = far_own.shape[0]
    for half, ref in enumerate((far_own, far_other)):
        far_low[pl.ds(pl.multiple_of((place_ref[1] ^ half) * rows, rows), rows), :] = ref[...]
    near, far = near_mixed[...], far_mixed[...]
    for out, near_rows, far_rows in zip(outs, cut(chip_low, count), cut(far_low, count)):
        out[...] = (dot(near, near_rows, 1, 0) + dot(far, far_rows, 1, 0)).T.astype(bf16)


def out_grads_call(place, chip_low, far_own, far_other, near_mixed, far_mixed, count):
    width, columns = chip_low.shape[1] // count, near_mixed.shape[0]
    return call(
        out_grads_kernel, "out_grads", tuple(shape_of(width, columns) for _ in range(count)),
        (place, chip_low, far_own, far_other, near_mixed, far_mixed),
        scratch=[pltpu.VMEM(chip_low.shape, bf16)],
    )


def join_kernel(*refs):
    count = len(refs) // 3
    for i in range(count):
        a, b, out = refs[2 * i], refs[2 * i + 1], refs[2 * count + i]
        out[...] = (a[...].astype(f32) + b[...].astype(f32)).astype(bf16)


def join_call(*pairs):
    outs = call(
        join_kernel, "join", tuple(shape_of(*a.shape) for a, _ in pairs), [x for pair in pairs for x in pair],
        scalars=0, mib=16,
    )
    return list(outs)


def collect(first, last, hit, todo):
    def step(at, count):
        todo[count] = at
        return count + hit(at).astype(jnp.int32)

    return lax.fori_loop(first, last, step, jnp.int32(0))


def two_ahead(count, todo, first, fill, work):
    def step(j, now):
        middle, after = todo[2 * j], todo[2 * j + 1]
        fill(1, middle)
        work(0, now)
        fill(0, after)
        work(1, middle)
        return after

    last = lax.fori_loop(0, count // 2, step, first)

    @pl.when(lax.rem(count, 2) == 0)
    def _():
        work(0, last)

    @pl.when(lax.rem(count, 2) == 1)
    def _():
        final = todo[count - 1]
        fill(1, final)
        work(0, last)
        work(1, final)


def fwd_kernel(todo_ref, place_ref, seg_ref, need_ref, *refs, first):
    outs, (score_a, score_b, top, total, todo) = refs[:-5], refs[-5:]
    if first:
        got_ref, qx_ref, kx_ref, out_ref, full_ref, lse_ref, keys, key_lanes, values, plain_values, queries = outs
        prep_kernel(place_ref, qx_ref, kx_ref, got_ref, keys, key_lanes, values, plain_values, queries)
    else:
        keys, values, queries, out_ref, full_ref, lse_ref = outs
    scores = (score_a, score_b)

    def attend(i, carry):
        at = todo_ref[i]
        need = need_ref[at]
        count = collect(0, at, lambda k: (seg_ref[k] & need) != 0, todo)
        query = queries[at]
        score_a[...] = causal(dot(keys[at], query, 1, 0))
        top[...] = jnp.full(top.shape, -BIG, f32)
        total[...] = jnp.zeros(total.shape, f32)

        def fill(slot, key_at):
            scores[slot][...] = dot(keys[key_at], query, 1, 0)

        def work(slot, key_at):
            score = scores[slot][...]
            old_top = top[...]
            new_top = jnp.maximum(old_top, jnp.max(score, axis=0, keepdims=True))
            weights = jnp.exp2(score - new_top).astype(bf16)
            total[...] = total[...] * jnp.exp2(old_top - new_top) + dot(values[key_at], weights, 1, 0)
            top[...] = new_top

        two_ahead(count, todo, at, fill, work)
        final = total[...]
        weight_sum = final[HEAD : HEAD + 1, :]
        mixed = final[:HEAD, :] * (1.0 / weight_sum)
        out_ref[i] = mixed.astype(bf16)
        full_ref[i] = mixed
        lse_ref[i] = three_parts(top[...] + jnp.log2(weight_sum))
        return carry

    lax.fori_loop(0, out_ref.shape[0], attend, 0)


def fwd_call(todo, place, seg, need, operands, first=False):
    count = todo.shape[0]
    if first:
        pieces, piece = 2 * operands[0].shape[0], operands[0].shape[2] // 2
        more = (
            shape_of(pieces, piece, 128),
            shape_of(pieces, HEAD, piece),
            shape_of(pieces, HEAD + 16, piece),
            shape_of(pieces, piece, 128),
            shape_of(pieces, 128, piece),
        )
    else:
        (pieces, _, piece), more = operands[2].shape, ()
    return call(
        functools.partial(fwd_kernel, first=first), "attend",
        (shape_of(count, HEAD, piece), shape_of(count, HEAD, piece, dtype=f32), shape_of(count, 16, piece)) + more,
        (todo, place, seg, need, *operands),
        scratch=[pltpu.VMEM((piece, piece), f32)] * 2
        + [pltpu.VMEM((1, piece), f32), pltpu.VMEM((HEAD + 16, piece), f32), pltpu.SMEM((pieces,), jnp.int32)],
        scalars=4,
    )


def bwd_kernel(todo_ref, place_ref, seg_ref, need_ref, cos_ref, sin_ref, keys, key_lanes, values, queries, *rest, stage, todo_count, extra, ready):
    if stage:
        grads, kept, sum_in, rest = rest[0], rest[1], rest[2], rest[3:]
    else:
        before, rest = rest[:6], rest[6:]
    outs, rest = rest[: (4, 3, 1)[stage]], rest[(4, 3, 1)[stage] :]
    if not stage:
        prep_back(place_ref, queries, *before, outs[1], outs[2], extra)
        queries, grads = outs[1], outs[2]
    score_a, grad_a, score_b, grad_b, key_sum, value_sum, todo = rest[:7]
    sums = rest[7] if stage == 2 else outs[-1]
    pieces = queries.shape[0]
    scores, prob_grads = (score_a, score_b), (grad_a, grad_b)
    sums[...] = sum_in[...] if stage else jnp.zeros(sums.shape, f32)
    if stage == 1:
        outs[0][:2] = kept[...]
    if stage == 2:
        outs[0][2:, : 2 * HEAD, :] = kept[...]
    ready()

    def attend(i, carry):
        at = todo_ref[i]
        seg = seg_ref[at]
        count = collect(at + 1, pieces, lambda q: (need_ref[q] & seg) != 0, todo)
        key, value, key_lane = keys[at], values[at], key_lanes[at]
        score_a[...] = causal(dot(key, queries[at], 1, 0))
        grad_a[...] = dot(value, grads[at], 1, 0)
        key_sum[...] = jnp.zeros(key_sum.shape, f32)
        value_sum[...] = jnp.zeros(value_sum.shape, f32)

        def fill(slot, query_at):
            scores[slot][...] = dot(key, queries[query_at], 1, 0)
            prob_grads[slot][...] = dot(value, grads[query_at], 1, 0)

        def work(slot, query_at):
            probs = jnp.exp2(scores[slot][...])
            score_grad = (probs * prob_grads[slot][...]).astype(bf16)
            value_sum[...] += dot(grads[query_at, :HEAD, :], probs.astype(bf16), 1, 1)
            key_sum[...] += dot(queries[query_at, :HEAD, :], score_grad, 1, 1)
            sums[query_at] += dot(key_lane, score_grad, 1, 0)

        two_ahead(count, todo, at, fill, work)
        key_grad = unrotate(key_sum[...] * (1.0 / LOG2E), cos_ref[at], sin_ref[at]).astype(bf16)
        value_grad = (0.5 * value_sum[...]).astype(bf16)

        def write(ref, place):
            ref[place, :HEAD, :] = key_grad
            ref[place, HEAD : 2 * HEAD, :] = value_grad

        if stage == 1:
            pl.when(i < 2)(lambda: write(outs[0], 2 + i))
            pl.when(i >= 2)(lambda: write(outs[1], i - 2))
        else:
            write(outs[0], i)
        return carry

    lax.fori_loop(0, todo_count, attend, 0)
    if stage == 2:
        for p in range(pieces):
            grad = unrotate(sums[p] * SCORE_SCALE, cos_ref[p], sin_ref[p]).astype(bf16)
            start = pl.multiple_of((2 + ((p % 2) ^ place_ref[0])) * HEAD, HEAD)
            outs[0][p // 2, pl.ds(start, HEAD), :] = grad


def bwd_call(stage, todo, place, seg, need, cosine, sine, keys, key_lanes, values, queries, more, extra):
    count, (pieces, _, piece) = todo.shape[0], queries.shape
    places = pieces // 2
    sums = shape_of(pieces, HEAD, piece, dtype=f32)
    outs = (
        (shape_of(2, 2 * HEAD, piece), shape_of(*queries.shape), shape_of(*queries.shape), sums),
        (shape_of(places, 2 * HEAD, piece), shape_of(2, 2 * HEAD, piece), sums),
        (shape_of(places, 4 * HEAD, piece),),
    )[stage]
    operands = (cosine, sine, keys, key_lanes, values, queries, *more)
    got = call(
        functools.partial(bwd_kernel, stage=stage, todo_count=count, extra=extra), "attend_back", outs,
        (todo, place, seg, need, *operands),
        scratch=[pltpu.VMEM((piece, piece), f32)] * 4
        + [pltpu.VMEM((HEAD, piece), f32)] * 2
        + [pltpu.SMEM((pieces,), jnp.int32)]
        + ([pltpu.VMEM(sums.shape, f32)] if stage == 2 else []),
        scalars=4, mib=36, late=(0, 1),
    )
    return got[0] if stage == 2 else got


def after(value, *earlier):
    return lax.optimization_barrier((value,) + earlier)[0]


def on_device(
    tokens, first_values, cotangent, parents, seg_lengths,
    w_query, w_key, w_value, w_out, w_gate, w_up, w_down, gain_attn, gain_ffn,
):
    assert tokens.shape[1] == 1
    fsdp_count, ctx_count, tp_count = (lax.axis_size(a) for a in ("fsdp", "ctx", "tp"))
    assert tp_count == 4 and ctx_count == 4
    fsdp_at, ctx_at, tp_at = (lax.axis_index(a) for a in ("fsdp", "ctx", "tp"))
    core_at, x_at = tp_at % 2, tp_at // 2
    own_rows, width = tokens.shape[0], tokens.shape[2]
    chip_rows = 2 * own_rows
    heads = w_query.shape[1] // HEAD
    head_width = heads * HEAD
    assert heads == ctx_count
    tree_len = own_rows * tp_count * ctx_count
    weight_rows, hidden = w_query.shape[0], w_gate.shape[1]
    two = fsdp_count == 2

    def over_core(value):
        return lax.ppermute(value, "tp", [(i, i ^ 1) for i in range(tp_count)])

    def over_x(value):
        return lax.ppermute(value, "tp", [(i, i ^ 2) for i in range(tp_count)])

    def over_fsdp(value):
        return lax.ppermute(value, "fsdp", [(0, 1), (1, 0)])

    def over_ctx(value, flip):
        return lax.ppermute(value, "ctx", [(i, i ^ flip) for i in range(ctx_count)])

    def exchange(by_place):
        return lax.all_to_all(by_place, "ctx", 0, 0, tiled=True)

    def relative(rows):
        if not two:
            return rows
        swapped = jnp.concatenate([rows[..., weight_rows:], rows[..., :weight_rows]], axis=-1)
        return jnp.where(fsdp_at == 0, rows, swapped)

    def by_x(near, far):
        return jnp.where(x_at == 0, jnp.concatenate([near, far], axis=0), jnp.concatenate([far, near], axis=0))

    def fsdp_sum(parts, axis=0):
        if not two:
            return lax.psum_scatter(parts[0], "fsdp", scatter_dimension=axis, tiled=True)
        return parts[0], over_fsdp(parts[1])

    def inward(low):
        return low, lax.ppermute(low, "ctx", [(0, 1), (3, 2)])

    def across(low):
        return low, lax.ppermute(low, "ctx", [(1, 2), (2, 1)])

    def outward(low):
        return low, lax.ppermute(low, "ctx", [(1, 0), (2, 3)])

    def join(pair):
        return (pair[0].astype(f32) + pair[1].astype(f32)).astype(bf16)

    def finish(pair):
        return jnp.where((ctx_at == 0) | (ctx_at == 3), pair[1], pair[0]).astype(f32)

    def hold(pair, *earlier):
        return (pair[0], after(pair[1], *earlier)) if isinstance(pair, tuple) else after(pair, *earlier)

    def step(*pairs):
        if not two:
            return [join(pair) if isinstance(pair, tuple) else pair for pair in pairs]
        return join_call(*pairs)

    three = (w_query, w_key, w_value)
    own_tokens, early_gains = tokens[:, 0, :], jnp.stack([gain_attn, gain_ffn])
    if two:
        own_three = stack_call(*three)
        qkv_weight = [own_three, over_fsdp(own_three)]
        own_tokens, early_gains = after(own_tokens, own_three), after(early_gains, own_three)
        gains = jnp.concatenate([early_gains, over_fsdp(early_gains)], axis=1)
    else:
        qkv_weight = [stack_call(*(lax.all_gather(w, "fsdp", axis=0, tiled=True) for w in three))]
        gains = lax.all_gather(early_gains, "fsdp", axis=1, tiled=True)
    token_x = over_x(own_tokens)
    token_core = over_core(own_tokens)
    attention_gain = gains[0].reshape(1, width).astype(f32)
    ffn_gain = gains[1].reshape(1, width).astype(f32)
    count = len(qkv_weight)

    place = jnp.stack([x_at, core_at, ctx_at, fsdp_at]).astype(jnp.int32)
    position, query_extra, key_extra, seg_bits, need_bits = layout_call(parents, seg_lengths, tree_len, chip_rows)
    frequency = jnp.exp(-math.log(10000.0) * jnp.arange(HALF, dtype=f32) / HALF)
    angles = frequency[None, :, None] * position
    cosine, sine = jnp.cos(angles), jnp.sin(angles)

    def normalize(rows_f32):
        return lax.rsqrt(jnp.mean(rows_f32 * rows_f32, axis=-1, keepdims=True) + epsilon)

    first_flat = first_values[:, 0, :]

    def spread(pieces):
        return [over_ctx(piece, flip) if flip else piece for flip, piece in enumerate(pieces)]

    by_head, near_normed, far_normed = project_call(
        place, (own_tokens, token_core, token_x, over_core(token_x)), attention_gain, cosine, sine, first_flat, qkv_weight, two
    )
    got = exchange(by_head)
    others = (w_gate, w_up, w_down, w_out)
    if two:
        feed_own = stack_call(*(after(w.T, by_head) for w in others))
        feed_weight = [feed_own, over_fsdp(feed_own)]
    else:
        feed_weight = [stack_call(*(lax.all_gather(w, "fsdp", axis=0, tiled=True).T for w in others))]
    own_cot = relative(after(cotangent[:, 0, :], by_head))
    half_places = jnp.arange(ctx_count, dtype=jnp.int32) * 2
    far_out, far_full, far_lse, keys, key_lanes, value_lanes, values, queries = fwd_call(
        after(half_places + (1 - x_at), own_cot), place, seg_bits, need_bits, (got, query_extra, key_extra), True
    )
    cot_x = over_x(after(own_cot, got))
    out_weight = pick_call([after(w, far_out) for w in feed_weight], head_width)
    out_weight_x = over_x(out_weight)
    cot_core = over_core(after(own_cot, got))
    cot_x_core = over_core(cot_x)

    near_out, near_full, near_lse = fwd_call(
        after(half_places + x_at, far_out, out_weight, cot_x), place, seg_bits, need_bits, (keys, value_lanes, queries)
    )
    far_mixed = after(exchange(far_out), near_out).reshape(head_width, chip_rows)
    far_mixed_got = over_x(far_mixed)
    near_mixed = exchange(after(near_out, far_mixed)).reshape(head_width, chip_rows)

    mine, other = output_call(place, near_mixed, far_mixed_got, out_weight, out_weight_x)
    own_single = relative(own_tokens).astype(f32)
    middle = own_single + mine + over_core(other).astype(f32)

    middle_scale = normalize(middle)
    ffn_own = (middle * middle_scale * ffn_gain).astype(bf16)
    ffn_x = over_x(ffn_own)
    ffn_core = over_core(ffn_own)
    near_hidden, near_gate, near_up, near_mine, near_sent = feed_call(
        ffn_own, ffn_core, own_cot, cot_core, feed_weight, hidden
    )
    ffn_x = after(ffn_x, near_mine)
    ffn_x_core = over_core(ffn_x)
    far_hidden, far_gate, far_up, far_mine, far_sent = feed_call(
        ffn_x, ffn_x_core, cot_x, cot_x_core, feed_weight, hidden
    )
    far_sum = (far_mine + over_core(far_sent).astype(f32)).astype(bf16)
    far_sum_got = over_x(far_sum)
    near_sum = near_mine + over_core(near_sent).astype(f32)

    all_cot = (after(own_cot, far_sum), cot_core, cot_x, cot_x_core)
    all_ffn = (after(ffn_own, far_sum), ffn_core, ffn_x, ffn_x_core)
    first_parts, second_parts = feed_grads_call(
        (near_gate, far_gate, near_up, far_up), (near_hidden, far_hidden), all_ffn, all_cot, count
    )
    first_sum = fsdp_sum(first_parts, 1)
    second_sum = fsdp_sum(second_parts, 1)
    ffn_grad = near_sum + after(far_sum_got, first_parts[0]).astype(f32)

    weighted = ffn_grad * ffn_gain
    middle_grad = (
        own_cot.astype(f32)
        + middle_scale * weighted
        - middle * (middle_scale**3 * jnp.mean(weighted * middle, axis=-1, keepdims=True))
    )
    middle_low = middle_grad.astype(bf16)
    near_heads, far_heads, chip_low = heads_call(place, middle_low, over_core(middle_low), out_weight, out_weight_x)
    far_out_grad = over_x(far_heads)
    near_grads = exchange(near_heads.reshape(heads, HEAD, chip_rows))
    far_grads = exchange(after(far_out_grad, near_grads).reshape(heads, HEAD, chip_rows))

    ffn_gain_part = jnp.sum(after(ffn_grad, near_heads) * middle * middle_scale, axis=0)
    low_x = over_x(after(middle_low, far_out_grad))
    low_x_core = over_core(low_x)
    near_result, far_result, sent = result_call(after(near_hidden, near_heads), far_hidden, feed_weight)
    sent_got = over_core(sent)
    (first_low,) = step(hold(first_sum, far_grads, sent))
    first_in = inward(first_low)
    def back(stage, places, more, *earlier):
        return bwd_call(
            stage, after(jnp.stack(places).astype(jnp.int32), *earlier), place, seg_bits, need_bits, cosine, sine,
            keys, key_lanes, values, more[0], more[1:], query_extra.shape[1],
        )

    far_at, near_at = [2 * i + 1 - x_at for i in range(4)], [2 * i + x_at for i in range(4)]
    first_kv, back_queries, grads, query_sum = back(
        0, far_at[:2], (queries, near_grads, far_grads, near_full, far_full, near_lse, far_lse), first_low
    )

    first_low, second_low = step(hold(first_in, first_kv), hold(second_sum, first_kv))
    first_across, second_in = across(first_low), inward(second_low)
    far_kv, near_kv, query_sum = back(
        1, far_at[2:] + near_at[2:], (back_queries, grads, first_kv, query_sum), first_low
    )

    first_low, second_low = step(hold(first_across, far_kv), hold(second_in, far_kv))
    first_done, second_across = outward(first_low), across(second_low)
    far_kv_got = exchange(after(far_kv, first_low))
    last = back(2, near_at[:2], (back_queries, grads, near_kv, query_sum), first_low)

    (second_low,) = step(hold(second_across, last))
    second_done = outward(second_low)
    last_got = exchange(after(last, second_low, first_done[1]))
    far_kv_got = after(far_kv_got, last)
    out_parts = out_grads_call(after(place, last), chip_low, low_x, low_x_core, near_mixed, far_mixed, count)
    out_sum = fsdp_sum(out_parts)
    far_result_got = over_x((after(far_result, out_parts[0]) + sent_got[1].astype(f32)).astype(bf16))
    second_all = finish(hold(second_done, out_parts[0]))
    layer_out = relative((after(middle, second_all) + near_result + sent_got[0].astype(f32) + far_result_got.astype(f32)).astype(bf16))
    first_all = finish(hold(first_done, second_low))
    (out_low,) = step(hold(out_sum, layer_out))
    last_got = after(last_got, first_all, out_low)
    out_in = inward(out_low)

    qkv_parts = weights_call(near_normed, far_normed, far_kv_got, last_got, count)
    qkv_sum = fsdp_sum(qkv_parts)
    near_mine, near_other, far_mine, far_other, gain_part, grad_values = rows_call(
        after(place, qkv_parts[0]), near_normed, far_normed, far_kv_got, last_got, qkv_weight
    )
    far_rows_got = over_x((far_mine + over_core(far_other).astype(f32)).astype(bf16))
    near_rows_got = over_core(near_other)
    gain_sum = jnp.concatenate([gain_part / attention_gain, ffn_gain_part[None]], axis=0)

    def light(*pairs):
        return [join(pair) if isinstance(pair, tuple) else pair for pair in pairs]

    qkv_low, out_low = light(hold(qkv_sum, near_mine), hold(out_in, near_mine))
    qkv_in, out_across = inward(qkv_low), across(out_low)
    if two:
        gain_sum = after(gain_sum, qkv_low)
        gain_sum = gain_sum + over_core(gain_sum)
        gain_sum = gain_sum + over_x(gain_sum)
        gain_sum = gain_sum[:, :weight_rows] + over_fsdp(gain_sum[:, weight_rows:])
    qkv_low, out_low = light(hold(qkv_in, gain_sum, far_rows_got), hold(out_across, gain_sum))
    lows = [qkv_low]
    qkv_across, out_done = across(qkv_low), outward(out_low)
    if two:
        gain_sum = after(gain_sum, qkv_low)
        gain_sum = gain_sum + over_ctx(gain_sum, 1)
    (qkv_low,) = light(hold(qkv_across, gain_sum, out_done[1]))
    if two:
        gain_sum = gain_sum + over_ctx(after(gain_sum, qkv_low), 2)
    else:
        gain_sum = lax.psum(gain_sum, ("fsdp", "ctx", "tp"))
        gain_sum = lax.dynamic_slice_in_dim(gain_sum, fsdp_at * weight_rows, weight_rows, 1)
    grad_query, grad_key, grad_value = jnp.split(finish(hold(outward(qkv_low), gain_sum)), 3)
    grad_out = finish(out_done)
    grad_gate, grad_up, grad_down = first_all[:hidden].T, first_all[hidden:].T, second_all.T

    normed_grad = after(near_mine, lows[0]) + near_rows_got.astype(f32) + far_rows_got.astype(f32)
    scale = normalize(own_single)
    weighted = normed_grad * attention_gain
    grad_tokens = (
        middle_grad + scale * weighted - own_single * (scale**3 * jnp.mean(weighted * own_single, axis=-1, keepdims=True))
    )
    return (
        layer_out[:, None, :],
        relative(grad_tokens)[:, None, :],
        grad_values.reshape(4 * own_rows, 1, head_width),
        grad_query,
        grad_key,
        grad_value,
        grad_out,
        grad_gate,
        grad_up,
        grad_down,
        gain_sum[0],
        gain_sum[1],
    )

def solution(mesh):
    rows, columns = P(("ctx", "tp"), "fsdp", None), P("ctx", "fsdp", "tp")
    weight, gain = P("fsdp", "tp"), P("fsdp")
    return jax.shard_map(
        on_device,
        mesh=mesh,
        in_specs=(rows, columns, rows, P("fsdp", None), P("fsdp", None)) + (weight,) * 7 + (gain,) * 2,
        out_specs=(rows, rows, columns) + (weight,) * 7 + (gain,) * 2,
        check_vma=False,
    )
```

```python
import functools
import math

import jax
import jax.numpy as jnp
from jax import lax
from jax.experimental import pallas as pl
from jax.experimental.pallas import tpu as pltpu
from jax.sharding import PartitionSpec as P

HEAD = 64
HALF = HEAD // 2
BIG = 1e30
LOG2E = 1.4426950408889634
SCORE_SCALE = HEAD**-0.5
QUERY_SCALE = SCORE_SCALE * LOG2E
epsilon = 1e-05
f32 = jnp.float32
bf16 = jnp.bfloat16


def dot(a, b, ca, cb):
    return lax.dot_general(a, b, (((ca,), (cb,)), ((), ())), preferred_element_type=f32)


def layout_kernel(par_ref, len_ref, pos_ref, qx_ref, kx_ref, seg_ref, need_ref, anc_sc, above_sc, *, segs, tokens, piece):
    token = lax.broadcasted_iota(jnp.int32, (1, tokens), 1)
    pos = jnp.zeros((1, tokens), jnp.int32)
    seg_of = jnp.full((1, tokens), -1, jnp.int32)
    bits = jnp.zeros((1, tokens), jnp.int32)
    for b in range(tokens // piece):
        seg_ref[b] = 0
        need_ref[b] = 0
    off = jnp.int32(0)
    for s in range(segs):
        length = len_ref[0, s]
        if s == 0:
            anc, above = jnp.int32(1), jnp.int32(0)
        else:
            parent = par_ref[0, s]
            anc = anc_sc[parent] | jnp.int32(1 << s)
            above = above_sc[parent] + len_ref[0, parent]
        anc_sc[s] = anc
        above_sc[s] = above
        started = token >= off
        seg_of = jnp.where(started, s, seg_of)
        pos = jnp.where(started, token - off + above, pos)
        bits = jnp.where(started, anc, bits)

        def mark(b, carry, anc=anc, s=s):
            seg_ref[b] = seg_ref[b] | jnp.int32(1 << s)
            need_ref[b] = need_ref[b] | anc
            return carry

        lax.fori_loop(off // piece, (off + length - 1) // piece + 1, mark, 0)
        off = off + length
    row = lax.broadcasted_iota(jnp.int32, (kx_ref.shape[1], tokens), 0)
    key_extra = jnp.where(row == seg_of, -BIG, 0.0).astype(bf16)
    linked = lax.shift_right_logical(jnp.broadcast_to(bits, row.shape), row) & 1
    query_extra = jnp.where(linked == 1, 0.0, 1.0).astype(bf16)
    for p in range(tokens // piece):
        lanes = slice(p * piece, (p + 1) * piece)
        pos_ref[p] = pos[:, lanes].astype(f32)
        kx_ref[p] = key_extra[:, lanes]
        qx_ref[p] = query_extra[:, lanes]


SMEM = pl.BlockSpec(memory_space=pltpu.SMEM)
VMEM = pl.BlockSpec(memory_space=pltpu.VMEM)


def layout_call(parents, lengths, tokens, piece):
    segs = parents.shape[-1]
    rows = -(-segs // 16) * 16
    return pl.pallas_call(
        functools.partial(layout_kernel, segs=segs, tokens=tokens, piece=piece),
        out_shape=(
            jax.ShapeDtypeStruct((tokens // piece, 1, piece), f32),
            jax.ShapeDtypeStruct((tokens // piece, rows, piece), bf16),
            jax.ShapeDtypeStruct((tokens // piece, rows, piece), bf16),
            jax.ShapeDtypeStruct((tokens // piece,), jnp.int32),
            jax.ShapeDtypeStruct((tokens // piece,), jnp.int32),
        ),
        in_specs=[SMEM, SMEM],
        out_specs=(VMEM, VMEM, VMEM, SMEM, SMEM),
        scratch_shapes=[pltpu.SMEM((segs,), jnp.int32), pltpu.SMEM((segs,), jnp.int32)],
        cost_estimate=pl.CostEstimate(flops=0, bytes_accessed=1 << 16, transcendentals=0),
        name="layout",
    )(parents, lengths)


def causal(scores):
    key_at = lax.broadcasted_iota(jnp.int32, scores.shape, 0)
    query_at = lax.broadcasted_iota(jnp.int32, scores.shape, 1)
    return jnp.where(key_at <= query_at, scores, -BIG)


def three_parts(row):
    at = lax.broadcasted_iota(jnp.int32, (16, row.shape[1]), 0)
    high = row.astype(bf16).astype(f32)
    rest = row - high
    mid = rest.astype(bf16).astype(f32)
    low = rest - mid
    return jnp.where(at == 0, high, jnp.where(at == 1, mid, jnp.where(at == 2, low, 0.0))).astype(bf16)


def unrotate(values, cosine, sine):
    a, b = values[:HALF], values[HALF:]
    return jnp.concatenate([a * cosine + b * sine, b * cosine - a * sine], axis=0)


def prep_kernel(place_ref, qx_ref, kx_ref, got_ref, keys, key_lanes, value_lanes, values, queries):
    piece = got_ref.shape[2] // 2
    extra = qx_ref.shape[1]
    minus = jnp.full((16, piece), -1.0, bf16)
    pad_key = jnp.zeros((128 - HEAD - extra - 16, piece), bf16)
    pad_value = jnp.zeros((128 - HEAD - 16, piece), bf16)
    for half in (0, 1):
        for p in range(got_ref.shape[0]):
            at = 2 * p + (place_ref[0] ^ half)
            got = got_ref[p, :, half * piece : (half + 1) * piece]
            query, key, value = got[:HEAD, :], got[HEAD : 2 * HEAD, :], got[2 * HEAD :, :]
            key_lanes[at] = key
            keys[at] = jnp.concatenate([key, kx_ref[at], minus, pad_key], axis=0).T
            value_lanes[at] = jnp.concatenate([value, -minus], axis=0)
            values[at] = jnp.concatenate([value, minus, pad_value], axis=0).T
            queries[at] = jnp.concatenate([query, qx_ref[at], jnp.zeros((128 - HEAD - extra, piece), bf16)], axis=0)


def shape_of(*sizes, dtype=bf16):
    return jax.ShapeDtypeStruct(sizes, dtype)


def call(kernel, name, out_shape, operands, scratch=(), scalars=1, mib=20, late=()):
    outs = out_shape if isinstance(out_shape, tuple) else (out_shape,)
    arrays = operands[scalars:]
    count, total = len(arrays), len(arrays) + len(outs)

    def body(*refs):
        first, rest = refs[:scalars], refs[scalars:]
        outside, inside, sems, rest = rest[:total], rest[total : 2 * total], rest[2 * total], rest[2 * total + 1 :]
        copies = [pltpu.make_async_copy(outside[i], inside[i], sems.at[i]) for i in range(count)]
        for copy in copies:
            copy.start()
        for i in range(count):
            if i not in late:
                copies[i].wait()
        more = {"ready": lambda: [copies[i].wait() for i in late]} if late else {}
        kernel(*first, *inside, *rest, **more)
        copies = [pltpu.make_async_copy(inside[i], outside[i], sems.at[i]) for i in range(count, total)]
        for copy in copies:
            copy.start()
        for copy in copies:
            copy.wait()

    got = pl.pallas_call(
        body,
        out_shape=outs,
        in_specs=[SMEM] * scalars + [pl.BlockSpec(memory_space=pltpu.HBM)] * count,
        out_specs=(pl.BlockSpec(memory_space=pltpu.HBM),) * len(outs),
        scratch_shapes=[pltpu.VMEM(x.shape, x.dtype) for x in (*arrays, *outs)]
        + [pltpu.SemaphoreType.DMA((total,))]
        + list(scratch),
        compiler_params=pltpu.CompilerParams(vmem_limit_bytes=60 << 20),
        cost_estimate=pl.CostEstimate(flops=0, bytes_accessed=1 << 16, transcendentals=0),
        name=name,
    )(*operands)
    return got if isinstance(out_shape, tuple) else got[0]


def cut(ref, count):
    size = ref.shape[1] // count
    return [ref[:, i * size : (i + 1) * size] for i in range(count)]


def project_kernel(place_ref, near_own, near_other, far_own, far_other, gain_ref, cos_ref, sin_ref, first_ref, *rest, count, swap):
    weights, (out, near_out, far_out, raw) = rest[:count], rest[count:]
    heads_width = raw.shape[0] // 3
    size, width = near_own.shape
    block = width // count
    for refs, normed in (((near_own, near_other), near_out), ((far_own, far_other), far_out)):
        for half, ref in enumerate(refs):
            single = ref[...].astype(f32)
            scale = lax.rsqrt(jnp.mean(single * single, axis=-1, keepdims=True) + epsilon)
            if swap:
                turned = jnp.concatenate([single[:, block:], single[:, :block]], axis=1)
                single = jnp.where(place_ref[3] == 0, single, turned)
            at = pl.multiple_of((place_ref[1] ^ half) * size, size)
            normed[pl.ds(at, size), :] = (single * scale * gain_ref[...]).astype(bf16)
    piece = 2 * size
    turned = [[w[i * block : (i + 1) * block, :].T for w in weights] for i in range(3)]
    for half, rows_ref in enumerate((near_out, far_out)):
        rows = cut(rows_ref, count)
        for i in range(3):
            raw[i * heads_width : (i + 1) * heads_width, :] = sum(dot(w, r, 1, 1) for w, r in zip(turned[i], rows))
        x_half = place_ref[0] ^ half
        at = 2 * place_ref[2] + x_half
        cosine, sine = cos_ref[at], sin_ref[at]
        start = pl.multiple_of(x_half * piece, piece)
        first = first_ref[pl.ds(start, piece), :].astype(f32).T

        def turn(values):
            a, b = values[:HALF], values[HALF:]
            return jnp.concatenate([a * cosine - b * sine, b * cosine + a * sine], axis=0)

        lanes = slice(half * piece, (half + 1) * piece)
        for at in range(heads_width // HEAD):
            rows_at = [slice(i * heads_width + at * HEAD, i * heads_width + (at + 1) * HEAD) for i in range(3)]
            value = 0.5 * raw[rows_at[2], :] + 0.5 * first[at * HEAD : (at + 1) * HEAD]
            out[at, :HEAD, lanes] = (turn(raw[rows_at[0], :]) * QUERY_SCALE).astype(bf16)
            out[at, HEAD : 2 * HEAD, lanes] = turn(raw[rows_at[1], :]).astype(bf16)
            out[at, 2 * HEAD :, lanes] = value.astype(bf16)


def project_call(place, rows, gain, cosine, sine, first, weights, swap):
    (size, width), columns = rows[0].shape, weights[0].shape[1]
    return call(
        functools.partial(project_kernel, count=len(weights), swap=swap), "project",
        (shape_of(columns // HEAD, 3 * HEAD, 4 * size), shape_of(2 * size, width), shape_of(2 * size, width)),
        (place, *rows, gain, cosine, sine, first, *weights),
        scratch=[pltpu.VMEM((3 * columns, 2 * size), f32)],
    )


def stack_kernel(*refs):
    out, at = refs[-1], 0
    for ref in refs[:-1]:
        rows = ref.shape[0]
        out[at : at + rows, :] = ref[...]
        at += rows


def pick_kernel(*refs):
    out = refs[-1]
    rows = out.shape[0]
    size = out.shape[1] // (len(refs) - 1)
    for i, ref in enumerate(refs[:-1]):
        out[:, i * size : (i + 1) * size] = ref[ref.shape[0] - rows :, :]


def pick_call(blocks, rows):
    return call(pick_kernel, "pick", shape_of(rows, blocks[0].shape[1] * len(blocks)), tuple(blocks), scalars=0)


def stack_call(*arrays):
    rows = sum(a.shape[0] for a in arrays)
    return call(stack_kernel, "stack", shape_of(rows, arrays[0].shape[1]), arrays, scalars=0, mib=16)


def split_core(place_ref, total, mine_ref, other_ref):
    rows = mine_ref.shape[0]
    mine_ref[...] = total[pl.ds(pl.multiple_of(place_ref[1] * rows, rows), rows), :]
    other_ref[...] = total[pl.ds(pl.multiple_of((1 - place_ref[1]) * rows, rows), rows), :].astype(bf16)


def output_kernel(place_ref, near_ref, far_ref, *rest):
    near_weight, far_weight, mine_ref, other_ref, total = rest
    total[...] = dot(near_ref[...].T, near_weight[...], 1, 0) + dot(far_ref[...].T, far_weight[...], 1, 0)
    split_core(place_ref, total, mine_ref, other_ref)


def output_call(place, near, far, near_weight, far_weight):
    rows, width = near.shape[1], near_weight.shape[1]
    return call(
        output_kernel, "out_project",
        (shape_of(rows // 2, width, dtype=f32), shape_of(rows // 2, width)),
        (place, near, far, near_weight, far_weight),
        scratch=[pltpu.VMEM((rows, width), f32)],
    )


def heads_kernel(place_ref, own_ref, other_ref, near_weight, far_weight, near_out, far_out, chip):
    rows = own_ref.shape[0]
    for half, ref in enumerate((own_ref, other_ref)):
        chip[pl.ds(pl.multiple_of((place_ref[1] ^ half) * rows, rows), rows), :] = ref[...]
    far_out[...] = dot(far_weight[...], chip[...], 1, 1).astype(bf16)
    near_out[...] = dot(near_weight[...], chip[...], 1, 1).astype(bf16)


def heads_call(place, own, other, near_weight, far_weight):
    rows, columns = 2 * own.shape[0], near_weight.shape[0]
    return call(
        heads_kernel, "out_back",
        (shape_of(columns, rows), shape_of(columns, rows), shape_of(rows, own.shape[1])),
        (place, own, other, near_weight, far_weight),
    )


def feed_kernel(rows_ref, other_ref, cot_ref, cot_other_ref, *rest, count):
    hidden = rest[count].shape[2]
    gate_w, up_w, down_w = ([w.at[i * hidden : (i + 1) * hidden] for w in rest[:count]] for i in range(3))
    hidden_ref, gate_ref, up_ref, mine_ref, sent_ref, rows_sc, cot_sc, back_sc = rest[count:]
    size = rows_ref.shape[0]
    rows_sc[0], rows_sc[1] = rows_ref[...], other_ref[...]
    cot_sc[0], cot_sc[1] = cot_ref[...], cot_other_ref[...]
    block = rows_ref.shape[1] // count

    def step(at, carry):
        lanes = [slice(i * block, (i + 1) * block) for i in range(count)]
        rows, cots = [rows_sc[at, :, s] for s in lanes], [cot_sc[at, :, s] for s in lanes]
        gate = sum(dot(r, w[...], 1, 1) for r, w in zip(rows, gate_w))
        up = sum(dot(r, w[...], 1, 1) for r, w in zip(rows, up_w))
        hidden_grad = sum(dot(r, w[...], 1, 1) for r, w in zip(cots, down_w))
        sig = 1.0 / (1.0 + jnp.exp(-gate))
        act = gate * sig
        hidden_ref[at] = (act * up).astype(bf16)
        gate_grad = (hidden_grad * up * (sig * (1.0 + gate * (1.0 - sig)))).astype(bf16)
        up_grad = (hidden_grad * act).astype(bf16)
        gate_ref[at] = gate_grad
        up_ref[at] = up_grad
        for i in range(count):
            back_sc[at, :, lanes[i]] = dot(gate_grad, gate_w[i][...], 1, 0) + dot(up_grad, up_w[i][...], 1, 0)
        return carry

    lax.fori_loop(0, 2, step, 0)
    mine_ref[...] = back_sc[0]
    sent_ref[...] = back_sc[1].astype(bf16)


def feed_call(rows, other, cot, cot_other, weights, hidden):
    size, width = rows.shape
    count = len(weights)
    return call(
        functools.partial(feed_kernel, count=count), "feed",
        (shape_of(2, size, hidden),) * 3 + (shape_of(size, width, dtype=f32), shape_of(size, width)),
        (rows, other, cot, cot_other, *weights),
        scratch=[pltpu.VMEM((2, size, width), bf16)] * 2 + [pltpu.VMEM((2, size, width), f32)],
        scalars=0, mib=40,
    )


def prep_back(place_ref, queries, near_grad, far_grad, near_full, far_full, near_lse, far_lse, queries_out, grads_out, extra):
    places, _, piece = near_grad.shape
    queries_out[...] = queries[...]
    pad = jnp.zeros((128 - HEAD - 16, piece), bf16)
    for half, (grad, full, lse) in enumerate(((near_grad, near_full, near_lse), (far_grad, far_full, far_lse))):
        for p in range(places):
            at = 2 * p + (place_ref[0] ^ half)
            queries_out[at, HEAD + extra : HEAD + extra + 16, :] = lse[p]
            delta = jnp.sum(grad[p].astype(f32) * full[p], axis=0, keepdims=True)
            grads_out[at] = jnp.concatenate([grad[p], three_parts(delta), pad], axis=0)


def by_projection(got):
    columns = got.shape[0] * HEAD
    flat = lambda at: got[:, at * HEAD : (at + 1) * HEAD, :].reshape(columns, got.shape[2])
    return (flat(2), flat(0), flat(1)), (flat(3), flat(4), flat(5))


def weights_kernel(near_rows, far_rows, last, *rest):
    count = len(rest) // 2
    out_parts, parts = rest[:count], rest[count:]
    size = near_rows.shape[1] // count
    for part, out_part in zip(parts, out_parts):
        part[3 * size :, :] = out_part[...]
    near, far = by_projection(last)
    for i in range(3):
        for b, part in enumerate(parts):
            lanes = slice(b * size, (b + 1) * size)
            sums = dot(near[i], near_rows[:, lanes], 1, 0) + dot(far[i], far_rows[:, lanes], 1, 0)
            part[i * size : (i + 1) * size, :] = sums.T.astype(bf16)


def weights_call(near_rows, far_rows, last, out_parts):
    width, columns, count = near_rows.shape[1], last.shape[0] * HEAD, len(out_parts)
    return call(
        weights_kernel, "weight_grads", tuple(shape_of(4 * width // count, columns) for _ in range(count)),
        (near_rows, far_rows, last, *out_parts), scalars=0,
    )


def rows_kernel(place_ref, near_rows, far_rows, last, *rest, count):
    weights, (near_mine, near_other, far_mine, far_other, gain_ref, value_ref, total) = rest[:count], rest[count:]
    size = near_rows.shape[1] // count
    near, far = by_projection(last)
    for half, grads in enumerate((near, far)):
        value = grads[2].T.astype(f32)
        tokens, columns = value.shape
        folds = columns // 128
        for j in range(folds):
            rows_at = pl.ds((place_ref[0] ^ half) * tokens * folds + j, tokens, stride=folds)
            value_ref[rows_at, :] = value[:, j * 128 : (j + 1) * 128]
    gain_ref[...] = jnp.zeros(gain_ref.shape, f32)
    for grads, rows, mine, other in ((far, far_rows, far_mine, far_other), (near, near_rows, near_mine, near_other)):
        turned = [g.T for g in grads]
        for b in range(count):
            lanes = slice(b * size, (b + 1) * size)
            part = sum(dot(g, weights[b][i * size : (i + 1) * size, :], 1, 1) for i, g in enumerate(turned))
            total[:, lanes] = part
            gain_ref[:, lanes] += jnp.sum(part * rows[:, lanes].astype(f32), axis=0, keepdims=True)
        split_core(place_ref, total, mine, other)


def rows_call(place, near_rows, far_rows, last, weights):
    size, width = near_rows.shape
    rows = (shape_of(size // 2, width, dtype=f32), shape_of(size // 2, width))
    values = shape_of(2 * size * last.shape[0] * HEAD // 128, 128, dtype=f32)
    return call(
        functools.partial(rows_kernel, count=len(weights)), "rows_back",
        rows + rows + (shape_of(1, width, dtype=f32), values),
        (place, near_rows, far_rows, last, *weights),
        scratch=[pltpu.VMEM((size, width), f32)],
    )


def feed_grads_kernel(near_gate, far_gate, near_up, far_up, near_hidden, far_hidden, *refs):
    rows, cots, outs = refs[:4], refs[4:8], refs[8:]
    count = len(outs) // 2
    size = rows[0].shape[1] // count
    hidden = near_gate.shape[2]
    half = hidden // 2
    pairs = ((near_gate, far_gate, rows), (near_up, far_up, rows), (near_hidden, far_hidden, cots))
    for b in range(count):
        lanes = slice(b * size, (b + 1) * size)
        first, second = outs[b], outs[count + b]
        for i, (near, far, right) in enumerate(pairs):
            near, far = (ref[...].reshape(2 * ref.shape[1], hidden) for ref in (near, far))
            near_right, far_right = (jnp.concatenate([right[j][:, lanes], right[j + 1][:, lanes]], axis=0) for j in (0, 2))
            total = (dot(near, near_right, 0, 0) + dot(far, far_right, 0, 0)).astype(bf16)
            if i == 0:
                first[:hidden, :] = total
            elif i == 1:
                first[hidden:, :] = total[:half]
                second[:half, :] = total[half:]
            else:
                second[half:, :] = total


def feed_grads_call(lefts, hiddens, rows, cots, count):
    hidden, size = lefts[0].shape[2], rows[0].shape[1] // count
    outs = call(
        feed_grads_kernel, "feed_grads", tuple(shape_of(3 * hidden // 2, size) for _ in range(2 * count)),
        (*lefts, *hiddens, *rows, *cots), scalars=0, mib=40,
    )
    return outs[:count], outs[count:]


def result_kernel(near_hidden, far_hidden, *rest, count):
    weights, (near_mine, far_mine, sent) = rest[:count], rest[count:]
    size = near_mine.shape[1] // count
    for at, (ref, mine) in enumerate(((near_hidden, near_mine), (far_hidden, far_mine))):
        for i in range(count):
            lanes = slice(i * size, (i + 1) * size)
            weight = weights[i][2 * ref.shape[2] : 3 * ref.shape[2], :]
            mine[:, lanes] = dot(ref[0], weight, 1, 0)
            sent[at, :, lanes] = dot(ref[1], weight, 1, 0).astype(bf16)


def result_call(near_hidden, far_hidden, weights):
    _, size, _ = near_hidden.shape
    count = len(weights)
    width = weights[0].shape[1] * count
    return call(
        functools.partial(result_kernel, count=count), "result",
        (shape_of(size, width, dtype=f32), shape_of(size, width, dtype=f32), shape_of(2, size, width)),
        (near_hidden, far_hidden, *weights), scalars=0, mib=24,
    )


def out_grads_kernel(place_ref, chip_low, far_own, far_other, near_mixed, far_mixed, *rest):
    outs, far_low = rest[:-1], rest[-1]
    count = len(outs)
    rows = far_own.shape[0]
    for half, ref in enumerate((far_own, far_other)):
        far_low[pl.ds(pl.multiple_of((place_ref[1] ^ half) * rows, rows), rows), :] = ref[...]
    near, far = near_mixed[...], far_mixed[...]
    for out, near_rows, far_rows in zip(outs, cut(chip_low, count), cut(far_low, count)):
        out[...] = (dot(near, near_rows, 1, 0) + dot(far, far_rows, 1, 0)).T.astype(bf16)


def out_grads_call(place, chip_low, far_own, far_other, near_mixed, far_mixed, count):
    width, columns = chip_low.shape[1] // count, near_mixed.shape[0]
    return call(
        out_grads_kernel, "out_grads", tuple(shape_of(width, columns) for _ in range(count)),
        (place, chip_low, far_own, far_other, near_mixed, far_mixed),
        scratch=[pltpu.VMEM(chip_low.shape, bf16)],
    )


def join_kernel(*refs):
    count = len(refs) // 3
    for i in range(count):
        a, b, out = refs[2 * i], refs[2 * i + 1], refs[2 * count + i]
        out[...] = (a[...].astype(f32) + b[...].astype(f32)).astype(bf16)


def join_call(*pairs):
    outs = call(
        join_kernel, "join", tuple(shape_of(*a.shape) for a, _ in pairs), [x for pair in pairs for x in pair],
        scalars=0, mib=16,
    )
    return list(outs)


def collect(first, last, hit, todo):
    def step(at, count):
        todo[count] = at
        return count + hit(at).astype(jnp.int32)

    return lax.fori_loop(first, last, step, jnp.int32(0))


def two_ahead(count, todo, first, fill, work):
    def step(j, now):
        middle, after = todo[2 * j], todo[2 * j + 1]
        fill(1, middle)
        work(0, now)
        fill(0, after)
        work(1, middle)
        return after

    last = lax.fori_loop(0, count // 2, step, first)

    @pl.when(lax.rem(count, 2) == 0)
    def _():
        work(0, last)

    @pl.when(lax.rem(count, 2) == 1)
    def _():
        final = todo[count - 1]
        fill(1, final)
        work(0, last)
        work(1, final)


def fwd_kernel(todo_ref, place_ref, seg_ref, need_ref, *refs, first):
    outs, (score_a, score_b, top, total, todo) = refs[:-5], refs[-5:]
    if first:
        got_ref, qx_ref, kx_ref, out_ref, full_ref, lse_ref, keys, key_lanes, values, plain_values, queries = outs
        prep_kernel(place_ref, qx_ref, kx_ref, got_ref, keys, key_lanes, values, plain_values, queries)
    else:
        keys, values, queries, out_ref, full_ref, lse_ref = outs
    scores = (score_a, score_b)

    def attend(i, carry):
        at = todo_ref[i]
        need = need_ref[at]
        count = collect(0, at, lambda k: (seg_ref[k] & need) != 0, todo)
        query = queries[at]
        score_a[...] = causal(dot(keys[at], query, 1, 0))
        top[...] = jnp.full(top.shape, -BIG, f32)
        total[...] = jnp.zeros(total.shape, f32)

        def fill(slot, key_at):
            scores[slot][...] = dot(keys[key_at], query, 1, 0)

        def work(slot, key_at):
            score = scores[slot][...]
            old_top = top[...]
            new_top = jnp.maximum(old_top, jnp.max(score, axis=0, keepdims=True))
            weights = jnp.exp2(score - new_top).astype(bf16)
            total[...] = total[...] * jnp.exp2(old_top - new_top) + dot(values[key_at], weights, 1, 0)
            top[...] = new_top

        two_ahead(count, todo, at, fill, work)
        final = total[...]
        weight_sum = final[HEAD : HEAD + 1, :]
        mixed = final[:HEAD, :] * (1.0 / weight_sum)
        out_ref[i] = mixed.astype(bf16)
        full_ref[i] = mixed
        lse_ref[i] = three_parts(top[...] + jnp.log2(weight_sum))
        return carry

    lax.fori_loop(0, out_ref.shape[0], attend, 0)


def fwd_call(todo, place, seg, need, operands, first=False):
    count = todo.shape[0]
    if first:
        pieces, piece = 2 * operands[0].shape[0], operands[0].shape[2] // 2
        more = (
            shape_of(pieces, piece, 128),
            shape_of(pieces, HEAD, piece),
            shape_of(pieces, HEAD + 16, piece),
            shape_of(pieces, piece, 128),
            shape_of(pieces, 128, piece),
        )
    else:
        (pieces, _, piece), more = operands[2].shape, ()
    return call(
        functools.partial(fwd_kernel, first=first), "attend",
        (shape_of(count, HEAD, piece), shape_of(count, HEAD, piece, dtype=f32), shape_of(count, 16, piece)) + more,
        (todo, place, seg, need, *operands),
        scratch=[pltpu.VMEM((piece, piece), f32)] * 2
        + [pltpu.VMEM((1, piece), f32), pltpu.VMEM((HEAD + 16, piece), f32), pltpu.SMEM((pieces,), jnp.int32)],
        scalars=4,
    )


def bwd_kernel(todo_ref, place_ref, seg_ref, need_ref, cos_ref, sin_ref, keys, key_lanes, values, queries, *rest, stage, todo_count, extra, ready):
    if stage:
        grads, kept, sum_in, rest = rest[0], rest[1], rest[2], rest[3:]
    else:
        before, rest = rest[:6], rest[6:]
    outs, rest = rest[: (4, 1)[stage]], rest[(4, 1)[stage] :]
    if not stage:
        prep_back(place_ref, queries, *before, outs[1], outs[2], extra)
        queries, grads = outs[1], outs[2]
    score_a, grad_a, score_b, grad_b, key_sum, value_sum, todo = rest[:7]
    sums = rest[7] if stage else outs[-1]
    pieces = queries.shape[0]
    scores, prob_grads = (score_a, score_b), (grad_a, grad_b)
    sums[...] = sum_in[...] if stage else jnp.zeros(sums.shape, f32)
    if stage:
        outs[0][:, 4 * HEAD :, :] = kept[...]
    ready()

    def attend(i, carry):
        at = todo_ref[i]
        seg = seg_ref[at]
        count = collect(at + 1, pieces, lambda q: (need_ref[q] & seg) != 0, todo)
        key, value, key_lane = keys[at], values[at], key_lanes[at]
        score_a[...] = causal(dot(key, queries[at], 1, 0))
        grad_a[...] = dot(value, grads[at], 1, 0)
        key_sum[...] = jnp.zeros(key_sum.shape, f32)
        value_sum[...] = jnp.zeros(value_sum.shape, f32)

        def fill(slot, query_at):
            scores[slot][...] = dot(key, queries[query_at], 1, 0)
            prob_grads[slot][...] = dot(value, grads[query_at], 1, 0)

        def work(slot, query_at):
            probs = jnp.exp2(scores[slot][...])
            score_grad = (probs * prob_grads[slot][...]).astype(bf16)
            value_sum[...] += dot(grads[query_at, :HEAD, :], probs.astype(bf16), 1, 1)
            key_sum[...] += dot(queries[query_at, :HEAD, :], score_grad, 1, 1)
            sums[query_at] += dot(key_lane, score_grad, 1, 0)

        two_ahead(count, todo, at, fill, work)
        key_grad = unrotate(key_sum[...] * (1.0 / LOG2E), cos_ref[at], sin_ref[at]).astype(bf16)
        value_grad = (0.5 * value_sum[...]).astype(bf16)

        outs[0][i, :HEAD, :] = key_grad
        outs[0][i, HEAD : 2 * HEAD, :] = value_grad
        return carry

    lax.fori_loop(0, todo_count, attend, 0)
    if stage:
        for p in range(pieces):
            grad = unrotate(sums[p] * SCORE_SCALE, cos_ref[p], sin_ref[p]).astype(bf16)
            start = pl.multiple_of((2 + ((p % 2) ^ place_ref[0])) * HEAD, HEAD)
            outs[0][p // 2, pl.ds(start, HEAD), :] = grad


def bwd_call(stage, todo, place, seg, need, cosine, sine, keys, key_lanes, values, queries, more, extra):
    count, (pieces, _, piece) = todo.shape[0], queries.shape
    places = pieces // 2
    sums = shape_of(pieces, HEAD, piece, dtype=f32)
    outs = (
        (shape_of(places, 2 * HEAD, piece), shape_of(*queries.shape), shape_of(*queries.shape), sums),
        (shape_of(places, 6 * HEAD, piece),),
    )[stage]
    operands = (cosine, sine, keys, key_lanes, values, queries, *more)
    got = call(
        functools.partial(bwd_kernel, stage=stage, todo_count=count, extra=extra), "attend_back", outs,
        (todo, place, seg, need, *operands),
        scratch=[pltpu.VMEM((piece, piece), f32)] * 4
        + [pltpu.VMEM((HEAD, piece), f32)] * 2
        + [pltpu.SMEM((pieces,), jnp.int32)]
        + ([pltpu.VMEM(sums.shape, f32)] if stage else []),
        scalars=4, mib=36, late=(0, 1),
    )
    return got[0] if stage else got


def after(value, *earlier):
    return lax.optimization_barrier((value,) + earlier)[0]


def on_device(
    tokens, first_values, cotangent, parents, seg_lengths,
    w_query, w_key, w_value, w_out, w_gate, w_up, w_down, gain_attn, gain_ffn,
):
    assert tokens.shape[1] == 1
    fsdp_count, ctx_count, tp_count = (lax.axis_size(a) for a in ("fsdp", "ctx", "tp"))
    assert tp_count == 4 and ctx_count == 4
    fsdp_at, ctx_at, tp_at = (lax.axis_index(a) for a in ("fsdp", "ctx", "tp"))
    core_at, x_at = tp_at % 2, tp_at // 2
    own_rows, width = tokens.shape[0], tokens.shape[2]
    chip_rows = 2 * own_rows
    heads = w_query.shape[1] // HEAD
    head_width = heads * HEAD
    assert heads == ctx_count
    tree_len = own_rows * tp_count * ctx_count
    weight_rows, hidden = w_query.shape[0], w_gate.shape[1]
    two = fsdp_count == 2

    def over_core(value):
        return lax.ppermute(value, "tp", [(i, i ^ 1) for i in range(tp_count)])

    def over_x(value):
        return lax.ppermute(value, "tp", [(i, i ^ 2) for i in range(tp_count)])

    def over_fsdp(value):
        return lax.ppermute(value, "fsdp", [(0, 1), (1, 0)])

    def over_ctx(value, flip):
        return lax.ppermute(value, "ctx", [(i, i ^ flip) for i in range(ctx_count)])

    def exchange(by_place):
        return lax.all_to_all(by_place, "ctx", 0, 0, tiled=True)

    def relative(rows):
        if not two:
            return rows
        swapped = jnp.concatenate([rows[..., weight_rows:], rows[..., :weight_rows]], axis=-1)
        return jnp.where(fsdp_at == 0, rows, swapped)

    def by_x(near, far):
        return jnp.where(x_at == 0, jnp.concatenate([near, far], axis=0), jnp.concatenate([far, near], axis=0))

    def fsdp_sum(parts, axis=0):
        if not two:
            return lax.psum_scatter(parts[0], "fsdp", scatter_dimension=axis, tiled=True)
        return parts[0], over_fsdp(parts[1])

    def inward(low):
        return low, lax.ppermute(low, "ctx", [(0, 1), (3, 2)])

    def across(low):
        return low, lax.ppermute(low, "ctx", [(1, 2), (2, 1)])

    def outward(low):
        return low, lax.ppermute(low, "ctx", [(1, 0), (2, 3)])

    def join(pair):
        return (pair[0].astype(f32) + pair[1].astype(f32)).astype(bf16)

    def finish(pair):
        return jnp.where((ctx_at == 0) | (ctx_at == 3), pair[1], pair[0]).astype(f32)

    def hold(pair, *earlier):
        return (pair[0], after(pair[1], *earlier)) if isinstance(pair, tuple) else after(pair, *earlier)

    def step(*pairs):
        if not two:
            return [join(pair) if isinstance(pair, tuple) else pair for pair in pairs]
        return join_call(*pairs)

    three = (w_query, w_key, w_value)
    own_tokens, early_gains = tokens[:, 0, :], jnp.stack([gain_attn, gain_ffn])
    if two:
        own_three = stack_call(*three)
        qkv_weight = [own_three, over_fsdp(own_three)]
        own_tokens, early_gains = after(own_tokens, own_three), after(early_gains, own_three)
        gains = jnp.concatenate([early_gains, over_fsdp(early_gains)], axis=1)
    else:
        qkv_weight = [stack_call(*(lax.all_gather(w, "fsdp", axis=0, tiled=True) for w in three))]
        gains = lax.all_gather(early_gains, "fsdp", axis=1, tiled=True)
    token_x = over_x(own_tokens)
    token_core = over_core(own_tokens)
    attention_gain = gains[0].reshape(1, width).astype(f32)
    ffn_gain = gains[1].reshape(1, width).astype(f32)
    count = len(qkv_weight)

    place = jnp.stack([x_at, core_at, ctx_at, fsdp_at]).astype(jnp.int32)
    position, query_extra, key_extra, seg_bits, need_bits = layout_call(parents, seg_lengths, tree_len, chip_rows)
    frequency = jnp.exp(-math.log(10000.0) * jnp.arange(HALF, dtype=f32) / HALF)
    angles = frequency[None, :, None] * position
    cosine, sine = jnp.cos(angles), jnp.sin(angles)

    def normalize(rows_f32):
        return lax.rsqrt(jnp.mean(rows_f32 * rows_f32, axis=-1, keepdims=True) + epsilon)

    first_flat = first_values[:, 0, :]

    def spread(pieces):
        return [over_ctx(piece, flip) if flip else piece for flip, piece in enumerate(pieces)]

    by_head, near_normed, far_normed = project_call(
        place, (own_tokens, token_core, token_x, over_core(token_x)), attention_gain, cosine, sine, first_flat, qkv_weight, two
    )
    got = exchange(by_head)
    others = (w_gate, w_up, w_down, w_out)
    if two:
        feed_own = stack_call(*(after(w.T, by_head) for w in others))
        feed_weight = [feed_own, over_fsdp(feed_own)]
    else:
        feed_weight = [stack_call(*(lax.all_gather(w, "fsdp", axis=0, tiled=True).T for w in others))]
    own_cot = relative(after(cotangent[:, 0, :], by_head))
    half_places = jnp.arange(ctx_count, dtype=jnp.int32) * 2
    far_out, far_full, far_lse, keys, key_lanes, value_lanes, values, queries = fwd_call(
        after(half_places + (1 - x_at), own_cot), place, seg_bits, need_bits, (got, query_extra, key_extra), True
    )
    cot_x = over_x(after(own_cot, got))
    out_weight = pick_call([after(w, far_out) for w in feed_weight], head_width)
    out_weight_x = over_x(out_weight)
    cot_core = over_core(after(own_cot, got))
    cot_x_core = over_core(cot_x)

    near_out, near_full, near_lse = fwd_call(
        after(half_places + x_at, far_out, out_weight, cot_x), place, seg_bits, need_bits, (keys, value_lanes, queries)
    )
    far_mixed = after(exchange(far_out), near_out).reshape(head_width, chip_rows)
    far_mixed_got = over_x(far_mixed)
    near_mixed = exchange(after(near_out, far_mixed)).reshape(head_width, chip_rows)

    mine, other = output_call(place, near_mixed, far_mixed_got, out_weight, out_weight_x)
    own_single = relative(own_tokens).astype(f32)
    middle = own_single + mine + over_core(other).astype(f32)

    middle_scale = normalize(middle)
    ffn_own = (middle * middle_scale * ffn_gain).astype(bf16)
    ffn_x = over_x(ffn_own)
    ffn_core = over_core(ffn_own)
    near_hidden, near_gate, near_up, near_mine, near_sent = feed_call(
        ffn_own, ffn_core, own_cot, cot_core, feed_weight, hidden
    )
    ffn_x = after(ffn_x, near_mine)
    ffn_x_core = over_core(ffn_x)
    far_hidden, far_gate, far_up, far_mine, far_sent = feed_call(
        ffn_x, ffn_x_core, cot_x, cot_x_core, feed_weight, hidden
    )
    far_sum = (far_mine + over_core(far_sent).astype(f32)).astype(bf16)
    far_sum_got = over_x(far_sum)
    near_sum = near_mine + over_core(near_sent).astype(f32)

    all_cot = (after(own_cot, far_sum), cot_core, cot_x, cot_x_core)
    all_ffn = (after(ffn_own, far_sum), ffn_core, ffn_x, ffn_x_core)
    first_parts, second_parts = feed_grads_call(
        (near_gate, far_gate, near_up, far_up), (near_hidden, far_hidden), all_ffn, all_cot, count
    )
    first_sum = fsdp_sum(first_parts, 1)
    second_sum = fsdp_sum(second_parts, 1)
    ffn_grad = near_sum + after(far_sum_got, first_parts[0]).astype(f32)

    weighted = ffn_grad * ffn_gain
    middle_grad = (
        own_cot.astype(f32)
        + middle_scale * weighted
        - middle * (middle_scale**3 * jnp.mean(weighted * middle, axis=-1, keepdims=True))
    )
    middle_low = middle_grad.astype(bf16)
    near_heads, far_heads, chip_low = heads_call(place, middle_low, over_core(middle_low), out_weight, out_weight_x)
    far_out_grad = over_x(far_heads)
    near_grads = exchange(near_heads.reshape(heads, HEAD, chip_rows))
    far_grads = exchange(after(far_out_grad, near_grads).reshape(heads, HEAD, chip_rows))

    ffn_gain_part = jnp.sum(after(ffn_grad, near_heads) * middle * middle_scale, axis=0)
    low_x = over_x(after(middle_low, far_out_grad))
    low_x_core = over_core(low_x)
    near_result, far_result, sent = result_call(after(near_hidden, near_heads), far_hidden, feed_weight)
    sent_got = over_core(sent)
    (first_low,) = step(hold(first_sum, far_grads, sent))
    first_in = inward(first_low)
    def back(stage, places, more, *earlier):
        return bwd_call(
            stage, after(jnp.stack(places).astype(jnp.int32), *earlier), place, seg_bits, need_bits, cosine, sine,
            keys, key_lanes, values, more[0], more[1:], query_extra.shape[1],
        )

    far_at, near_at = [2 * i + 1 - x_at for i in range(4)], [2 * i + x_at for i in range(4)]
    far_kv, back_queries, grads, query_sum = back(
        0, far_at, (queries, near_grads, far_grads, near_full, far_full, near_lse, far_lse), first_low
    )

    first_low, second_low = step(hold(first_in, far_kv), hold(second_sum, far_kv))
    first_across, second_in = across(first_low), inward(second_low)
    last = back(1, near_at, (back_queries, grads, far_kv, query_sum), first_low)
    first_got, second_got = hold(first_across, last), hold(second_in, last)

    last_got = exchange(last)
    out_parts = out_grads_call(after(place, last), chip_low, low_x, low_x_core, near_mixed, far_mixed, count)
    far_result_got = over_x((after(far_result, out_parts[0]) + sent_got[1].astype(f32)).astype(bf16))
    layer_out = relative((middle + near_result + sent_got[0].astype(f32) + far_result_got.astype(f32)).astype(bf16))
    last_got = after(last_got, layer_out)

    qkv_parts = weights_call(near_normed, far_normed, last_got, out_parts)
    qkv_sum = fsdp_sum(qkv_parts)
    first_low, second_low = step(hold(first_got, qkv_parts[0]), hold(second_got, qkv_parts[0]))
    first_done, second_across = outward(first_low), across(second_low)
    near_mine, near_other, far_mine, far_other, gain_part, grad_values = rows_call(
        after(place, first_low), near_normed, far_normed, last_got, qkv_weight
    )
    far_rows_got = over_x((far_mine + over_core(far_other).astype(f32)).astype(bf16))
    near_rows_got = over_core(near_other)
    gain_sum = jnp.concatenate([gain_part / attention_gain, ffn_gain_part[None]], axis=0)

    def light(*pairs):
        return [join(pair) if isinstance(pair, tuple) else pair for pair in pairs]

    qkv_low, second_low = light(hold(qkv_sum, near_mine), hold(second_across, near_mine))
    qkv_in, second_done = inward(qkv_low), outward(second_low)
    first_all = finish(hold(first_done, qkv_in[1] if isinstance(qkv_in, tuple) else qkv_in))
    if two:
        gain_sum = after(gain_sum, qkv_low)
        gain_sum = gain_sum + over_core(gain_sum)
        gain_sum = gain_sum + over_x(gain_sum)
        gain_sum = gain_sum[:, :weight_rows] + over_fsdp(gain_sum[:, weight_rows:])
    (qkv_low,) = light(hold(qkv_in, gain_sum, far_rows_got, first_all))
    lows = [qkv_low]
    qkv_across = across(qkv_low)
    if two:
        gain_sum = after(gain_sum, qkv_low)
        gain_sum = gain_sum + over_ctx(gain_sum, 1)
    second_all = finish(hold(second_done, qkv_across[1]))
    (qkv_low,) = light(hold(qkv_across, gain_sum, second_all))
    if two:
        gain_sum = gain_sum + over_ctx(after(gain_sum, qkv_low), 2)
    else:
        gain_sum = lax.psum(gain_sum, ("fsdp", "ctx", "tp"))
        gain_sum = lax.dynamic_slice_in_dim(gain_sum, fsdp_at * weight_rows, weight_rows, 1)
    grad_query, grad_key, grad_value, grad_out = jnp.split(finish(hold(outward(qkv_low), gain_sum)), 4)
    grad_gate, grad_down = first_all[:hidden].T, second_all[hidden // 2 :].T
    grad_up = jnp.concatenate([first_all[hidden:], second_all[: hidden // 2]], axis=0).T

    normed_grad = after(near_mine, lows[0]) + near_rows_got.astype(f32) + far_rows_got.astype(f32)
    scale = normalize(own_single)
    weighted = normed_grad * attention_gain
    grad_tokens = (
        middle_grad + scale * weighted - own_single * (scale**3 * jnp.mean(weighted * own_single, axis=-1, keepdims=True))
    )
    return (
        layer_out[:, None, :],
        relative(grad_tokens)[:, None, :],
        grad_values.reshape(4 * own_rows, 1, head_width),
        grad_query,
        grad_key,
        grad_value,
        grad_out,
        grad_gate,
        grad_up,
        grad_down,
        gain_sum[0],
        gain_sum[1],
    )

def solution(mesh):
    rows, columns = P(("ctx", "tp"), "fsdp", None), P("ctx", "fsdp", "tp")
    weight, gain = P("fsdp", "tp"), P("fsdp")
    return jax.shard_map(
        on_device,
        mesh=mesh,
        in_specs=(rows, columns, rows, P("fsdp", None), P("fsdp", None)) + (weight,) * 7 + (gain,) * 2,
        out_specs=(rows, rows, columns) + (weight,) * 7 + (gain,) * 2,
        check_vma=False,
    )
```

```python
import functools
import math

import jax
import jax.numpy as jnp
from jax import lax
from jax.experimental import pallas as pl
from jax.experimental.pallas import tpu as pltpu
from jax.sharding import PartitionSpec as P

HEAD = 64
HALF = HEAD // 2
BIG = 1e30
LOG2E = 1.4426950408889634
SCORE_SCALE = HEAD**-0.5
QUERY_SCALE = SCORE_SCALE * LOG2E
epsilon = 1e-05
f32 = jnp.float32
bf16 = jnp.bfloat16


def dot(a, b, ca, cb):
    return lax.dot_general(a, b, (((ca,), (cb,)), ((), ())), preferred_element_type=f32)


def layout_kernel(par_ref, len_ref, pos_ref, qx_ref, kx_ref, seg_ref, need_ref, anc_sc, above_sc, *, segs, tokens, piece):
    token = lax.broadcasted_iota(jnp.int32, (1, tokens), 1)
    pos = jnp.zeros((1, tokens), jnp.int32)
    seg_of = jnp.full((1, tokens), -1, jnp.int32)
    bits = jnp.zeros((1, tokens), jnp.int32)
    for b in range(tokens // piece):
        seg_ref[b] = 0
        need_ref[b] = 0
    off = jnp.int32(0)
    for s in range(segs):
        length = len_ref[0, s]
        if s == 0:
            anc, above = jnp.int32(1), jnp.int32(0)
        else:
            parent = par_ref[0, s]
            anc = anc_sc[parent] | jnp.int32(1 << s)
            above = above_sc[parent] + len_ref[0, parent]
        anc_sc[s] = anc
        above_sc[s] = above
        started = token >= off
        seg_of = jnp.where(started, s, seg_of)
        pos = jnp.where(started, token - off + above, pos)
        bits = jnp.where(started, anc, bits)

        def mark(b, carry, anc=anc, s=s):
            seg_ref[b] = seg_ref[b] | jnp.int32(1 << s)
            need_ref[b] = need_ref[b] | anc
            return carry

        lax.fori_loop(off // piece, (off + length - 1) // piece + 1, mark, 0)
        off = off + length
    row = lax.broadcasted_iota(jnp.int32, (kx_ref.shape[1], tokens), 0)
    key_extra = jnp.where(row == seg_of, -BIG, 0.0).astype(bf16)
    linked = lax.shift_right_logical(jnp.broadcast_to(bits, row.shape), row) & 1
    query_extra = jnp.where(linked == 1, 0.0, 1.0).astype(bf16)
    for p in range(tokens // piece):
        lanes = slice(p * piece, (p + 1) * piece)
        pos_ref[p] = pos[:, lanes].astype(f32)
        kx_ref[p] = key_extra[:, lanes]
        qx_ref[p] = query_extra[:, lanes]


SMEM = pl.BlockSpec(memory_space=pltpu.SMEM)
VMEM = pl.BlockSpec(memory_space=pltpu.VMEM)


def layout_call(parents, lengths, tokens, piece):
    segs = parents.shape[-1]
    rows = -(-segs // 16) * 16
    return pl.pallas_call(
        functools.partial(layout_kernel, segs=segs, tokens=tokens, piece=piece),
        out_shape=(
            jax.ShapeDtypeStruct((tokens // piece, 1, piece), f32),
            jax.ShapeDtypeStruct((tokens // piece, rows, piece), bf16),
            jax.ShapeDtypeStruct((tokens // piece, rows, piece), bf16),
            jax.ShapeDtypeStruct((tokens // piece,), jnp.int32),
            jax.ShapeDtypeStruct((tokens // piece,), jnp.int32),
        ),
        in_specs=[SMEM, SMEM],
        out_specs=(VMEM, VMEM, VMEM, SMEM, SMEM),
        scratch_shapes=[pltpu.SMEM((segs,), jnp.int32), pltpu.SMEM((segs,), jnp.int32)],
        cost_estimate=pl.CostEstimate(flops=0, bytes_accessed=1 << 16, transcendentals=0),
        name="layout",
    )(parents, lengths)


def causal(scores):
    key_at = lax.broadcasted_iota(jnp.int32, scores.shape, 0)
    query_at = lax.broadcasted_iota(jnp.int32, scores.shape, 1)
    return jnp.where(key_at <= query_at, scores, -BIG)


def three_parts(row):
    at = lax.broadcasted_iota(jnp.int32, (16, row.shape[1]), 0)
    high = row.astype(bf16).astype(f32)
    rest = row - high
    mid = rest.astype(bf16).astype(f32)
    low = rest - mid
    return jnp.where(at == 0, high, jnp.where(at == 1, mid, jnp.where(at == 2, low, 0.0))).astype(bf16)


def unrotate(values, cosine, sine):
    a, b = values[:HALF], values[HALF:]
    return jnp.concatenate([a * cosine + b * sine, b * cosine - a * sine], axis=0)


def prep_kernel(place_ref, qx_ref, kx_ref, got_ref, keys, key_lanes, value_lanes, values, queries):
    piece = got_ref.shape[2] // 2
    extra = qx_ref.shape[1]
    minus = jnp.full((16, piece), -1.0, bf16)
    pad_key = jnp.zeros((128 - HEAD - extra - 16, piece), bf16)
    pad_value = jnp.zeros((128 - HEAD - 16, piece), bf16)
    for half in (0, 1):
        for p in range(got_ref.shape[0]):
            at = 2 * p + (place_ref[0] ^ half)
            got = got_ref[p, :, half * piece : (half + 1) * piece]
            query, key, value = got[:HEAD, :], got[HEAD : 2 * HEAD, :], got[2 * HEAD :, :]
            key_lanes[at] = key
            keys[at] = jnp.concatenate([key, kx_ref[at], minus, pad_key], axis=0).T
            value_lanes[at] = jnp.concatenate([value, -minus], axis=0)
            values[at] = jnp.concatenate([value, minus, pad_value], axis=0).T
            queries[at] = jnp.concatenate([query, qx_ref[at], jnp.zeros((128 - HEAD - extra, piece), bf16)], axis=0)


def shape_of(*sizes, dtype=bf16):
    return jax.ShapeDtypeStruct(sizes, dtype)


def call(kernel, name, out_shape, operands, scratch=(), scalars=1, mib=20, late=()):
    outs = out_shape if isinstance(out_shape, tuple) else (out_shape,)
    arrays = operands[scalars:]
    count, total = len(arrays), len(arrays) + len(outs)

    def body(*refs):
        first, rest = refs[:scalars], refs[scalars:]
        outside, inside, sems, rest = rest[:total], rest[total : 2 * total], rest[2 * total], rest[2 * total + 1 :]
        copies = [pltpu.make_async_copy(outside[i], inside[i], sems.at[i]) for i in range(count)]
        for copy in copies:
            copy.start()
        for i in range(count):
            if i not in late:
                copies[i].wait()
        more = {"ready": lambda: [copies[i].wait() for i in late]} if late else {}
        kernel(*first, *inside, *rest, **more)
        copies = [pltpu.make_async_copy(inside[i], outside[i], sems.at[i]) for i in range(count, total)]
        for copy in copies:
            copy.start()
        for copy in copies:
            copy.wait()

    got = pl.pallas_call(
        body,
        out_shape=outs,
        in_specs=[SMEM] * scalars + [pl.BlockSpec(memory_space=pltpu.HBM)] * count,
        out_specs=(pl.BlockSpec(memory_space=pltpu.HBM),) * len(outs),
        scratch_shapes=[pltpu.VMEM(x.shape, x.dtype) for x in (*arrays, *outs)]
        + [pltpu.SemaphoreType.DMA((total,))]
        + list(scratch),
        compiler_params=pltpu.CompilerParams(vmem_limit_bytes=60 << 20),
        cost_estimate=pl.CostEstimate(flops=0, bytes_accessed=1 << 16, transcendentals=0),
        name=name,
    )(*operands)
    return got if isinstance(out_shape, tuple) else got[0]


def cut(ref, count):
    size = ref.shape[1] // count
    return [ref[:, i * size : (i + 1) * size] for i in range(count)]


def project_kernel(place_ref, near_own, near_other, far_own, far_other, gain_ref, cos_ref, sin_ref, first_ref, *rest, count, swap):
    weights, (out, near_out, far_out, raw) = rest[:count], rest[count:]
    heads_width = raw.shape[0] // 3
    size, width = near_own.shape
    block = width // count
    for refs, normed in (((near_own, near_other), near_out), ((far_own, far_other), far_out)):
        for half, ref in enumerate(refs):
            single = ref[...].astype(f32)
            scale = lax.rsqrt(jnp.mean(single * single, axis=-1, keepdims=True) + epsilon)
            if swap:
                turned = jnp.concatenate([single[:, block:], single[:, :block]], axis=1)
                single = jnp.where(place_ref[3] == 0, single, turned)
            at = pl.multiple_of((place_ref[1] ^ half) * size, size)
            normed[pl.ds(at, size), :] = (single * scale * gain_ref[...]).astype(bf16)
    piece = 2 * size
    turned = [[w[i * block : (i + 1) * block, :].T for w in weights] for i in range(3)]
    for half, rows_ref in enumerate((near_out, far_out)):
        rows = cut(rows_ref, count)
        for i in range(3):
            raw[i * heads_width : (i + 1) * heads_width, :] = sum(dot(w, r, 1, 1) for w, r in zip(turned[i], rows))
        x_half = place_ref[0] ^ half
        at = 2 * place_ref[2] + x_half
        cosine, sine = cos_ref[at], sin_ref[at]
        start = pl.multiple_of(x_half * piece, piece)
        first = first_ref[pl.ds(start, piece), :].astype(f32).T

        def turn(values):
            a, b = values[:HALF], values[HALF:]
            return jnp.concatenate([a * cosine - b * sine, b * cosine + a * sine], axis=0)

        lanes = slice(half * piece, (half + 1) * piece)
        for at in range(heads_width // HEAD):
            rows_at = [slice(i * heads_width + at * HEAD, i * heads_width + (at + 1) * HEAD) for i in range(3)]
            value = 0.5 * raw[rows_at[2], :] + 0.5 * first[at * HEAD : (at + 1) * HEAD]
            out[at, :HEAD, lanes] = (turn(raw[rows_at[0], :]) * QUERY_SCALE).astype(bf16)
            out[at, HEAD : 2 * HEAD, lanes] = turn(raw[rows_at[1], :]).astype(bf16)
            out[at, 2 * HEAD :, lanes] = value.astype(bf16)


def project_call(place, rows, gain, cosine, sine, first, weights, swap):
    (size, width), columns = rows[0].shape, weights[0].shape[1]
    return call(
        functools.partial(project_kernel, count=len(weights), swap=swap), "project",
        (shape_of(columns // HEAD, 3 * HEAD, 4 * size), shape_of(2 * size, width), shape_of(2 * size, width)),
        (place, *rows, gain, cosine, sine, first, *weights),
        scratch=[pltpu.VMEM((3 * columns, 2 * size), f32)],
    )


def stack_kernel(*refs):
    out, at = refs[-1], 0
    for ref in refs[:-1]:
        rows = ref.shape[0]
        out[at : at + rows, :] = ref[...]
        at += rows


def pick_kernel(*refs):
    out, inside, sems = refs[-3:]
    blocks, rows = refs[:-3], out.shape[0]
    size = out.shape[1] // len(blocks)
    copies = [
        pltpu.make_async_copy(ref.at[pl.ds(ref.shape[0] - rows, rows), :], inside.at[:, pl.ds(i * size, size)], sems.at[i])
        for i, ref in enumerate(blocks)
    ]
    for copy in copies:
        copy.start()
    for copy in copies:
        copy.wait()
    copy = pltpu.make_async_copy(inside, out, sems.at[len(blocks)])
    copy.start()
    copy.wait()


def pick_call(blocks, rows):
    out = shape_of(rows, blocks[0].shape[1] * len(blocks))
    return pl.pallas_call(
        pick_kernel,
        out_shape=out,
        in_specs=[pl.BlockSpec(memory_space=pltpu.HBM)] * len(blocks),
        out_specs=pl.BlockSpec(memory_space=pltpu.HBM),
        scratch_shapes=[pltpu.VMEM(out.shape, out.dtype), pltpu.SemaphoreType.DMA((len(blocks) + 1,))],
        compiler_params=pltpu.CompilerParams(vmem_limit_bytes=60 << 20),
        cost_estimate=pl.CostEstimate(flops=0, bytes_accessed=1 << 16, transcendentals=0),
        name="pick",
    )(*blocks)


def stack_call(*arrays):
    rows = sum(a.shape[0] for a in arrays)
    return call(stack_kernel, "stack", shape_of(rows, arrays[0].shape[1]), arrays, scalars=0, mib=16)


def split_core(place_ref, total, mine_ref, other_ref):
    rows = mine_ref.shape[0]
    mine_ref[...] = total[pl.ds(pl.multiple_of(place_ref[1] * rows, rows), rows), :]
    other_ref[...] = total[pl.ds(pl.multiple_of((1 - place_ref[1]) * rows, rows), rows), :].astype(bf16)


def output_kernel(place_ref, near_ref, far_ref, *rest):
    near_weight, far_weight, mine_ref, other_ref, total = rest
    total[...] = dot(near_ref[...].T, near_weight[...], 1, 0) + dot(far_ref[...].T, far_weight[...], 1, 0)
    split_core(place_ref, total, mine_ref, other_ref)


def output_call(place, near, far, near_weight, far_weight):
    rows, width = near.shape[1], near_weight.shape[1]
    return call(
        output_kernel, "out_project",
        (shape_of(rows // 2, width, dtype=f32), shape_of(rows // 2, width)),
        (place, near, far, near_weight, far_weight),
        scratch=[pltpu.VMEM((rows, width), f32)],
    )


def heads_kernel(place_ref, own_ref, other_ref, near_weight, far_weight, near_out, far_out, chip):
    rows = own_ref.shape[0]
    for half, ref in enumerate((own_ref, other_ref)):
        chip[pl.ds(pl.multiple_of((place_ref[1] ^ half) * rows, rows), rows), :] = ref[...]
    far_out[...] = dot(far_weight[...], chip[...], 1, 1).astype(bf16)
    near_out[...] = dot(near_weight[...], chip[...], 1, 1).astype(bf16)


def heads_call(place, own, other, near_weight, far_weight):
    rows, columns = 2 * own.shape[0], near_weight.shape[0]
    return call(
        heads_kernel, "out_back",
        (shape_of(columns, rows), shape_of(columns, rows), shape_of(rows, own.shape[1])),
        (place, own, other, near_weight, far_weight),
    )


def feed_kernel(rows_ref, other_ref, cot_ref, cot_other_ref, *rest, count):
    hidden = rest[count].shape[2]
    gate_w, up_w, down_w = ([w.at[i * hidden : (i + 1) * hidden] for w in rest[:count]] for i in range(3))
    hidden_ref, gate_ref, up_ref, mine_ref, sent_ref, rows_sc, cot_sc, back_sc = rest[count:]
    size = rows_ref.shape[0]
    rows_sc[0], rows_sc[1] = rows_ref[...], other_ref[...]
    cot_sc[0], cot_sc[1] = cot_ref[...], cot_other_ref[...]
    block = rows_ref.shape[1] // count

    def step(at, carry):
        lanes = [slice(i * block, (i + 1) * block) for i in range(count)]
        rows, cots = [rows_sc[at, :, s] for s in lanes], [cot_sc[at, :, s] for s in lanes]
        gate = sum(dot(r, w[...], 1, 1) for r, w in zip(rows, gate_w))
        up = sum(dot(r, w[...], 1, 1) for r, w in zip(rows, up_w))
        hidden_grad = sum(dot(r, w[...], 1, 1) for r, w in zip(cots, down_w))
        sig = 1.0 / (1.0 + jnp.exp(-gate))
        act = gate * sig
        hidden_ref[at] = (act * up).astype(bf16)
        gate_grad = (hidden_grad * up * (sig * (1.0 + gate * (1.0 - sig)))).astype(bf16)
        up_grad = (hidden_grad * act).astype(bf16)
        gate_ref[at] = gate_grad
        up_ref[at] = up_grad
        for i in range(count):
            back_sc[at, :, lanes[i]] = dot(gate_grad, gate_w[i][...], 1, 0) + dot(up_grad, up_w[i][...], 1, 0)
        return carry

    lax.fori_loop(0, 2, step, 0)
    mine_ref[...] = back_sc[0]
    sent_ref[...] = back_sc[1].astype(bf16)


def feed_call(rows, other, cot, cot_other, weights, hidden):
    size, width = rows.shape
    count = len(weights)
    return call(
        functools.partial(feed_kernel, count=count), "feed",
        (shape_of(2, size, hidden),) * 3 + (shape_of(size, width, dtype=f32), shape_of(size, width)),
        (rows, other, cot, cot_other, *weights),
        scratch=[pltpu.VMEM((2, size, width), bf16)] * 2 + [pltpu.VMEM((2, size, width), f32)],
        scalars=0, mib=40,
    )


def prep_back(place_ref, queries, near_grad, far_grad, near_full, far_full, near_lse, far_lse, queries_out, grads_out, extra):
    places, _, piece = near_grad.shape
    queries_out[...] = queries[...]
    pad = jnp.zeros((128 - HEAD - 16, piece), bf16)
    for half, (grad, full, lse) in enumerate(((near_grad, near_full, near_lse), (far_grad, far_full, far_lse))):
        for p in range(places):
            at = 2 * p + (place_ref[0] ^ half)
            queries_out[at, HEAD + extra : HEAD + extra + 16, :] = lse[p]
            delta = jnp.sum(grad[p].astype(f32) * full[p], axis=0, keepdims=True)
            grads_out[at] = jnp.concatenate([grad[p], three_parts(delta), pad], axis=0)


def by_projection(got):
    columns = got.shape[0] * HEAD
    flat = lambda at: got[:, at * HEAD : (at + 1) * HEAD, :].reshape(columns, got.shape[2])
    return (flat(2), flat(0), flat(1)), (flat(3), flat(4), flat(5))


def weights_kernel(near_rows, far_rows, last, *rest):
    count = len(rest) // 2
    out_parts, parts = rest[:count], rest[count:]
    size = near_rows.shape[1] // count
    for part, out_part in zip(parts, out_parts):
        part[3 * size :, :] = out_part[...]
    near, far = by_projection(last)
    for i in range(3):
        for b, part in enumerate(parts):
            lanes = slice(b * size, (b + 1) * size)
            sums = dot(near[i], near_rows[:, lanes], 1, 0) + dot(far[i], far_rows[:, lanes], 1, 0)
            part[i * size : (i + 1) * size, :] = sums.T.astype(bf16)


def weights_call(near_rows, far_rows, last, out_parts):
    width, columns, count = near_rows.shape[1], last.shape[0] * HEAD, len(out_parts)
    return call(
        weights_kernel, "weight_grads", tuple(shape_of(4 * width // count, columns) for _ in range(count)),
        (near_rows, far_rows, last, *out_parts), scalars=0,
    )


def rows_kernel(place_ref, near_rows, far_rows, last, *rest, count):
    weights, (near_mine, near_other, far_mine, far_other, gain_ref, value_ref, total) = rest[:count], rest[count:]
    size = near_rows.shape[1] // count
    near, far = by_projection(last)
    for half, grads in enumerate((near, far)):
        value = grads[2].T.astype(f32)
        tokens, columns = value.shape
        folds = columns // 128
        for j in range(folds):
            rows_at = pl.ds((place_ref[0] ^ half) * tokens * folds + j, tokens, stride=folds)
            value_ref[rows_at, :] = value[:, j * 128 : (j + 1) * 128]
    gain_ref[...] = jnp.zeros(gain_ref.shape, f32)
    for grads, rows, mine, other in ((far, far_rows, far_mine, far_other), (near, near_rows, near_mine, near_other)):
        turned = [g.T for g in grads]
        for b in range(count):
            lanes = slice(b * size, (b + 1) * size)
            part = sum(dot(g, weights[b][i * size : (i + 1) * size, :], 1, 1) for i, g in enumerate(turned))
            total[:, lanes] = part
            gain_ref[:, lanes] += jnp.sum(part * rows[:, lanes].astype(f32), axis=0, keepdims=True)
        split_core(place_ref, total, mine, other)


def rows_call(place, near_rows, far_rows, last, weights):
    size, width = near_rows.shape
    rows = (shape_of(size // 2, width, dtype=f32), shape_of(size // 2, width))
    values = shape_of(2 * size * last.shape[0] * HEAD // 128, 128, dtype=f32)
    return call(
        functools.partial(rows_kernel, count=len(weights)), "rows_back",
        rows + rows + (shape_of(1, width, dtype=f32), values),
        (place, near_rows, far_rows, last, *weights),
        scratch=[pltpu.VMEM((size, width), f32)],
    )


def feed_grads_kernel(near_gate, far_gate, near_up, far_up, near_hidden, far_hidden, *refs):
    rows, cots, outs = refs[:4], refs[4:8], refs[8:]
    count = len(outs) // 2
    size = rows[0].shape[1] // count
    hidden = near_gate.shape[2]
    half = hidden // 2
    pairs = ((near_gate, far_gate, rows), (near_up, far_up, rows), (near_hidden, far_hidden, cots))
    for b in range(count):
        lanes = slice(b * size, (b + 1) * size)
        first, second = outs[b], outs[count + b]
        for i, (near, far, right) in enumerate(pairs):
            near, far = (ref[...].reshape(2 * ref.shape[1], hidden) for ref in (near, far))
            near_right, far_right = (jnp.concatenate([right[j][:, lanes], right[j + 1][:, lanes]], axis=0) for j in (0, 2))
            total = (dot(near, near_right, 0, 0) + dot(far, far_right, 0, 0)).astype(bf16)
            if i == 0:
                first[:hidden, :] = total
            elif i == 1:
                first[hidden:, :] = total[:half]
                second[:half, :] = total[half:]
            else:
                second[half:, :] = total


def feed_grads_call(lefts, hiddens, rows, cots, count):
    hidden, size = lefts[0].shape[2], rows[0].shape[1] // count
    outs = call(
        feed_grads_kernel, "feed_grads", tuple(shape_of(3 * hidden // 2, size) for _ in range(2 * count)),
        (*lefts, *hiddens, *rows, *cots), scalars=0, mib=40,
    )
    return outs[:count], outs[count:]


def result_kernel(near_hidden, far_hidden, *rest, count):
    weights, (near_mine, far_mine, sent) = rest[:count], rest[count:]
    size = near_mine.shape[1] // count
    for at, (ref, mine) in enumerate(((near_hidden, near_mine), (far_hidden, far_mine))):
        for i in range(count):
            lanes = slice(i * size, (i + 1) * size)
            weight = weights[i][2 * ref.shape[2] : 3 * ref.shape[2], :]
            mine[:, lanes] = dot(ref[0], weight, 1, 0)
            sent[at, :, lanes] = dot(ref[1], weight, 1, 0).astype(bf16)


def result_call(near_hidden, far_hidden, weights):
    _, size, _ = near_hidden.shape
    count = len(weights)
    width = weights[0].shape[1] * count
    return call(
        functools.partial(result_kernel, count=count), "result",
        (shape_of(size, width, dtype=f32), shape_of(size, width, dtype=f32), shape_of(2, size, width)),
        (near_hidden, far_hidden, *weights), scalars=0, mib=24,
    )


def out_grads_kernel(place_ref, chip_low, far_own, far_other, near_mixed, far_mixed, *rest):
    outs, far_low = rest[:-1], rest[-1]
    count = len(outs)
    rows = far_own.shape[0]
    for half, ref in enumerate((far_own, far_other)):
        far_low[pl.ds(pl.multiple_of((place_ref[1] ^ half) * rows, rows), rows), :] = ref[...]
    near, far = near_mixed[...], far_mixed[...]
    for out, near_rows, far_rows in zip(outs, cut(chip_low, count), cut(far_low, count)):
        out[...] = (dot(near, near_rows, 1, 0) + dot(far, far_rows, 1, 0)).T.astype(bf16)


def out_grads_call(place, chip_low, far_own, far_other, near_mixed, far_mixed, count):
    width, columns = chip_low.shape[1] // count, near_mixed.shape[0]
    return call(
        out_grads_kernel, "out_grads", tuple(shape_of(width, columns) for _ in range(count)),
        (place, chip_low, far_own, far_other, near_mixed, far_mixed),
        scratch=[pltpu.VMEM(chip_low.shape, bf16)],
    )


def join_kernel(*refs):
    count = len(refs) // 3
    for i in range(count):
        a, b, out = refs[2 * i], refs[2 * i + 1], refs[2 * count + i]
        out[...] = (a[...].astype(f32) + b[...].astype(f32)).astype(bf16)


def join_call(*pairs):
    outs = call(
        join_kernel, "join", tuple(shape_of(*a.shape) for a, _ in pairs), [x for pair in pairs for x in pair],
        scalars=0, mib=16,
    )
    return list(outs)


def collect(first, last, hit, todo):
    def step(at, count):
        todo[count] = at
        return count + hit(at).astype(jnp.int32)

    return lax.fori_loop(first, last, step, jnp.int32(0))


def two_ahead(count, todo, first, fill, work):
    def step(j, now):
        middle, after = todo[2 * j], todo[2 * j + 1]
        fill(1, middle)
        work(0, now)
        fill(0, after)
        work(1, middle)
        return after

    last = lax.fori_loop(0, count // 2, step, first)

    @pl.when(lax.rem(count, 2) == 0)
    def _():
        work(0, last)

    @pl.when(lax.rem(count, 2) == 1)
    def _():
        final = todo[count - 1]
        fill(1, final)
        work(0, last)
        work(1, final)


def fwd_kernel(todo_ref, place_ref, seg_ref, need_ref, *refs, first):
    outs, (score_a, score_b, top, total, todo) = refs[:-5], refs[-5:]
    if first:
        got_ref, qx_ref, kx_ref, out_ref, full_ref, lse_ref, keys, key_lanes, values, plain_values, queries = outs
        prep_kernel(place_ref, qx_ref, kx_ref, got_ref, keys, key_lanes, values, plain_values, queries)
    else:
        keys, values, queries, out_ref, full_ref, lse_ref = outs
    scores = (score_a, score_b)

    def attend(i, carry):
        at = todo_ref[i]
        need = need_ref[at]
        count = collect(0, at, lambda k: (seg_ref[k] & need) != 0, todo)
        query = queries[at]
        score_a[...] = causal(dot(keys[at], query, 1, 0))
        top[...] = jnp.full(top.shape, -BIG, f32)
        total[...] = jnp.zeros(total.shape, f32)

        def fill(slot, key_at):
            scores[slot][...] = dot(keys[key_at], query, 1, 0)

        def work(slot, key_at):
            score = scores[slot][...]
            old_top = top[...]
            new_top = jnp.maximum(old_top, jnp.max(score, axis=0, keepdims=True))
            weights = jnp.exp2(score - new_top).astype(bf16)
            total[...] = total[...] * jnp.exp2(old_top - new_top) + dot(values[key_at], weights, 1, 0)
            top[...] = new_top

        two_ahead(count, todo, at, fill, work)
        final = total[...]
        weight_sum = final[HEAD : HEAD + 1, :]
        mixed = final[:HEAD, :] * (1.0 / weight_sum)
        out_ref[i] = mixed.astype(bf16)
        full_ref[i] = mixed
        lse_ref[i] = three_parts(top[...] + jnp.log2(weight_sum))
        return carry

    lax.fori_loop(0, out_ref.shape[0], attend, 0)


def fwd_call(todo, place, seg, need, operands, first=False):
    count = todo.shape[0]
    if first:
        pieces, piece = 2 * operands[0].shape[0], operands[0].shape[2] // 2
        more = (
            shape_of(pieces, piece, 128),
            shape_of(pieces, HEAD, piece),
            shape_of(pieces, HEAD + 16, piece),
            shape_of(pieces, piece, 128),
            shape_of(pieces, 128, piece),
        )
    else:
        (pieces, _, piece), more = operands[2].shape, ()
    return call(
        functools.partial(fwd_kernel, first=first), "attend",
        (shape_of(count, HEAD, piece), shape_of(count, HEAD, piece, dtype=f32), shape_of(count, 16, piece)) + more,
        (todo, place, seg, need, *operands),
        scratch=[pltpu.VMEM((piece, piece), f32)] * 2
        + [pltpu.VMEM((1, piece), f32), pltpu.VMEM((HEAD + 16, piece), f32), pltpu.SMEM((pieces,), jnp.int32)],
        scalars=4,
    )


def bwd_kernel(todo_ref, place_ref, seg_ref, need_ref, cos_ref, sin_ref, keys, key_lanes, values, queries, *rest, stage, todo_count, extra, ready):
    if stage:
        grads, kept, sum_in, rest = rest[0], rest[1], rest[2], rest[3:]
    else:
        before, rest = rest[:6], rest[6:]
    outs, rest = rest[: (4, 1)[stage]], rest[(4, 1)[stage] :]
    if not stage:
        prep_back(place_ref, queries, *before, outs[1], outs[2], extra)
        queries, grads = outs[1], outs[2]
    score_a, grad_a, score_b, grad_b, key_sum, value_sum, todo = rest[:7]
    sums = rest[7] if stage else outs[-1]
    pieces = queries.shape[0]
    scores, prob_grads = (score_a, score_b), (grad_a, grad_b)
    sums[...] = sum_in[...] if stage else jnp.zeros(sums.shape, f32)
    if stage:
        outs[0][:, 4 * HEAD :, :] = kept[...]
    ready()

    def attend(i, carry):
        at = todo_ref[i]
        seg = seg_ref[at]
        count = collect(at + 1, pieces, lambda q: (need_ref[q] & seg) != 0, todo)
        key, value, key_lane = keys[at], values[at], key_lanes[at]
        score_a[...] = causal(dot(key, queries[at], 1, 0))
        grad_a[...] = dot(value, grads[at], 1, 0)
        key_sum[...] = jnp.zeros(key_sum.shape, f32)
        value_sum[...] = jnp.zeros(value_sum.shape, f32)

        def fill(slot, query_at):
            scores[slot][...] = dot(key, queries[query_at], 1, 0)
            prob_grads[slot][...] = dot(value, grads[query_at], 1, 0)

        def work(slot, query_at):
            probs = jnp.exp2(scores[slot][...])
            score_grad = (probs * prob_grads[slot][...]).astype(bf16)
            value_sum[...] += dot(grads[query_at, :HEAD, :], probs.astype(bf16), 1, 1)
            key_sum[...] += dot(queries[query_at, :HEAD, :], score_grad, 1, 1)
            sums[query_at] += dot(key_lane, score_grad, 1, 0)

        two_ahead(count, todo, at, fill, work)
        key_grad = unrotate(key_sum[...] * (1.0 / LOG2E), cos_ref[at], sin_ref[at]).astype(bf16)
        value_grad = (0.5 * value_sum[...]).astype(bf16)

        outs[0][i, :HEAD, :] = key_grad
        outs[0][i, HEAD : 2 * HEAD, :] = value_grad
        return carry

    lax.fori_loop(0, todo_count, attend, 0)
    if stage:
        for p in range(pieces):
            grad = unrotate(sums[p] * SCORE_SCALE, cos_ref[p], sin_ref[p]).astype(bf16)
            start = pl.multiple_of((2 + ((p % 2) ^ place_ref[0])) * HEAD, HEAD)
            outs[0][p // 2, pl.ds(start, HEAD), :] = grad


def bwd_call(stage, todo, place, seg, need, cosine, sine, keys, key_lanes, values, queries, more, extra):
    count, (pieces, _, piece) = todo.shape[0], queries.shape
    places = pieces // 2
    sums = shape_of(pieces, HEAD, piece, dtype=f32)
    outs = (
        (shape_of(places, 2 * HEAD, piece), shape_of(*queries.shape), shape_of(*queries.shape), sums),
        (shape_of(places, 6 * HEAD, piece),),
    )[stage]
    operands = (cosine, sine, keys, key_lanes, values, queries, *more)
    got = call(
        functools.partial(bwd_kernel, stage=stage, todo_count=count, extra=extra), "attend_back", outs,
        (todo, place, seg, need, *operands),
        scratch=[pltpu.VMEM((piece, piece), f32)] * 4
        + [pltpu.VMEM((HEAD, piece), f32)] * 2
        + [pltpu.SMEM((pieces,), jnp.int32)]
        + ([pltpu.VMEM(sums.shape, f32)] if stage else []),
        scalars=4, mib=36, late=(0, 1),
    )
    return got[0] if stage else got


def after(value, *earlier):
    return lax.optimization_barrier((value,) + earlier)[0]


def on_device(
    tokens, first_values, cotangent, parents, seg_lengths,
    w_query, w_key, w_value, w_out, w_gate, w_up, w_down, gain_attn, gain_ffn,
):
    assert tokens.shape[1] == 1
    fsdp_count, ctx_count, tp_count = (lax.axis_size(a) for a in ("fsdp", "ctx", "tp"))
    assert tp_count == 4 and ctx_count == 4
    fsdp_at, ctx_at, tp_at = (lax.axis_index(a) for a in ("fsdp", "ctx", "tp"))
    core_at, x_at = tp_at % 2, tp_at // 2
    own_rows, width = tokens.shape[0], tokens.shape[2]
    chip_rows = 2 * own_rows
    heads = w_query.shape[1] // HEAD
    head_width = heads * HEAD
    assert heads == ctx_count
    tree_len = own_rows * tp_count * ctx_count
    weight_rows, hidden = w_query.shape[0], w_gate.shape[1]
    two = fsdp_count == 2

    def over_core(value):
        return lax.ppermute(value, "tp", [(i, i ^ 1) for i in range(tp_count)])

    def over_x(value):
        return lax.ppermute(value, "tp", [(i, i ^ 2) for i in range(tp_count)])

    def over_fsdp(value):
        return lax.ppermute(value, "fsdp", [(0, 1), (1, 0)])

    def over_ctx(value, flip):
        return lax.ppermute(value, "ctx", [(i, i ^ flip) for i in range(ctx_count)])

    def exchange(by_place):
        return lax.all_to_all(by_place, "ctx", 0, 0, tiled=True)

    def relative(rows):
        if not two:
            return rows
        swapped = jnp.concatenate([rows[..., weight_rows:], rows[..., :weight_rows]], axis=-1)
        return jnp.where(fsdp_at == 0, rows, swapped)

    def by_x(near, far):
        return jnp.where(x_at == 0, jnp.concatenate([near, far], axis=0), jnp.concatenate([far, near], axis=0))

    def fsdp_sum(parts, axis=0):
        if not two:
            return lax.psum_scatter(parts[0], "fsdp", scatter_dimension=axis, tiled=True)
        return parts[0], over_fsdp(parts[1])

    def inward(low):
        return low, lax.ppermute(low, "ctx", [(0, 1), (3, 2)])

    def across(low):
        return low, lax.ppermute(low, "ctx", [(1, 2), (2, 1)])

    def outward(low):
        return low, lax.ppermute(low, "ctx", [(1, 0), (2, 3)])

    def join(pair):
        return (pair[0].astype(f32) + pair[1].astype(f32)).astype(bf16)

    def finish(pair):
        return jnp.where((ctx_at == 0) | (ctx_at == 3), pair[1], pair[0]).astype(f32)

    def hold(pair, *earlier):
        return (pair[0], after(pair[1], *earlier)) if isinstance(pair, tuple) else after(pair, *earlier)

    def step(*pairs):
        if not two:
            return [join(pair) if isinstance(pair, tuple) else pair for pair in pairs]
        return join_call(*pairs)

    three = (w_query, w_key, w_value)
    own_tokens, early_gains = tokens[:, 0, :], jnp.stack([gain_attn, gain_ffn])
    if two:
        own_three = stack_call(*three)
        qkv_weight = [own_three, over_fsdp(own_three)]
        own_tokens, early_gains = after(own_tokens, own_three), after(early_gains, own_three)
        gains = jnp.concatenate([early_gains, over_fsdp(early_gains)], axis=1)
    else:
        qkv_weight = [stack_call(*(lax.all_gather(w, "fsdp", axis=0, tiled=True) for w in three))]
        gains = lax.all_gather(early_gains, "fsdp", axis=1, tiled=True)
    token_x = over_x(own_tokens)
    token_core = over_core(own_tokens)
    attention_gain = gains[0].reshape(1, width).astype(f32)
    ffn_gain = gains[1].reshape(1, width).astype(f32)
    count = len(qkv_weight)

    place = jnp.stack([x_at, core_at, ctx_at, fsdp_at]).astype(jnp.int32)
    position, query_extra, key_extra, seg_bits, need_bits = layout_call(parents, seg_lengths, tree_len, chip_rows)
    frequency = jnp.exp(-math.log(10000.0) * jnp.arange(HALF, dtype=f32) / HALF)
    angles = frequency[None, :, None] * position
    cosine, sine = jnp.cos(angles), jnp.sin(angles)

    def normalize(rows_f32):
        return lax.rsqrt(jnp.mean(rows_f32 * rows_f32, axis=-1, keepdims=True) + epsilon)

    first_flat = first_values[:, 0, :]

    def spread(pieces):
        return [over_ctx(piece, flip) if flip else piece for flip, piece in enumerate(pieces)]

    by_head, near_normed, far_normed = project_call(
        place, (own_tokens, token_core, token_x, over_core(token_x)), attention_gain, cosine, sine, first_flat, qkv_weight, two
    )
    got = exchange(by_head)
    others = (w_gate, w_up, w_down, w_out)
    if two:
        feed_own = stack_call(*(after(w.T, by_head) for w in others))
        feed_weight = [feed_own, over_fsdp(feed_own)]
    else:
        feed_weight = [stack_call(*(lax.all_gather(w, "fsdp", axis=0, tiled=True).T for w in others))]
    own_cot = relative(after(cotangent[:, 0, :], by_head))
    half_places = jnp.arange(ctx_count, dtype=jnp.int32) * 2
    far_out, far_full, far_lse, keys, key_lanes, value_lanes, values, queries = fwd_call(
        after(half_places + (1 - x_at), own_cot), place, seg_bits, need_bits, (got, query_extra, key_extra), True
    )
    cot_x = over_x(after(own_cot, got))
    out_weight = pick_call([after(w, far_out) for w in feed_weight], head_width)
    out_weight_x = over_x(out_weight)
    cot_core = over_core(after(own_cot, got))
    cot_x_core = over_core(cot_x)

    near_out, near_full, near_lse = fwd_call(
        after(half_places + x_at, far_out, out_weight, cot_x), place, seg_bits, need_bits, (keys, value_lanes, queries)
    )
    far_mixed = after(exchange(far_out), near_out).reshape(head_width, chip_rows)
    far_mixed_got = over_x(far_mixed)
    near_mixed = exchange(after(near_out, far_mixed)).reshape(head_width, chip_rows)

    mine, other = output_call(place, near_mixed, far_mixed_got, out_weight, out_weight_x)
    own_single = relative(own_tokens).astype(f32)
    middle = own_single + mine + over_core(other).astype(f32)

    middle_scale = normalize(middle)
    ffn_own = (middle * middle_scale * ffn_gain).astype(bf16)
    ffn_x = over_x(ffn_own)
    ffn_core = over_core(ffn_own)
    near_hidden, near_gate, near_up, near_mine, near_sent = feed_call(
        ffn_own, ffn_core, own_cot, cot_core, feed_weight, hidden
    )
    ffn_x = after(ffn_x, near_mine)
    ffn_x_core = over_core(ffn_x)
    far_hidden, far_gate, far_up, far_mine, far_sent = feed_call(
        ffn_x, ffn_x_core, cot_x, cot_x_core, feed_weight, hidden
    )
    far_sum = (far_mine + over_core(far_sent).astype(f32)).astype(bf16)
    far_sum_got = over_x(far_sum)
    near_sum = near_mine + over_core(near_sent).astype(f32)

    all_cot = (after(own_cot, far_sum), cot_core, cot_x, cot_x_core)
    all_ffn = (after(ffn_own, far_sum), ffn_core, ffn_x, ffn_x_core)
    first_parts, second_parts = feed_grads_call(
        (near_gate, far_gate, near_up, far_up), (near_hidden, far_hidden), all_ffn, all_cot, count
    )
    first_sum = fsdp_sum(first_parts, 1)
    second_sum = fsdp_sum(second_parts, 1)
    ffn_grad = near_sum + after(far_sum_got, first_parts[0]).astype(f32)

    weighted = ffn_grad * ffn_gain
    middle_grad = (
        own_cot.astype(f32)
        + middle_scale * weighted
        - middle * (middle_scale**3 * jnp.mean(weighted * middle, axis=-1, keepdims=True))
    )
    middle_low = middle_grad.astype(bf16)
    near_heads, far_heads, chip_low = heads_call(place, middle_low, over_core(middle_low), out_weight, out_weight_x)
    far_out_grad = over_x(far_heads)
    near_grads = exchange(near_heads.reshape(heads, HEAD, chip_rows))
    far_grads = exchange(after(far_out_grad, near_grads).reshape(heads, HEAD, chip_rows))

    ffn_gain_part = jnp.sum(after(ffn_grad, near_heads) * middle * middle_scale, axis=0)
    low_x = over_x(after(middle_low, far_out_grad))
    low_x_core = over_core(low_x)
    near_result, far_result, sent = result_call(after(near_hidden, near_heads), far_hidden, feed_weight)
    sent_got = over_core(sent)
    (first_low,) = step(hold(first_sum, far_grads, sent))
    first_in = inward(first_low)
    def back(stage, places, more, *earlier):
        return bwd_call(
            stage, after(jnp.stack(places).astype(jnp.int32), *earlier), place, seg_bits, need_bits, cosine, sine,
            keys, key_lanes, values, more[0], more[1:], query_extra.shape[1],
        )

    far_at, near_at = [2 * i + 1 - x_at for i in range(4)], [2 * i + x_at for i in range(4)]
    far_kv, back_queries, grads, query_sum = back(
        0, far_at, (queries, near_grads, far_grads, near_full, far_full, near_lse, far_lse), first_low
    )

    first_low, second_low = step(hold(first_in, far_kv), hold(second_sum, far_kv))
    first_across, second_in = across(first_low), inward(second_low)
    last = back(1, near_at, (back_queries, grads, far_kv, query_sum), first_low)
    first_got, second_got = hold(first_across, last), hold(second_in, last)

    last_got = exchange(last)
    out_parts = out_grads_call(after(place, last), chip_low, low_x, low_x_core, near_mixed, far_mixed, count)
    far_result_got = over_x((after(far_result, out_parts[0]) + sent_got[1].astype(f32)).astype(bf16))
    layer_out = relative((middle + near_result + sent_got[0].astype(f32) + far_result_got.astype(f32)).astype(bf16))
    last_got = after(last_got, layer_out)

    qkv_parts = weights_call(near_normed, far_normed, last_got, out_parts)
    qkv_sum = fsdp_sum(qkv_parts)
    first_low, second_low = step(hold(first_got, qkv_parts[0]), hold(second_got, qkv_parts[0]))
    first_done, second_across = outward(first_low), across(second_low)
    near_mine, near_other, far_mine, far_other, gain_part, grad_values = rows_call(
        after(place, first_low), near_normed, far_normed, last_got, qkv_weight
    )
    far_rows_got = over_x((far_mine + over_core(far_other).astype(f32)).astype(bf16))
    near_rows_got = over_core(near_other)
    gain_sum = jnp.concatenate([gain_part / attention_gain, ffn_gain_part[None]], axis=0)

    def light(*pairs):
        return [join(pair) if isinstance(pair, tuple) else pair for pair in pairs]

    qkv_low, second_low = light(hold(qkv_sum, near_mine), hold(second_across, near_mine))
    qkv_in, second_done = inward(qkv_low), outward(second_low)
    first_all = finish(hold(first_done, qkv_in[1] if isinstance(qkv_in, tuple) else qkv_in))
    if two:
        gain_sum = after(gain_sum, qkv_low)
        gain_sum = gain_sum + over_core(gain_sum)
        gain_sum = gain_sum + over_x(gain_sum)
        gain_sum = gain_sum[:, :weight_rows] + over_fsdp(gain_sum[:, weight_rows:])
    (qkv_low,) = light(hold(qkv_in, gain_sum, far_rows_got, first_all))
    lows = [qkv_low]
    qkv_across = across(qkv_low)
    if two:
        gain_sum = after(gain_sum, qkv_low)
        gain_sum = gain_sum + over_ctx(gain_sum, 1)
    second_all = finish(hold(second_done, qkv_across[1]))
    (qkv_low,) = light(hold(qkv_across, gain_sum, second_all))
    if two:
        gain_sum = gain_sum + over_ctx(after(gain_sum, qkv_low), 2)
    else:
        gain_sum = lax.psum(gain_sum, ("fsdp", "ctx", "tp"))
        gain_sum = lax.dynamic_slice_in_dim(gain_sum, fsdp_at * weight_rows, weight_rows, 1)
    grad_query, grad_key, grad_value, grad_out = jnp.split(finish(hold(outward(qkv_low), gain_sum)), 4)
    grad_gate, grad_down = first_all[:hidden].T, second_all[hidden // 2 :].T
    grad_up = jnp.concatenate([first_all[hidden:], second_all[: hidden // 2]], axis=0).T

    normed_grad = after(near_mine, lows[0]) + near_rows_got.astype(f32) + far_rows_got.astype(f32)
    scale = normalize(own_single)
    weighted = normed_grad * attention_gain
    grad_tokens = (
        middle_grad + scale * weighted - own_single * (scale**3 * jnp.mean(weighted * own_single, axis=-1, keepdims=True))
    )
    return (
        layer_out[:, None, :],
        relative(grad_tokens)[:, None, :],
        grad_values.reshape(4 * own_rows, 1, head_width),
        grad_query,
        grad_key,
        grad_value,
        grad_out,
        grad_gate,
        grad_up,
        grad_down,
        gain_sum[0],
        gain_sum[1],
    )

def solution(mesh):
    rows, columns = P(("ctx", "tp"), "fsdp", None), P("ctx", "fsdp", "tp")
    weight, gain = P("fsdp", "tp"), P("fsdp")
    return jax.shard_map(
        on_device,
        mesh=mesh,
        in_specs=(rows, columns, rows, P("fsdp", None), P("fsdp", None)) + (weight,) * 7 + (gain,) * 2,
        out_specs=(rows, rows, columns) + (weight,) * 7 + (gain,) * 2,
        check_vma=False,
    )
```
